256 devices in a mesh: ctx: 32 (over z_lo, y, core), cp: 8 (over z_hi, x).
Axes of the slice: x: 4, y: 4, z: 8 (z_hi: 2, z_lo: 4; z = z_hi * 4 + z_lo), core: 2. Of those that a mesh axis runs over, the one named last changes fastest.
Arguments:
- signal: bfloat16 [524288, 128], P(('ctx', 'cp')), may hold values from -6 to 6
- gate: bfloat16 [524288, 128], P(('ctx', 'cp')), may hold values from -6 to 6
- filters: bfloat16 [2, 4096, 256, 128], P(None, ('ctx', 'cp')), as said below
- skip: float32 [128], replicated, may hold values from 0.5 to 1.5
Outputs:
- mixed: bfloat16 [524288, 128], P(('ctx', 'cp'))
The draws below stay inside these ranges and needn't reach their ends.
Inputs may be any that keep to these rules, and one draw needn't show every extreme that they name: The filter spectra are those of real filters: response[(1048576 - k) % 1048576, c] is the complex conjugate of response[k, c] for every k and c.
All inputs are finite; a program needn't handle non-finite values.
Results may differ from the reference program's by a relative error of at most 0.001.
Values may be sent and summed in bfloat16 or wider, within the bound.
A program may use at most 128 MiB of HBM per device.

```python
import jax
import jax.numpy as jnp
from jax import lax

LENGTH = 524288
CH = 128
COLS = 4096
N_CTX = 32
N_CP = 8
DEVICES = 256


def mirror_whole(values):
    width = COLS // DEVICES
    piece = width // 2
    blocks = values.reshape(DEVICES, 2, piece, DEVICES, CH)
    swapped = blocks[:, ::-1].reshape(COLS, DEVICES, CH)
    generic = swapped[:, ::-1]
    first = jnp.roll(values[0][::-1], 1, axis=0)
    nyquist_row = values[piece][::-1]
    return generic.at[0].set(first).at[piece].set(nyquist_row)


def draw_filters(key, part):
    raw = jax.random.normal(key, (2, COLS, DEVICES, CH), jnp.float32)
    raw = jnp.clip(raw, -4.0, 4.0)
    real_part = raw[0] + mirror_whole(raw[0])
    imag_part = raw[1] - mirror_whole(raw[1])
    return (jnp.stack([real_part, imag_part]) * 0.70710678).astype(jnp.bfloat16)


def shard_levels(own_key, dims, shards, smallest, largest):
    gain, own = 1.0, jax.random.fold_in(own_key, 6)
    for dim, parts in shards:
        heights = jnp.exp(jax.random.uniform(jax.random.fold_in(own, dim), (parts,), jnp.float32, smallest / len(shards), largest / len(shards)))
        gain = gain * jnp.repeat(heights, dims[dim] // parts).reshape([-1 if axis == dim else 1 for axis in range(len(dims))])
    return gain


def centred(own_key, extent, spread, limit, cuts=(), held_as=jnp.bfloat16):
    loudness = shard_levels(own_key, extent, cuts, -0.22, 0.18) if cuts else 1.0
    result = jax.random.normal(own_key, extent, jnp.float32) * spread * loudness
    return jnp.minimum(jnp.maximum(result, -limit), limit).astype(held_as)


def setup_inputs(seed: int = 0) -> dict:
    key_list = jax.random.split(jax.random.key(seed), 5)
    return {
        "signal": centred(key_list[0], (LENGTH, CH), 1.0, 6.0, ((0, 256),)),
        "gate": centred(key_list[1], (LENGTH, CH), 1.0, 6.0, ((0, 256),)),
        "filters": draw_filters(jax.random.fold_in(key_list[4], 71), 0),
        "skip": jnp.clip(jax.random.uniform(key_list[3], (CH,), jnp.float32, 0.5, 1.5), 0.5, 1.5),
    }


def reference(signal, gate, filters, skip):
    full = 2 * LENGTH
    devices = N_CTX * N_CP
    half = COLS // 2
    piece = (COLS // devices) // 2
    fine = jnp.arange(COLS, dtype=jnp.int32)
    lower = fine < half
    mirrored = jnp.where(lower, fine, (COLS - fine) % half)
    row_index = (mirrored // piece) * (2 * piece) + mirrored % piece + jnp.where(lower, 0, piece)
    row_index = row_index.astype(jnp.int32)

    def one_channel(index):
        column = lax.dynamic_index_in_dim(signal, index, 1, keepdims=False).astype(jnp.float32)
        spectrum = jnp.fft.fft(column, n=full)
        part_re = lax.dynamic_index_in_dim(filters[0], index, 2, keepdims=False).astype(jnp.float32)
        part_im = lax.dynamic_index_in_dim(filters[1], index, 2, keepdims=False).astype(jnp.float32)
        resp_re = jnp.transpose(part_re[row_index]).reshape(full)
        resp_im = jnp.transpose(part_im[row_index]).reshape(full)
        product = spectrum * (resp_re + 1j * resp_im)
        return jnp.real(jnp.fft.ifft(product))[:LENGTH].astype(jnp.float32)

    conv = lax.map(one_channel, jnp.arange(CH, dtype=jnp.int32))
    conv = jnp.transpose(conv)
    mixed = gate.astype(jnp.float32) * (conv + skip[None, :] * signal.astype(jnp.float32))
    return mixed.astype(jnp.bfloat16)
```

```python
import functools
import math

import jax
import jax.numpy as jnp
import ml_dtypes
import numpy as np
from jax import lax
from jax.experimental import pallas as pl
from jax.experimental.pallas import tpu as pltpu
from jax.sharding import PartitionSpec as P


FULL = 1 << 20
ROWS = 144
F32 = jnp.float32
BF16 = jnp.bfloat16

LOW = ((2, 4, 6, 0), (3, 5, 7, 1))
UPP = ((6, 4, 2, 0), (5, 3, 1, 7))


def phase(product, length):
    angle = 2 * math.pi * (np.asarray(product, dtype=np.int64) % length) / length
    return np.cos(angle), np.sin(angle)


def split_np(array):
    high = array.astype(ml_dtypes.bfloat16)
    low = (array - high.astype(np.float64)).astype(ml_dtypes.bfloat16)
    return high, low


def row_sigma(core):
    index = np.concatenate([4 * np.arange(32) + t for t in (1, 2, 3, 0)] + [np.array([128])])
    sigma = 2 * index + core
    if core == 1:
        sigma[128] = 0
    return sigma


@functools.lru_cache(maxsize=None)
def tables():
    pos = np.arange(256)
    core_of, chip_of = pos // 128, pos % 128
    block = ((chip_of // 8) * 2 + core_of) * 8 + chip_of % 8
    m256 = []
    tb = np.zeros((2, 2, ROWS, 256), np.float32)
    ta = np.zeros((2, ROWS, 128), np.float32)
    beta, al = np.arange(256), np.arange(8)
    for core in (0, 1):
        sigma = row_sigma(core)
        cos, sin = phase(sigma[:128, None] * block[None, :], 512)
        fwd = np.concatenate([cos, -sin], 0)
        inv = np.concatenate([cos.T, -sin.T], 1)
        if core == 0:
            nyquist = phase(256 * block, 512)[0]
            fwd[128 + 96] = nyquist
            inv[:, 128 + 96] = nyquist
        inv = inv * (2.0 / FULL)
        m256.append(np.stack([*split_np(fwd), *split_np(inv)]))
        cos, sin = phase(sigma[:, None] * beta[None, :], FULL)
        tb[core, 0, :129], tb[core, 1, :129] = cos, -sin
        cos, sin = phase(sigma[:, None] * al[None, :], 4096)
        ta[core, :129, 0:8], ta[core, :129, 8:16] = cos, -sin
    cos, sin = phase(beta[:, None] * beta[None, :], 256)
    m512 = np.stack(
        [
            *split_np(np.block([[cos, -sin], [sin, cos]])),
            *split_np(np.block([[cos, sin], [-sin, cos]])),
        ]
    )
    cos, sin = phase(al[:, None] * beta[None, :], 2048)
    t2 = np.stack([cos, -sin]).astype(np.float32)
    return np.stack(m256), m512, tb, ta, t2


def cmul(a, b, c, d):
    return a * c - b * d, a * d + b * c


def dft8(re, im, sign):
    root = math.sqrt(0.5)

    def turn(x, y, power):
        if power == 0:
            return x, y
        if power == 2:
            return (-y, x) if sign > 0 else (y, -x)
        if power == 1:
            if sign > 0:
                return (x - y) * root, (x + y) * root
            return (x + y) * root, (y - x) * root
        if sign > 0:
            return (-x - y) * root, (x - y) * root
        return (y - x) * root, (-x - y) * root

    def step(res, ims):
        n = len(res)
        if n == 1:
            return res, ims
        h = n // 2
        er = [res[j] + res[j + h] for j in range(h)]
        ei = [ims[j] + ims[j + h] for j in range(h)]
        odd = [turn(res[j] - res[j + h], ims[j] - ims[j + h], j * (8 // n)) for j in range(h)]
        er, ei = step(er, ei)
        dr, di = step([o[0] for o in odd], [o[1] for o in odd])
        outr, outi = [], []
        for j in range(h):
            outr += [er[j], dr[j]]
            outi += [ei[j], di[j]]
        return outr, outi

    return step(re, im)


def split(x):
    high = x.astype(BF16)
    return high, (x - high.astype(F32)).astype(BF16)


def dot(a, b):
    return jnp.dot(a, b, preferred_element_type=F32)


def kernel(
    sig, filt, gate, skip, m256, m512, tb, ta, t2, out,
    fv, ev, gv, m256v, m512v, tbv, tav, t2v,
    s32, xs, xb, x32, fs, es, hb, eb, hf, fz, tw, zh, zl, gg, ce, ch, cl,
    yo, yw, ys, pb, yb, lsem, ssem, rsem,
):
    ctx, cp = lax.axis_index("ctx"), lax.axis_index("cp")
    core = lax.rem(ctx, 2)
    other = 1 - core
    chip = (ctx // 2) * 8 + cp
    here = ctx * 8 + cp
    even = (1 - core).astype(F32)

    def device(t, k):
        return ((t // 8) * 2 + k, lax.rem(t, 8))

    def remote(src, dst, sem, t, k):
        return pltpu.make_async_remote_copy(
            src_ref=src, dst_ref=dst, send_sem=ssem.at[sem], recv_sem=rsem.at[sem],
            device_id=device(t, k), device_id_type=pl.DeviceIdType.MESH,
        )

    def loop(n, body, start=0):
        def wrapped(i, carry):
            body(i)
            return carry

        lax.fori_loop(start, n, wrapped, 0)

    barrier = pltpu.get_barrier_semaphore()

    def greet(i):
        t = lax.rem(here + i, 256)
        pl.semaphore_signal(
            barrier, inc=1, device_id=(t // 8, lax.rem(t, 8)), device_id_type=pl.DeviceIdType.MESH
        )

    loop(256, greet, 1)

    group, place = here // 64, lax.rem(here, 64)
    upper = (place >= 32).astype(jnp.int32)
    loads = [
        pltpu.make_async_copy(filt.at[:, pl.ds(upper * 8, 8)], fv, lsem.at[0]),
        pltpu.make_async_copy(filt.at[:, pl.ds(8, 1)], ev, lsem.at[1]),
        pltpu.make_async_copy(ta.at[core], tav, lsem.at[2]),
        pltpu.make_async_copy(tb.at[core], tbv, lsem.at[3]),
        pltpu.make_async_copy(m256.at[core], m256v, lsem.at[4]),
        pltpu.make_async_copy(m512, m512v, lsem.at[5]),
        pltpu.make_async_copy(t2, t2v, lsem.at[6]),
        pltpu.make_async_copy(gate, gv, lsem.at[7]),
    ]
    for load in loads:
        load.start()

    def turn_signal(a):
        block = sig[pl.ds(pl.multiple_of(a * 128, 128), 128), :].astype(F32)
        s32[pl.ds(a, 128, stride=16), :] = block.T

    loop(16, turn_signal)

    def pack(dst, base):
        def body(i):
            rows = s32[pl.ds(pl.multiple_of(i * 256, 256), 256), :]
            dst[pl.ds(base + i * 16, 16)] = rows.astype(BF16).reshape(16, 16, 128)

        loop(8, body)

    pack(xs, 0)

    loads[0].wait()
    loads[1].wait()

    def turn_filter(k):
        for blk in range(4):
            row = jnp.where(upper == 1, UPP[k][blk], LOW[k][blk])

            def body(j, row=row, blk=blk):
                ri, qh = j // 2, lax.rem(j, 2)
                block = fv[ri, row, pl.ds(pl.multiple_of(qh * 128, 128), 128), :].astype(F32)
                s32[pl.ds(ri * 8 + blk * 2 + qh, 128, stride=16), :] = block.T

            loop(4, body)

    for k in range(2):
        turn_filter(k)
        pack(fs, k * 128)

    @pl.when(here == 0)
    def _():
        def body(j):
            ri, qh = j // 2, lax.rem(j, 2)
            block = ev[ri, 0, pl.ds(pl.multiple_of(qh * 128, 128), 128), :].astype(F32).T
            for blk in range(4):
                s32[pl.ds(ri * 8 + blk * 2 + qh, 128, stride=16), :] = block

        loop(4, body)
        pack(es, 0)

    loads[2].wait()
    loads[3].wait()

    def make_twiddle(r):
        rows = pl.ds(pl.multiple_of(r * 16, 16), 16)
        cols = tav[rows, :]
        for al in range(8):
            c = jnp.broadcast_to(cols[:, al : al + 1], (16, 256))
            s = jnp.broadcast_to(cols[:, 8 + al : 9 + al], (16, 256))
            tw[al, 0, rows, :], tw[al, 1, rows, :] = cmul(c, s, tbv[0, rows, :], tbv[1, rows, :])

    loop(9, make_twiddle)

    pl.semaphore_wait(barrier, 255)
    slot = core * 128 + chip

    def send_signal(i):
        t = lax.rem(chip + i, 128)
        remote(xs.at[t], xb.at[slot], 0, t, core).start()

    pltpu.make_async_copy(xs.at[chip], xb.at[slot], rsem.at[0]).start()
    loop(128, send_signal, 1)

    fslot = jnp.where(upper == 1, (7 - group) * 32 + 63 - place, group * 32 + place)

    def send_filter(i):
        t = lax.rem(chip + i, 128)
        for k in range(2):
            remote(fs.at[k * 128 + t], hb.at[fslot], 1, t, k).start()

    pltpu.make_async_copy(fs.at[core * 128 + chip], hb.at[fslot], rsem.at[1]).start()
    remote(fs.at[other * 128 + chip], hb.at[fslot], 1, chip, other).start()
    loop(128, send_filter, 1)

    @pl.when(here == 0)
    def _():
        def body(t):
            remote(es.at[t], eb.at[0], 2, t, 0).start()

        pltpu.make_async_copy(es.at[0], eb.at[0], rsem.at[2]).start()
        loop(128, body, 1)

    mine = xb.at[pl.ds(core * 128, 128)]
    theirs = xb.at[pl.ds(other * 128, 128)]
    pltpu.make_async_copy(mine, mine, rsem.at[0]).wait()
    forward = remote(mine, mine, 3, chip, other)
    forward.start()
    for load in loads[4:]:
        load.wait()
    pltpu.make_async_copy(theirs, theirs, rsem.at[3]).wait()

    def widen(src, dst):
        def body(i):
            dst[pl.ds(pl.multiple_of(i * 256, 256), 256), :] = (
                src[pl.ds(i * 16, 16)].astype(F32).reshape(256, 128)
            )

        loop(16, body)

    widen(xb, x32)

    top = (lax.broadcasted_iota(jnp.int32, (8, 256), 0) == 0).astype(F32)

    def first(al):
        x = jnp.concatenate(
            [x32[pl.ds(2 * al, 256, stride=16), :], x32[pl.ds(2 * al + 1, 256, stride=16), :]], 1
        ).astype(BF16)
        f = dot(m256v[0], x) + dot(m256v[1], x)
        fz[al, 0, 0:128, :] = f[0:128]
        fz[al, 1, 0:128, :] = f[128:256]
        lone = f[224:232] * (top * even)
        fz[al, 1, 96:104, :] = f[224:232] - lone
        fz[al, 0, 128:136, :] = lone
        fz[al, 0, 136:144, :] = jnp.zeros((8, 256), F32)
        fz[al, 1, 128:144, :] = jnp.zeros((16, 256), F32)

    loop(8, first)

    def second(r):
        rows = pl.ds(pl.multiple_of(r * 16, 16), 16)
        for half in range(2):
            ln = slice(half * 128, half * 128 + 128)
            lm = slice(256 + half * 128, 384 + half * 128)
            pairs = [
                cmul(fz[al, 0, rows, ln], fz[al, 1, rows, ln], tw[al, 0, rows, ln], tw[al, 1, rows, ln])
                for al in range(8)
            ]
            re, im = dft8([p[0] for p in pairs], [p[1] for p in pairs], -1)
            for e in range(8):
                a, b = re[e], im[e]
                if e:
                    a, b = cmul(a, b, t2v[0, e : e + 1, ln], t2v[1, e : e + 1, ln])
                zh[e, rows, ln], zl[e, rows, ln] = split(a)
                zh[e, rows, lm], zl[e, rows, lm] = split(b)

    loop(9, second)

    def third(base):
        def body(j):
            a = zh[pl.ds(j * 2, 2)].reshape(2 * ROWS, 512)
            b = zl[pl.ds(j * 2, 2)].reshape(2 * ROWS, 512)
            g = dot(a, m512v[base]) + dot(a, m512v[base + 1]) + dot(b, m512v[base])
            gg[pl.ds(j * 2, 2)] = g.reshape(2, ROWS, 512)

        loop(4, body)

    third(0)

    pltpu.make_async_copy(hb, hb, rsem.at[1]).wait()
    widen(hb, x32)

    def place_filter(e, shift):
        for ri in range(2):
            hf[e, ri, 128:144, :] = jnp.zeros((16, 256), F32)
            if shift:
                hf[e, ri, 96:104, :] = jnp.zeros((8, 256), F32)
            for blk in range(4):
                lo = blk * 32 + (1 if shift and blk == 3 else 0)
                for qh in range(2):
                    start = e * 512 + (ri * 8 + blk * 2 + qh)
                    hf[e, ri, lo : lo + 32, qh * 128 : qh * 128 + 128] = x32[
                        pl.ds(start, 32, stride=16), :
                    ]

    loop(4, lambda e: place_filter(e, False))

    @pl.when(core == 1)
    def _():
        loop(8, lambda e: place_filter(e, False), 4)

    @pl.when(core == 0)
    def _():
        loop(8, lambda e: place_filter(e, True), 4)
        pltpu.make_async_copy(eb, eb, rsem.at[2]).wait()
        extra = eb[0].astype(F32)
        for ri in range(2):
            hf[0, ri, 96:97, :] = hf[0, ri, 96:97, :] * 0.5
            for qh in range(2):
                row = ri * 8 + 6 + qh
                hf[4, ri, 96:97, qh * 128 : qh * 128 + 128] = extra[row : row + 1] * 0.5

    def apply_filter(e):
        def body(r):
            rows = pl.ds(pl.multiple_of(r * 16, 16), 16)
            a, b = cmul(
                gg[e, rows, 0:256], gg[e, rows, 256:512], hf[e, 0, rows, :], hf[e, 1, rows, :]
            )
            zh[e, rows, 0:256], zl[e, rows, 0:256] = split(a)
            zh[e, rows, 256:512], zl[e, rows, 256:512] = split(b)

        loop(9, body)

    loop(8, apply_filter)
    third(2)

    def back(r, last):
        rows = pl.ds(r * 16, 16) if last else pl.ds(pl.multiple_of(r * 16, 16), 16)
        for half in range(2):
            ln = slice(half * 128, half * 128 + 128)
            lm = slice(256 + half * 128, 384 + half * 128)
            re, im = [], []
            for e in range(8):
                a, b = gg[e, rows, ln], gg[e, rows, lm]
                if e:
                    a, b = cmul(a, b, t2v[0, e : e + 1, ln], -t2v[1, e : e + 1, ln])
                re.append(a)
                im.append(b)
            re, im = dft8(re, im, 1)
            for al in range(8):
                a, b = cmul(re[al], im[al], tw[al, 0, rows, ln], -tw[al, 1, rows, ln])
                if last:
                    ce[al, :, ln] = a[0:8]
                else:
                    mark = top[:, 0:128] * (even * (r == 6).astype(F32))
                    head = b[0:8] * (1.0 - mark) + ce[al, 0:1, ln] * mark
                    b = jnp.concatenate([head, b[8:16]], 0)
                    down = pl.ds(pl.multiple_of(128 + r * 16, 16), 16)
                    ch[al, rows, ln], cl[al, rows, ln] = split(a)
                    ch[al, down, ln], cl[al, down, ln] = split(b)

    back(8, True)
    loop(8, lambda r: back(r, False))

    def combine(k, dst):
        rows = pl.ds(pl.multiple_of(k * 128, 128), 128)

        def body(al):
            vh, vl = m256v[2, rows, :], m256v[3, rows, :]
            y = dot(vh, ch[al]) + dot(vh, cl[al]) + dot(vl, ch[al])
            dst[pl.ds(2 * al, 128, stride=16), :] = y[:, 0:128]
            dst[pl.ds(2 * al + 1, 128, stride=16), :] = y[:, 128:256]

        loop(8, body)

    combine(other, yo)
    swap = remote(yo, pb, 4, chip, other)
    swap.start()
    combine(core, yw)
    pltpu.make_async_copy(pb, pb, rsem.at[4]).wait()

    def rows_of(t):
        return pl.ds(pl.multiple_of(t * 16, 16), 16)

    def send_out(i):
        t = lax.rem(chip + i, 128)
        ys[rows_of(t), :] = yw[rows_of(t), :] + pb[rows_of(t), :]
        remote(ys.at[rows_of(t)], yb.at[rows_of(chip)], 5, t, core).start()

    loop(128, send_out, 1)
    ys[rows_of(chip), :] = yw[rows_of(chip), :] + pb[rows_of(chip), :]
    pltpu.make_async_copy(ys.at[rows_of(chip)], yb.at[rows_of(chip)], rsem.at[5]).start()
    pltpu.make_async_copy(yb, yb, rsem.at[5]).wait()

    def finish(a):
        rows = pl.ds(pl.multiple_of(a * 128, 128), 128)
        conv = yb[pl.ds(a, 128, stride=16), :].T
        value = conv + skip[...] * sig[rows, :].astype(F32)
        out[rows, :] = (gv[rows, :].astype(F32) * value).astype(BF16)

    loop(16, finish)

    def sent(ref, sem):
        pltpu.make_async_copy(ref, ref, ssem.at[sem]).wait()

    sent(xs.at[pl.ds(0, 127)], 0)
    sent(fs.at[pl.ds(0, 255)], 1)

    @pl.when(here == 0)
    def _():
        sent(es.at[pl.ds(0, 127)], 2)

    forward.wait_send()
    swap.wait_send()
    sent(ys.at[pl.ds(0, 127 * 16)], 5)


def body(signal, gate, filters, skip):
    m256, m512, tb, ta, t2 = (jnp.asarray(t) for t in tables())
    vmem = pl.BlockSpec(memory_space=pltpu.VMEM)
    hbm = pl.BlockSpec(memory_space=pl.ANY)
    return pl.pallas_call(
        kernel,
        out_shape=jax.ShapeDtypeStruct(signal.shape, BF16),
        in_specs=[vmem, hbm, hbm, vmem, hbm, hbm, hbm, hbm, hbm],
        out_specs=vmem,
        scratch_shapes=[
            pltpu.VMEM((2, 8, 256, 128), BF16),
            pltpu.VMEM((2, 1, 256, 128), BF16),
            pltpu.VMEM((2048, 128), BF16),
            pltpu.VMEM((4, 256, 256), BF16),
            pltpu.VMEM((4, 512, 512), BF16),
            pltpu.VMEM((2, ROWS, 256), F32),
            pltpu.VMEM((ROWS, 128), F32),
            pltpu.VMEM((2, 8, 256), F32),
            pltpu.VMEM((2048, 128), F32),
            pltpu.VMEM((128, 16, 128), BF16),
            pltpu.VMEM((256, 16, 128), BF16),
            pltpu.VMEM((4096, 128), F32),
            pltpu.VMEM((256, 16, 128), BF16),
            pltpu.VMEM((128, 16, 128), BF16),
            pltpu.VMEM((256, 16, 128), BF16),
            pltpu.VMEM((1, 16, 128), BF16),
            pltpu.VMEM((8, 2, ROWS, 256), F32),
            pltpu.VMEM((8, 2, ROWS, 256), F32),
            pltpu.VMEM((8, 2, ROWS, 256), F32),
            pltpu.VMEM((8, ROWS, 512), BF16),
            pltpu.VMEM((8, ROWS, 512), BF16),
            pltpu.VMEM((8, ROWS, 512), F32),
            pltpu.VMEM((8, 8, 256), F32),
            pltpu.VMEM((8, 256, 256), BF16),
            pltpu.VMEM((8, 256, 256), BF16),
            pltpu.VMEM((2048, 128), F32),
            pltpu.VMEM((2048, 128), F32),
            pltpu.VMEM((2048, 128), F32),
            pltpu.VMEM((2048, 128), F32),
            pltpu.VMEM((2048, 128), F32),
            pltpu.SemaphoreType.DMA((8,)),
            pltpu.SemaphoreType.DMA((6,)),
            pltpu.SemaphoreType.DMA((6,)),
        ],
        compiler_params=pltpu.CompilerParams(
            collective_id=0, has_side_effects=True, vmem_limit_bytes=56 << 20
        ),
    )(signal, filters, gate, skip[None, :], m256, m512, tb, ta, t2)


def solution(mesh):
    placed = (
        P(("ctx", "cp"), None),
        P(("ctx", "cp"), None),
        P(None, ("ctx", "cp"), None, None),
        P(),
    )
    return jax.shard_map(
        body, mesh=mesh, in_specs=placed, out_specs=P(("ctx", "cp"), None), check_vma=False
    )
```

```python
import functools
import math

import jax
import jax.numpy as jnp
import ml_dtypes
import numpy as np
from jax import lax
from jax.experimental import pallas as pl
from jax.experimental.pallas import tpu as pltpu
from jax.sharding import PartitionSpec as P


FULL = 1 << 20
SPAN = 2.0**7.75
ROWS = 144
F32 = jnp.float32
BF16 = jnp.bfloat16

LOW = ((2, 4, 6, 0), (3, 5, 7, 1))
UPP = ((6, 4, 2, 0), (5, 3, 1, 7))


def phase(product, length):
    angle = 2 * math.pi * (np.asarray(product, dtype=np.int64) % length) / length
    return np.cos(angle), np.sin(angle)


def split_np(array):
    high = array.astype(ml_dtypes.bfloat16)
    low = (array - high.astype(np.float64)).astype(ml_dtypes.bfloat16)
    return high, low


def row_sigma(core):
    index = np.concatenate([4 * np.arange(32) + t for t in (1, 2, 3, 0)] + [np.array([128])])
    sigma = 2 * index + core
    if core == 1:
        sigma[128] = 0
    return sigma


@functools.lru_cache(maxsize=None)
def tables():
    pos = np.arange(256)
    core_of, chip_of = pos // 128, pos % 128
    block = ((chip_of // 8) * 2 + core_of) * 8 + chip_of % 8
    m256 = []
    tb = np.zeros((2, 2, ROWS, 256), np.float32)
    ta = np.zeros((2, ROWS, 128), np.float32)
    beta, al = np.arange(256), np.arange(8)
    for core in (0, 1):
        sigma = row_sigma(core)
        cos, sin = phase(sigma[:128, None] * block[None, :], 512)
        fwd = np.concatenate([cos, -sin], 0)
        inv = np.concatenate([cos.T, -sin.T], 1)
        if core == 0:
            nyquist = phase(256 * block, 512)[0]
            fwd[128 + 96] = nyquist
            inv[:, 128 + 96] = nyquist
        inv = inv * (2.0 / FULL)
        m256.append(np.stack([*split_np(fwd), *split_np(inv)]))
        cos, sin = phase(sigma[:, None] * beta[None, :], FULL)
        tb[core, 0, :129], tb[core, 1, :129] = cos, -sin
        cos, sin = phase(sigma[:, None] * al[None, :], 4096)
        ta[core, :129, 0:8], ta[core, :129, 8:16] = cos, -sin
    cos, sin = phase(beta[:, None] * beta[None, :], 256)
    m512 = np.stack(split_np(np.block([[cos, -sin], [sin, cos]])))
    cos, sin = phase(al[:, None] * beta[None, :], 2048)
    t2 = np.stack([cos, -sin]).astype(np.float32)
    return np.stack(m256), m512, tb, ta, t2


def cmul(a, b, c, d):
    return a * c - b * d, a * d + b * c


def dft8(re, im, sign):
    root = math.sqrt(0.5)

    def turn(x, y, power):
        if power == 0:
            return x, y
        if power == 2:
            return (-y, x) if sign > 0 else (y, -x)
        if power == 1:
            if sign > 0:
                return (x - y) * root, (x + y) * root
            return (x + y) * root, (y - x) * root
        if sign > 0:
            return (-x - y) * root, (x - y) * root
        return (y - x) * root, (-x - y) * root

    def step(res, ims):
        n = len(res)
        if n == 1:
            return res, ims
        h = n // 2
        er = [res[j] + res[j + h] for j in range(h)]
        ei = [ims[j] + ims[j + h] for j in range(h)]
        odd = [turn(res[j] - res[j + h], ims[j] - ims[j + h], j * (8 // n)) for j in range(h)]
        er, ei = step(er, ei)
        dr, di = step([o[0] for o in odd], [o[1] for o in odd])
        outr, outi = [], []
        for j in range(h):
            outr += [er[j], dr[j]]
            outi += [ei[j], di[j]]
        return outr, outi

    return step(re, im)


def split(x):
    high = x.astype(BF16)
    return high, (x - high.astype(F32)).astype(BF16)


def dot(a, b):
    return jnp.dot(a, b, preferred_element_type=F32)


def dot_t(a, b):
    return lax.dot_general(a, b, (((1,), (1,)), ((), ())), preferred_element_type=F32)


def kernel(
    sig, filt, gate, skip, m256, m512, tb, ta, t2, out,
    fv, ev, gv, m256v, m512v, tbv, tav, t2v,
    s32, xs, xb, x32, fs, es, hb, eb, hf, fz, tw, zh, zl, gg, ce, ch, cl,
    yo, yw, pb, ye, yb, se, sb, lsem, ssem, rsem,
):
    ctx, cp = lax.axis_index("ctx"), lax.axis_index("cp")
    core = lax.rem(ctx, 2)
    other = 1 - core
    chip = (ctx // 2) * 8 + cp
    here = ctx * 8 + cp
    even = (1 - core).astype(F32)

    def device(t, k):
        return ((t // 8) * 2 + k, lax.rem(t, 8))

    def remote(src, dst, sem, t, k):
        return pltpu.make_async_remote_copy(
            src_ref=src, dst_ref=dst, send_sem=ssem.at[sem], recv_sem=rsem.at[sem],
            device_id=device(t, k), device_id_type=pl.DeviceIdType.MESH,
        )

    def loop(n, body, start=0):
        def wrapped(i, carry):
            body(i)
            return carry

        lax.fori_loop(start, n, wrapped, 0)

    barrier = pltpu.get_barrier_semaphore()

    def greet(i):
        t = lax.rem(here + i, 256)
        pl.semaphore_signal(
            barrier, inc=1, device_id=(t // 8, lax.rem(t, 8)), device_id_type=pl.DeviceIdType.MESH
        )

    loop(256, greet, 1)

    group, place = here // 64, lax.rem(here, 64)
    upper = (place >= 32).astype(jnp.int32)
    loads = [
        pltpu.make_async_copy(filt.at[:, pl.ds(upper * 8, 8)], fv, lsem.at[0]),
        pltpu.make_async_copy(filt.at[:, pl.ds(8, 1)], ev, lsem.at[1]),
        pltpu.make_async_copy(ta.at[core], tav, lsem.at[2]),
        pltpu.make_async_copy(tb.at[core], tbv, lsem.at[3]),
        pltpu.make_async_copy(m256.at[core], m256v, lsem.at[4]),
        pltpu.make_async_copy(m512, m512v, lsem.at[5]),
        pltpu.make_async_copy(t2, t2v, lsem.at[6]),
        pltpu.make_async_copy(gate, gv, lsem.at[7]),
    ]
    for load in loads:
        load.start()

    def turn_signal(a):
        block = sig[pl.ds(pl.multiple_of(a * 128, 128), 128), :].astype(F32)
        s32[pl.ds(a, 128, stride=16), :] = block.T

    loop(16, turn_signal)

    def pack(dst, base):
        def body(i):
            rows = s32[pl.ds(pl.multiple_of(i * 256, 256), 256), :]
            dst[pl.ds(base + i * 16, 16)] = rows.astype(BF16).reshape(16, 16, 128)

        loop(8, body)

    pack(xs, 0)

    loads[0].wait()
    loads[1].wait()

    def turn_filter(k):
        for blk in range(4):
            row = jnp.where(upper == 1, UPP[k][blk], LOW[k][blk])

            def body(j, row=row, blk=blk):
                ri, qh = j // 2, lax.rem(j, 2)
                block = fv[ri, row, pl.ds(pl.multiple_of(qh * 128, 128), 128), :].astype(F32)
                s32[pl.ds(ri * 8 + blk * 2 + qh, 128, stride=16), :] = block.T

            loop(4, body)

    for k in range(2):
        turn_filter(k)
        pack(fs, k * 128)

    @pl.when(here == 0)
    def _():
        def body(j):
            ri, qh = j // 2, lax.rem(j, 2)
            block = ev[ri, 0, pl.ds(pl.multiple_of(qh * 128, 128), 128), :].astype(F32).T
            for blk in range(4):
                s32[pl.ds(ri * 8 + blk * 2 + qh, 128, stride=16), :] = block

        loop(4, body)
        pack(es, 0)

    loads[2].wait()
    loads[3].wait()

    def make_twiddle(r):
        rows = pl.ds(pl.multiple_of(r * 16, 16), 16)
        cols = tav[rows, :]
        for al in range(8):
            c = jnp.broadcast_to(cols[:, al : al + 1], (16, 256))
            s = jnp.broadcast_to(cols[:, 8 + al : 9 + al], (16, 256))
            tw[al, 0, rows, :], tw[al, 1, rows, :] = cmul(c, s, tbv[0, rows, :], tbv[1, rows, :])

    loop(9, make_twiddle)

    pl.semaphore_wait(barrier, 255)
    slot = core * 128 + chip

    def send_signal(i):
        t = lax.rem(chip + i, 128)
        remote(xs.at[t], xb.at[slot], 0, t, core).start()

    pltpu.make_async_copy(xs.at[chip], xb.at[slot], rsem.at[0]).start()
    loop(128, send_signal, 1)

    fslot = jnp.where(upper == 1, (7 - group) * 32 + 63 - place, group * 32 + place)

    def send_filter(i):
        t = lax.rem(chip + i, 128)
        for k in range(2):
            remote(fs.at[k * 128 + t], hb.at[fslot], 1, t, k).start()

    pltpu.make_async_copy(fs.at[core * 128 + chip], hb.at[fslot], rsem.at[1]).start()
    remote(fs.at[other * 128 + chip], hb.at[fslot], 1, chip, other).start()
    loop(128, send_filter, 1)

    @pl.when(here == 0)
    def _():
        def body(t):
            remote(es.at[t], eb.at[0], 2, t, 0).start()

        pltpu.make_async_copy(es.at[0], eb.at[0], rsem.at[2]).start()
        loop(128, body, 1)

    mine = xb.at[pl.ds(core * 128, 128)]
    theirs = xb.at[pl.ds(other * 128, 128)]
    pltpu.make_async_copy(mine, mine, rsem.at[0]).wait()
    forward = remote(mine, mine, 3, chip, other)
    forward.start()
    for load in loads[4:]:
        load.wait()
    pltpu.make_async_copy(theirs, theirs, rsem.at[3]).wait()

    def widen(src, dst):
        def body(i):
            dst[pl.ds(pl.multiple_of(i * 256, 256), 256), :] = (
                src[pl.ds(i * 16, 16)].astype(F32).reshape(256, 128)
            )

        loop(16, body)

    widen(xb, x32)

    top = (lax.broadcasted_iota(jnp.int32, (8, 256), 0) == 0).astype(F32)

    def first(al):
        x = jnp.concatenate(
            [x32[pl.ds(2 * al, 256, stride=16), :], x32[pl.ds(2 * al + 1, 256, stride=16), :]], 1
        ).astype(BF16)
        f = dot(m256v[0], x) + dot(m256v[1], x)
        fz[al, 0, 0:128, :] = f[0:128]
        fz[al, 1, 0:128, :] = f[128:256]
        lone = f[224:232] * (top * even)
        fz[al, 1, 96:104, :] = f[224:232] - lone
        fz[al, 0, 128:136, :] = lone
        fz[al, 0, 136:144, :] = jnp.zeros((8, 256), F32)
        fz[al, 1, 128:144, :] = jnp.zeros((16, 256), F32)

    loop(8, first)

    def second(r):
        rows = pl.ds(pl.multiple_of(r * 16, 16), 16)
        for half in range(2):
            ln = slice(half * 128, half * 128 + 128)
            lm = slice(256 + half * 128, 384 + half * 128)
            pairs = [
                cmul(fz[al, 0, rows, ln], fz[al, 1, rows, ln], tw[al, 0, rows, ln], tw[al, 1, rows, ln])
                for al in range(8)
            ]
            re, im = dft8([p[0] for p in pairs], [p[1] for p in pairs], -1)
            for e in range(8):
                a, b = re[e], im[e]
                if e:
                    a, b = cmul(a, b, t2v[0, e : e + 1, ln], t2v[1, e : e + 1, ln])
                zh[e, rows, ln], zl[e, rows, ln] = split(a)
                zh[e, rows, lm], zl[e, rows, lm] = split(b)

    loop(9, second)

    def third(mul):
        def body(j):
            a = zh[pl.ds(j * 2, 2)].reshape(2 * ROWS, 512)
            b = zl[pl.ds(j * 2, 2)].reshape(2 * ROWS, 512)
            g = mul(a, m512v[0]) + mul(a, m512v[1]) + mul(b, m512v[0])
            gg[pl.ds(j * 2, 2)] = g.reshape(2, ROWS, 512)

        loop(4, body)

    third(dot)

    pltpu.make_async_copy(hb, hb, rsem.at[1]).wait()
    widen(hb, x32)

    def place_filter(e, shift):
        for ri in range(2):
            hf[e, ri, 128:144, :] = jnp.zeros((16, 256), F32)
            if shift:
                hf[e, ri, 96:104, :] = jnp.zeros((8, 256), F32)
            for blk in range(4):
                lo = blk * 32 + (1 if shift and blk == 3 else 0)
                for qh in range(2):
                    start = e * 512 + (ri * 8 + blk * 2 + qh)
                    hf[e, ri, lo : lo + 32, qh * 128 : qh * 128 + 128] = x32[
                        pl.ds(start, 32, stride=16), :
                    ]

    loop(4, lambda e: place_filter(e, False))

    @pl.when(core == 1)
    def _():
        loop(8, lambda e: place_filter(e, False), 4)

    @pl.when(core == 0)
    def _():
        loop(8, lambda e: place_filter(e, True), 4)
        pltpu.make_async_copy(eb, eb, rsem.at[2]).wait()
        extra = eb[0].astype(F32)
        for ri in range(2):
            hf[0, ri, 96:97, :] = hf[0, ri, 96:97, :] * 0.5
            for qh in range(2):
                row = ri * 8 + 6 + qh
                hf[4, ri, 96:97, qh * 128 : qh * 128 + 128] = extra[row : row + 1] * 0.5

    def apply_filter(e):
        def body(r):
            rows = pl.ds(pl.multiple_of(r * 16, 16), 16)
            a, b = cmul(
                gg[e, rows, 0:256], gg[e, rows, 256:512], hf[e, 0, rows, :], hf[e, 1, rows, :]
            )
            zh[e, rows, 0:256], zl[e, rows, 0:256] = split(a)
            zh[e, rows, 256:512], zl[e, rows, 256:512] = split(b)

        loop(9, body)

    loop(8, apply_filter)
    third(dot_t)

    def back(r, last):
        rows = pl.ds(r * 16, 16) if last else pl.ds(pl.multiple_of(r * 16, 16), 16)
        for half in range(2):
            ln = slice(half * 128, half * 128 + 128)
            lm = slice(256 + half * 128, 384 + half * 128)
            re, im = [], []
            for e in range(8):
                a, b = gg[e, rows, ln], gg[e, rows, lm]
                if e:
                    a, b = cmul(a, b, t2v[0, e : e + 1, ln], -t2v[1, e : e + 1, ln])
                re.append(a)
                im.append(b)
            re, im = dft8(re, im, 1)
            for al in range(8):
                a, b = cmul(re[al], im[al], tw[al, 0, rows, ln], -tw[al, 1, rows, ln])
                if last:
                    ce[al, :, ln] = a[0:8]
                else:
                    mark = top[:, 0:128] * (even * (r == 6).astype(F32))
                    head = b[0:8] * (1.0 - mark) + ce[al, 0:1, ln] * mark
                    b = jnp.concatenate([head, b[8:16]], 0)
                    down = pl.ds(pl.multiple_of(128 + r * 16, 16), 16)
                    ch[al, rows, ln], cl[al, rows, ln] = split(a)
                    ch[al, down, ln], cl[al, down, ln] = split(b)

    back(8, True)
    loop(8, lambda r: back(r, False))

    def combine(k, dst):
        rows = pl.ds(pl.multiple_of(k * 128, 128), 128)

        def body(al):
            vh, vl = m256v[2, rows, :], m256v[3, rows, :]
            y = dot(vh, ch[al]) + dot(vh, cl[al]) + dot(vl, ch[al])
            dst[pl.ds(2 * al, 128, stride=16), :] = y[:, 0:128]
            dst[pl.ds(2 * al + 1, 128, stride=16), :] = y[:, 128:256]

        loop(8, body)

    combine(other, yo)
    swap = remote(yo, pb, 4, chip, other)
    swap.start()
    combine(core, yw)
    pltpu.make_async_copy(pb, pb, rsem.at[4]).wait()

    weight = skip[chip]

    def add_up(i, peak):
        rows = pl.ds(pl.multiple_of(i * 128, 128), 128)
        x = xb[pl.ds(core * 128 + i * 8, 8)].astype(F32).reshape(128, 128)
        value = yw[rows, :] + pb[rows, :] + weight * x
        yw[rows, :] = value
        size = jnp.abs(value).reshape(16, 8, 128)
        return jnp.maximum(peak, jnp.max(size, axis=0))

    peak = lax.fori_loop(0, 16, add_up, jnp.zeros((8, 128), F32))
    peak = jnp.max(jnp.max(peak, axis=1, keepdims=True), axis=0, keepdims=True)
    peak = jnp.maximum(jnp.broadcast_to(peak, (1, 128)), 2.0**-118)
    se[0] = peak * (1.0 / SPAN)
    shrink = SPAN / peak

    def encode(i):
        rows = pl.ds(pl.multiple_of(i * 128, 128), 128)
        value = yw[rows, :] * shrink
        power = value * value
        power = power * power
        power = power * power
        power = power * power
        code = jnp.where(value < 0, -power, power)
        ye[pl.ds(i * 8, 8)] = code.astype(BF16).reshape(8, 16, 128)

    loop(16, encode)

    def send_out(i):
        t = lax.rem(chip + i, 128)
        remote(ye.at[t], yb.at[chip], 5, t, core).start()

    def send_scale(i):
        t = lax.rem(chip + i, 128)
        remote(se.at[0], sb.at[chip], 6, t, core).start()

    pltpu.make_async_copy(ye.at[chip], yb.at[chip], rsem.at[5]).start()
    pltpu.make_async_copy(se.at[0], sb.at[chip], rsem.at[6]).start()
    loop(128, send_out, 1)
    loop(128, send_scale, 1)
    pltpu.make_async_copy(sb, sb, rsem.at[6]).wait()
    pltpu.make_async_copy(yb, yb, rsem.at[5]).wait()

    def decode(i):
        for j in range(8):
            code = yb[i * 8 + j].astype(F32)
            size = jnp.exp2(jnp.log2(jnp.abs(code)) * (1.0 / 16)) * sb[i * 8 + j]
            rows = pl.ds(pl.multiple_of(i * 128 + j * 16, 16), 16)
            yo[rows, :] = jnp.where(code < 0, -size, size)

    def finish(a):
        rows = pl.ds(pl.multiple_of(a * 128, 128), 128)
        value = yo[pl.ds(a, 128, stride=16), :].T
        out[rows, :] = (gv[rows, :].astype(F32) * value).astype(BF16)

    swap.wait_send()
    loop(16, decode)
    loop(16, finish)

    def sent(ref, sem):
        pltpu.make_async_copy(ref, ref, ssem.at[sem]).wait()

    sent(xs.at[pl.ds(0, 127)], 0)
    sent(fs.at[pl.ds(0, 255)], 1)

    @pl.when(here == 0)
    def _():
        sent(es.at[pl.ds(0, 127)], 2)

    forward.wait_send()
    sent(ye.at[pl.ds(0, 127)], 5)
    sent(sb.at[pl.ds(0, 127)], 6)


def body(signal, gate, filters, skip):
    m256, m512, tb, ta, t2 = (jnp.asarray(t) for t in tables())
    vmem = pl.BlockSpec(memory_space=pltpu.VMEM)
    hbm = pl.BlockSpec(memory_space=pl.ANY)
    smem = pl.BlockSpec(memory_space=pltpu.SMEM)
    return pl.pallas_call(
        kernel,
        out_shape=jax.ShapeDtypeStruct(signal.shape, BF16),
        in_specs=[vmem, hbm, hbm, smem, hbm, hbm, hbm, hbm, hbm],
        out_specs=vmem,
        scratch_shapes=[
            pltpu.VMEM((2, 8, 256, 128), BF16),
            pltpu.VMEM((2, 1, 256, 128), BF16),
            pltpu.VMEM((2048, 128), BF16),
            pltpu.VMEM((4, 256, 256), BF16),
            pltpu.VMEM((2, 512, 512), BF16),
            pltpu.VMEM((2, ROWS, 256), F32),
            pltpu.VMEM((ROWS, 128), F32),
            pltpu.VMEM((2, 8, 256), F32),
            pltpu.VMEM((2048, 128), F32),
            pltpu.VMEM((128, 16, 128), BF16),
            pltpu.VMEM((256, 16, 128), BF16),
            pltpu.VMEM((4096, 128), F32),
            pltpu.VMEM((256, 16, 128), BF16),
            pltpu.VMEM((128, 16, 128), BF16),
            pltpu.VMEM((256, 16, 128), BF16),
            pltpu.VMEM((1, 16, 128), BF16),
            pltpu.VMEM((8, 2, ROWS, 256), F32),
            pltpu.VMEM((8, 2, ROWS, 256), F32),
            pltpu.VMEM((8, 2, ROWS, 256), F32),
            pltpu.VMEM((8, ROWS, 512), BF16),
            pltpu.VMEM((8, ROWS, 512), BF16),
            pltpu.VMEM((8, ROWS, 512), F32),
            pltpu.VMEM((8, 8, 256), F32),
            pltpu.VMEM((8, 256, 256), BF16),
            pltpu.VMEM((8, 256, 256), BF16),
            pltpu.VMEM((2048, 128), F32),
            pltpu.VMEM((2048, 128), F32),
            pltpu.VMEM((2048, 128), F32),
            pltpu.VMEM((128, 16, 128), BF16),
            pltpu.VMEM((128, 16, 128), BF16),
            pltpu.VMEM((1, 1, 128), F32),
            pltpu.VMEM((128, 1, 128), F32),
            pltpu.SemaphoreType.DMA((8,)),
            pltpu.SemaphoreType.DMA((7,)),
            pltpu.SemaphoreType.DMA((7,)),
        ],
        compiler_params=pltpu.CompilerParams(
            collective_id=0, has_side_effects=True, vmem_limit_bytes=56 << 20
        ),
    )(signal, filters, gate, skip, m256, m512, tb, ta, t2)


def solution(mesh):
    placed = (
        P(("ctx", "cp"), None),
        P(("ctx", "cp"), None),
        P(None, ("ctx", "cp"), None, None),
        P(),
    )
    return jax.shard_map(
        body, mesh=mesh, in_specs=placed, out_specs=P(("ctx", "cp"), None), check_vma=False
    )
```

```python
import functools
import math

import jax
import jax.numpy as jnp
import ml_dtypes
import numpy as np
from jax import lax
from jax.experimental import pallas as pl
from jax.experimental.pallas import tpu as pltpu
from jax.sharding import PartitionSpec as P


FULL = 1 << 20
SPAN = 2.0**7.75
ROWS = 144
F32 = jnp.float32
BF16 = jnp.bfloat16

LOW = ((2, 4, 6, 0), (3, 5, 7, 1))
UPP = ((6, 4, 2, 0), (5, 3, 1, 7))


def phase(product, length):
    angle = 2 * math.pi * (np.asarray(product, dtype=np.int64) % length) / length
    return np.cos(angle), np.sin(angle)


def split_np(array):
    high = array.astype(ml_dtypes.bfloat16)
    low = (array - high.astype(np.float64)).astype(ml_dtypes.bfloat16)
    return high, low


def row_sigma(core):
    index = np.concatenate([4 * np.arange(32) + t for t in (1, 2, 3, 0)] + [np.array([128])])
    sigma = 2 * index + core
    if core == 1:
        sigma[128] = 0
    return sigma


@functools.lru_cache(maxsize=None)
def tables():
    pos = np.arange(256)
    core_of, chip_of = pos // 128, pos % 128
    block = ((chip_of // 8) * 2 + core_of) * 8 + chip_of % 8
    m256 = []
    tb = np.zeros((2, 2, ROWS, 256), np.float32)
    ta = np.zeros((2, ROWS, 128), np.float32)
    beta, al = np.arange(256), np.arange(8)
    for core in (0, 1):
        sigma = row_sigma(core)
        cos, sin = phase(sigma[:128, None] * block[None, :], 512)
        fwd = np.concatenate([cos, -sin], 0)
        inv = np.concatenate([cos.T, -sin.T], 1)
        if core == 0:
            nyquist = phase(256 * block, 512)[0]
            fwd[128 + 96] = nyquist
            inv[:, 128 + 96] = nyquist
        inv = np.roll(inv, 128 * core - 128, axis=0) * (2.0 / FULL)
        m256.append(np.stack([*split_np(fwd), *split_np(inv)]))
        cos, sin = phase(sigma[:, None] * beta[None, :], FULL)
        tb[core, 0, :129], tb[core, 1, :129] = cos, -sin
        cos, sin = phase(sigma[:, None] * al[None, :], 4096)
        ta[core, :129, 0:8], ta[core, :129, 8:16] = cos, -sin
    cos, sin = phase(beta[:, None] * beta[None, :], 256)
    m512 = np.stack(split_np(np.block([[cos, -sin], [sin, cos]])))
    cos, sin = phase(al[:, None] * beta[None, :], 2048)
    t2 = np.stack([cos, -sin]).astype(np.float32)
    return np.stack(m256), m512, tb, ta, t2


def cmul(a, b, c, d):
    return a * c - b * d, a * d + b * c


def dft8(re, im, sign):
    root = math.sqrt(0.5)

    def turn(x, y, power):
        if power == 0:
            return x, y
        if power == 2:
            return (-y, x) if sign > 0 else (y, -x)
        if power == 1:
            if sign > 0:
                return (x - y) * root, (x + y) * root
            return (x + y) * root, (y - x) * root
        if sign > 0:
            return (-x - y) * root, (x - y) * root
        return (y - x) * root, (-x - y) * root

    def step(res, ims):
        n = len(res)
        if n == 1:
            return res, ims
        h = n // 2
        er = [res[j] + res[j + h] for j in range(h)]
        ei = [ims[j] + ims[j + h] for j in range(h)]
        odd = [turn(res[j] - res[j + h], ims[j] - ims[j + h], j * (8 // n)) for j in range(h)]
        er, ei = step(er, ei)
        dr, di = step([o[0] for o in odd], [o[1] for o in odd])
        outr, outi = [], []
        for j in range(h):
            outr += [er[j], dr[j]]
            outi += [ei[j], di[j]]
        return outr, outi

    return step(re, im)


def split(x):
    high = x.astype(BF16)
    return high, (x - high.astype(F32)).astype(BF16)


def dot(a, b):
    return jnp.dot(a, b, preferred_element_type=F32)


def dot_t(a, b):
    return lax.dot_general(a, b, (((1,), (1,)), ((), ())), preferred_element_type=F32)


def kernel(
    sig, filt, gate, skip, m256, m512, tb, ta, t2, out,
    fv, ev, gv, m256v, m512v, tbv, tav, t2v,
    s32, xs, xb, x32, fs, es, hb, eb, hf, fz, tw, zh, zl, gg, ce, ch, cl,
    yo, yw, pb, v32, h32, ye, yb, se, sb, lsem, ssem, rsem, swap_s, swap_r,
):
    ctx, cp = lax.axis_index("ctx"), lax.axis_index("cp")
    core = lax.rem(ctx, 2)
    other = 1 - core
    chip = (ctx // 2) * 8 + cp
    here = ctx * 8 + cp
    even = (1 - core).astype(F32)

    def device(t, k):
        return ((t // 8) * 2 + k, lax.rem(t, 8))

    def remote(src, dst, sem, t, k):
        return pltpu.make_async_remote_copy(
            src_ref=src, dst_ref=dst, send_sem=ssem.at[sem], recv_sem=rsem.at[sem],
            device_id=device(t, k), device_id_type=pl.DeviceIdType.MESH,
        )

    def loop(n, body, start=0):
        def wrapped(i, carry):
            body(i)
            return carry

        lax.fori_loop(start, n, wrapped, 0)

    barrier = pltpu.get_barrier_semaphore()

    def greet(i):
        t = lax.rem(here + i, 256)
        pl.semaphore_signal(
            barrier, inc=1, device_id=(t // 8, lax.rem(t, 8)), device_id_type=pl.DeviceIdType.MESH
        )

    loop(256, greet, 1)

    group, place = here // 64, lax.rem(here, 64)
    upper = (place >= 32).astype(jnp.int32)
    loads = [
        pltpu.make_async_copy(filt.at[:, pl.ds(upper * 8, 8)], fv, lsem.at[0]),
        pltpu.make_async_copy(filt.at[:, pl.ds(8, 1)], ev, lsem.at[1]),
        pltpu.make_async_copy(ta.at[core], tav, lsem.at[2]),
        pltpu.make_async_copy(tb.at[core], tbv, lsem.at[3]),
        pltpu.make_async_copy(m256.at[core], m256v, lsem.at[4]),
        pltpu.make_async_copy(m512, m512v, lsem.at[5]),
        pltpu.make_async_copy(t2, t2v, lsem.at[6]),
        pltpu.make_async_copy(gate, gv, lsem.at[7]),
    ]
    for load in loads:
        load.start()

    def turn_signal(a):
        block = sig[pl.ds(pl.multiple_of(a * 128, 128), 128), :].astype(F32)
        s32[pl.ds(a, 128, stride=16), :] = block.T

    loop(16, turn_signal)

    def pack(dst, base):
        def body(i):
            rows = s32[pl.ds(pl.multiple_of(i * 256, 256), 256), :]
            dst[pl.ds(base + i * 16, 16)] = rows.astype(BF16).reshape(16, 16, 128)

        loop(8, body)

    pack(xs, 0)

    loads[0].wait()
    loads[1].wait()

    def turn_filter(k):
        for blk in range(4):
            row = jnp.where(upper == 1, UPP[k][blk], LOW[k][blk])

            def body(j, row=row, blk=blk):
                ri, qh = j // 2, lax.rem(j, 2)
                block = fv[ri, row, pl.ds(pl.multiple_of(qh * 128, 128), 128), :].astype(F32)
                s32[pl.ds(ri * 8 + blk * 2 + qh, 128, stride=16), :] = block.T

            loop(4, body)

    for k in range(2):
        turn_filter(k)
        pack(fs, k * 128)

    @pl.when(here == 0)
    def _():
        def body(j):
            ri, qh = j // 2, lax.rem(j, 2)
            block = ev[ri, 0, pl.ds(pl.multiple_of(qh * 128, 128), 128), :].astype(F32).T
            for blk in range(4):
                s32[pl.ds(ri * 8 + blk * 2 + qh, 128, stride=16), :] = block

        loop(4, body)
        pack(es, 0)

    loads[2].wait()
    loads[3].wait()

    def make_twiddle(r):
        rows = pl.ds(pl.multiple_of(r * 16, 16), 16)
        cols = tav[rows, :]
        for al in range(8):
            c = jnp.broadcast_to(cols[:, al : al + 1], (16, 256))
            s = jnp.broadcast_to(cols[:, 8 + al : 9 + al], (16, 256))
            tw[al, 0, rows, :], tw[al, 1, rows, :] = cmul(c, s, tbv[0, rows, :], tbv[1, rows, :])

    loop(9, make_twiddle)

    pl.semaphore_wait(barrier, 255)
    slot = core * 128 + chip

    def send_signal(i):
        t = lax.rem(chip + i, 128)
        remote(xs.at[t], xb.at[slot], 0, t, core).start()

    pltpu.make_async_copy(xs.at[chip], xb.at[slot], rsem.at[0]).start()
    loop(128, send_signal, 1)

    fslot = jnp.where(upper == 1, (7 - group) * 32 + 63 - place, group * 32 + place)

    def send_filter(i):
        t = lax.rem(chip + i, 128)
        for k in range(2):
            remote(fs.at[k * 128 + t], hb.at[fslot], 1, t, k).start()

    pltpu.make_async_copy(fs.at[core * 128 + chip], hb.at[fslot], rsem.at[1]).start()
    remote(fs.at[other * 128 + chip], hb.at[fslot], 1, chip, other).start()
    loop(128, send_filter, 1)

    @pl.when(here == 0)
    def _():
        def body(t):
            remote(es.at[t], eb.at[0], 2, t, 0).start()

        pltpu.make_async_copy(es.at[0], eb.at[0], rsem.at[2]).start()
        loop(128, body, 1)

    mine = xb.at[pl.ds(core * 128, 128)]
    theirs = xb.at[pl.ds(other * 128, 128)]
    pltpu.make_async_copy(mine, mine, rsem.at[0]).wait()
    forward = remote(mine, mine, 3, chip, other)
    forward.start()
    for load in loads[4:]:
        load.wait()
    pltpu.make_async_copy(theirs, theirs, rsem.at[3]).wait()

    def widen(src, dst):
        def body(i):
            dst[pl.ds(pl.multiple_of(i * 256, 256), 256), :] = (
                src[pl.ds(i * 16, 16)].astype(F32).reshape(256, 128)
            )

        loop(16, body)

    widen(xb, x32)

    top = (lax.broadcasted_iota(jnp.int32, (8, 256), 0) == 0).astype(F32)

    def first(al):
        x = jnp.concatenate(
            [x32[pl.ds(2 * al, 256, stride=16), :], x32[pl.ds(2 * al + 1, 256, stride=16), :]], 1
        ).astype(BF16)
        f = dot(m256v[0], x) + dot(m256v[1], x)
        fz[al, 0, 0:128, :] = f[0:128]
        fz[al, 1, 0:128, :] = f[128:256]
        lone = f[224:232] * (top * even)
        fz[al, 1, 96:104, :] = f[224:232] - lone
        fz[al, 0, 128:136, :] = lone
        fz[al, 0, 136:144, :] = jnp.zeros((8, 256), F32)
        fz[al, 1, 128:144, :] = jnp.zeros((16, 256), F32)

    loop(8, first)

    def second(r):
        rows = pl.ds(pl.multiple_of(r * 16, 16), 16)
        for half in range(2):
            ln = slice(half * 128, half * 128 + 128)
            lm = slice(256 + half * 128, 384 + half * 128)
            pairs = [
                cmul(fz[al, 0, rows, ln], fz[al, 1, rows, ln], tw[al, 0, rows, ln], tw[al, 1, rows, ln])
                for al in range(8)
            ]
            re, im = dft8([p[0] for p in pairs], [p[1] for p in pairs], -1)
            for e in range(8):
                a, b = re[e], im[e]
                if e:
                    a, b = cmul(a, b, t2v[0, e : e + 1, ln], t2v[1, e : e + 1, ln])
                zh[e, rows, ln], zl[e, rows, ln] = split(a)
                zh[e, rows, lm], zl[e, rows, lm] = split(b)

    loop(9, second)

    def third(mul):
        def body(j):
            a = zh[pl.ds(j * 2, 2)].reshape(2 * ROWS, 512)
            b = zl[pl.ds(j * 2, 2)].reshape(2 * ROWS, 512)
            g = mul(a, m512v[0]) + mul(a, m512v[1]) + mul(b, m512v[0])
            gg[pl.ds(j * 2, 2)] = g.reshape(2, ROWS, 512)

        loop(4, body)

    third(dot)

    pltpu.make_async_copy(hb, hb, rsem.at[1]).wait()
    widen(hb, h32)

    def place_filter(e, shift):
        for ri in range(2):
            hf[e, ri, 128:144, :] = jnp.zeros((16, 256), F32)
            if shift:
                hf[e, ri, 96:104, :] = jnp.zeros((8, 256), F32)
            for blk in range(4):
                lo = blk * 32 + (1 if shift and blk == 3 else 0)
                for qh in range(2):
                    start = e * 512 + (ri * 8 + blk * 2 + qh)
                    hf[e, ri, lo : lo + 32, qh * 128 : qh * 128 + 128] = h32[
                        pl.ds(start, 32, stride=16), :
                    ]

    loop(4, lambda e: place_filter(e, False))

    @pl.when(core == 1)
    def _():
        loop(8, lambda e: place_filter(e, False), 4)

    @pl.when(core == 0)
    def _():
        loop(8, lambda e: place_filter(e, True), 4)
        pltpu.make_async_copy(eb, eb, rsem.at[2]).wait()
        extra = eb[0].astype(F32)
        for ri in range(2):
            hf[0, ri, 96:97, :] = hf[0, ri, 96:97, :] * 0.5
            for qh in range(2):
                row = ri * 8 + 6 + qh
                hf[4, ri, 96:97, qh * 128 : qh * 128 + 128] = extra[row : row + 1] * 0.5

    def apply_filter(e):
        def body(r):
            rows = pl.ds(pl.multiple_of(r * 16, 16), 16)
            a, b = cmul(
                gg[e, rows, 0:256], gg[e, rows, 256:512], hf[e, 0, rows, :], hf[e, 1, rows, :]
            )
            zh[e, rows, 0:256], zl[e, rows, 0:256] = split(a)
            zh[e, rows, 256:512], zl[e, rows, 256:512] = split(b)

        loop(9, body)

    loop(8, apply_filter)
    third(dot_t)

    def back(r, last):
        rows = pl.ds(r * 16, 16) if last else pl.ds(pl.multiple_of(r * 16, 16), 16)
        for half in range(2):
            ln = slice(half * 128, half * 128 + 128)
            lm = slice(256 + half * 128, 384 + half * 128)
            re, im = [], []
            for e in range(8):
                a, b = gg[e, rows, ln], gg[e, rows, lm]
                if e:
                    a, b = cmul(a, b, t2v[0, e : e + 1, ln], -t2v[1, e : e + 1, ln])
                re.append(a)
                im.append(b)
            re, im = dft8(re, im, 1)
            for al in range(8):
                a, b = cmul(re[al], im[al], tw[al, 0, rows, ln], -tw[al, 1, rows, ln])
                if last:
                    ce[al, :, ln] = a[0:8]
                else:
                    mark = top[:, 0:128] * (even * (r == 6).astype(F32))
                    head = b[0:8] * (1.0 - mark) + ce[al, 0:1, ln] * mark
                    b = jnp.concatenate([head, b[8:16]], 0)
                    down = pl.ds(pl.multiple_of(128 + r * 16, 16), 16)
                    ch[al, rows, ln], cl[al, rows, ln] = split(a)
                    ch[al, down, ln], cl[al, down, ln] = split(b)

    back(8, True)
    loop(8, lambda r: back(r, False))

    def swap(al):
        return pltpu.make_async_remote_copy(
            src_ref=yo.at[al], dst_ref=pb.at[al], send_sem=swap_s.at[al], recv_sem=swap_r.at[al],
            device_id=device(chip, other), device_id_type=pl.DeviceIdType.MESH,
        )

    def combine(al):
        vh, vl = m256v[2], m256v[3]
        y = dot(vh, ch[al]) + dot(vh, cl[al]) + dot(vl, ch[al])
        yo[al] = y[0:128]
        swap(al).start()
        yw[al] = y[128:256]

    loop(8, combine)

    weight = skip[chip]

    def add_up(al, peak):
        swap(al).wait()
        for half in range(2):
            ln = slice(half * 128, half * 128 + 128)
            x = x32[pl.ds(core * 2048 + 2 * al + half, 128, stride=16), :]
            value = yw[al, :, ln] + pb[al, :, ln] + weight * x
            v32[pl.ds(2 * al + half, 128, stride=16), :] = value
            peak = jnp.maximum(peak, jnp.max(jnp.abs(value).reshape(16, 8, 128), axis=0))
        return peak

    peak = lax.fori_loop(0, 8, add_up, jnp.zeros((8, 128), F32))
    peak = jnp.max(jnp.max(peak, axis=1, keepdims=True), axis=0, keepdims=True)
    peak = jnp.maximum(jnp.broadcast_to(peak, (1, 128)), 2.0**-118)
    se[0] = peak * (1.0 / SPAN)
    shrink = SPAN / peak

    def encode(i):
        rows = pl.ds(pl.multiple_of(i * 128, 128), 128)
        value = v32[rows, :] * shrink
        power = value * value
        power = power * power
        power = power * power
        power = power * power
        code = jnp.where(value < 0, -power, power)
        ye[pl.ds(i * 8, 8)] = code.astype(BF16).reshape(8, 16, 128)

    loop(16, encode)

    def send_out(i):
        t = lax.rem(chip + i, 128)
        remote(ye.at[t], yb.at[chip], 5, t, core).start()

    def send_scale(i):
        t = lax.rem(chip + i, 128)
        remote(se.at[0], sb.at[chip], 6, t, core).start()

    pltpu.make_async_copy(ye.at[chip], yb.at[chip], rsem.at[5]).start()
    pltpu.make_async_copy(se.at[0], sb.at[chip], rsem.at[6]).start()
    loop(128, send_out, 1)
    loop(128, send_scale, 1)
    pltpu.make_async_copy(sb, sb, rsem.at[6]).wait()
    pltpu.make_async_copy(yb, yb, rsem.at[5]).wait()

    def decode(i):
        for j in range(8):
            code = yb[i * 8 + j].astype(F32)
            size = jnp.maximum(jnp.abs(code), 2.0**-126)
            size = lax.rsqrt(lax.rsqrt(lax.rsqrt(lax.rsqrt(size)))) * sb[i * 8 + j]
            rows = pl.ds(pl.multiple_of(i * 128 + j * 16, 16), 16)
            s32[rows, :] = jnp.where(code < 0, -size, size)

    def finish(a):
        rows = pl.ds(pl.multiple_of(a * 128, 128), 128)
        value = s32[pl.ds(a, 128, stride=16), :].T
        out[rows, :] = (gv[rows, :].astype(F32) * value).astype(BF16)

    loop(16, decode)
    loop(16, finish)

    def sent(ref, sem):
        pltpu.make_async_copy(ref, ref, ssem.at[sem]).wait()

    sent(xs.at[pl.ds(0, 127)], 0)
    sent(fs.at[pl.ds(0, 255)], 1)

    @pl.when(here == 0)
    def _():
        sent(es.at[pl.ds(0, 127)], 2)

    forward.wait_send()
    sent(ye.at[pl.ds(0, 127)], 5)
    sent(sb.at[pl.ds(0, 127)], 6)


def body(signal, gate, filters, skip):
    m256, m512, tb, ta, t2 = (jnp.asarray(t) for t in tables())
    vmem = pl.BlockSpec(memory_space=pltpu.VMEM)
    hbm = pl.BlockSpec(memory_space=pl.ANY)
    smem = pl.BlockSpec(memory_space=pltpu.SMEM)
    return pl.pallas_call(
        kernel,
        out_shape=jax.ShapeDtypeStruct(signal.shape, BF16),
        in_specs=[vmem, hbm, hbm, smem, hbm, hbm, hbm, hbm, hbm],
        out_specs=vmem,
        scratch_shapes=[
            pltpu.VMEM((2, 8, 256, 128), BF16),
            pltpu.VMEM((2, 1, 256, 128), BF16),
            pltpu.VMEM((2048, 128), BF16),
            pltpu.VMEM((4, 256, 256), BF16),
            pltpu.VMEM((2, 512, 512), BF16),
            pltpu.VMEM((2, ROWS, 256), F32),
            pltpu.VMEM((ROWS, 128), F32),
            pltpu.VMEM((2, 8, 256), F32),
            pltpu.VMEM((2048, 128), F32),
            pltpu.VMEM((128, 16, 128), BF16),
            pltpu.VMEM((256, 16, 128), BF16),
            pltpu.VMEM((4096, 128), F32),
            pltpu.VMEM((256, 16, 128), BF16),
            pltpu.VMEM((128, 16, 128), BF16),
            pltpu.VMEM((256, 16, 128), BF16),
            pltpu.VMEM((1, 16, 128), BF16),
            pltpu.VMEM((8, 2, ROWS, 256), F32),
            pltpu.VMEM((8, 2, ROWS, 256), F32),
            pltpu.VMEM((8, 2, ROWS, 256), F32),
            pltpu.VMEM((8, ROWS, 512), BF16),
            pltpu.VMEM((8, ROWS, 512), BF16),
            pltpu.VMEM((8, ROWS, 512), F32),
            pltpu.VMEM((8, 8, 256), F32),
            pltpu.VMEM((8, 256, 256), BF16),
            pltpu.VMEM((8, 256, 256), BF16),
            pltpu.VMEM((8, 128, 256), F32),
            pltpu.VMEM((8, 128, 256), F32),
            pltpu.VMEM((8, 128, 256), F32),
            pltpu.VMEM((2048, 128), F32),
            pltpu.VMEM((4096, 128), F32),
            pltpu.VMEM((128, 16, 128), BF16),
            pltpu.VMEM((128, 16, 128), BF16),
            pltpu.VMEM((1, 1, 128), F32),
            pltpu.VMEM((128, 1, 128), F32),
            pltpu.SemaphoreType.DMA((8,)),
            pltpu.SemaphoreType.DMA((7,)),
            pltpu.SemaphoreType.DMA((7,)),
            pltpu.SemaphoreType.DMA((8,)),
            pltpu.SemaphoreType.DMA((8,)),
        ],
        compiler_params=pltpu.CompilerParams(
            collective_id=0, has_side_effects=True, vmem_limit_bytes=56 << 20
        ),
    )(signal, filters, gate, skip, m256, m512, tb, ta, t2)


def solution(mesh):
    placed = (
        P(("ctx", "cp"), None),
        P(("ctx", "cp"), None),
        P(None, ("ctx", "cp"), None, None),
        P(),
    )
    return jax.shard_map(
        body, mesh=mesh, in_specs=placed, out_specs=P(("ctx", "cp"), None), check_vma=False
    )
```

```python
import functools
import math

import jax
import jax.numpy as jnp
import ml_dtypes
import numpy as np
from jax import lax
from jax.experimental import pallas as pl
from jax.experimental.pallas import tpu as pltpu
from jax.sharding import PartitionSpec as P


FULL = 1 << 20
SPAN = 2.0**7.75
ROWS = 144
F32 = jnp.float32
BF16 = jnp.bfloat16

LOW = ((2, 4, 6, 0), (3, 5, 7, 1))
UPP = ((6, 4, 2, 0), (5, 3, 1, 7))


def phase(product, length):
    angle = 2 * math.pi * (np.asarray(product, dtype=np.int64) % length) / length
    return np.cos(angle), np.sin(angle)


def split_np(array):
    high = array.astype(ml_dtypes.bfloat16)
    low = (array - high.astype(np.float64)).astype(ml_dtypes.bfloat16)
    return high, low


def row_sigma(core):
    index = np.concatenate([4 * np.arange(32) + t for t in (1, 2, 3, 0)] + [np.array([128])])
    sigma = 2 * index + core
    if core == 1:
        sigma[128] = 0
    return sigma


@functools.lru_cache(maxsize=None)
def tables():
    pos = np.arange(256)
    core_of, chip_of = pos // 128, pos % 128
    block = ((chip_of // 8) * 2 + core_of) * 8 + chip_of % 8
    m256 = []
    tb = np.zeros((2, 2, ROWS, 256), np.float32)
    ta = np.zeros((2, ROWS, 128), np.float32)
    beta, al = np.arange(256), np.arange(8)
    for core in (0, 1):
        sigma = row_sigma(core)
        cos, sin = phase(sigma[:128, None] * block[None, :], 512)
        fwd = np.concatenate([cos, -sin], 0)
        inv = np.concatenate([cos.T, -sin.T], 1)
        if core == 0:
            nyquist = phase(256 * block, 512)[0]
            fwd[128 + 96] = nyquist
            inv[:, 128 + 96] = nyquist
        inv = np.roll(inv, 128 * core - 128, axis=0) * (2.0 / FULL)
        m256.append(np.stack([*split_np(fwd), *split_np(inv)]))
        cos, sin = phase(sigma[:, None] * beta[None, :], FULL)
        tb[core, 0, :129], tb[core, 1, :129] = cos, -sin
        cos, sin = phase(sigma[:, None] * al[None, :], 4096)
        ta[core, :129, 0:8], ta[core, :129, 8:16] = cos, -sin
    cos, sin = phase(beta[:, None] * beta[None, :], 256)
    m512 = np.stack(split_np(np.block([[cos, -sin], [sin, cos]])))
    cos, sin = phase(al[:, None] * beta[None, :], 2048)
    t2 = np.stack([cos, -sin]).astype(np.float32)
    return np.stack(m256), m512, tb, ta, t2


def cmul(a, b, c, d):
    return a * c - b * d, a * d + b * c


def dft8(re, im, sign):
    root = math.sqrt(0.5)

    def turn(x, y, power):
        if power == 0:
            return x, y
        if power == 2:
            return (-y, x) if sign > 0 else (y, -x)
        if power == 1:
            if sign > 0:
                return (x - y) * root, (x + y) * root
            return (x + y) * root, (y - x) * root
        if sign > 0:
            return (-x - y) * root, (x - y) * root
        return (y - x) * root, (-x - y) * root

    def step(res, ims):
        n = len(res)
        if n == 1:
            return res, ims
        h = n // 2
        er = [res[j] + res[j + h] for j in range(h)]
        ei = [ims[j] + ims[j + h] for j in range(h)]
        odd = [turn(res[j] - res[j + h], ims[j] - ims[j + h], j * (8 // n)) for j in range(h)]
        er, ei = step(er, ei)
        dr, di = step([o[0] for o in odd], [o[1] for o in odd])
        outr, outi = [], []
        for j in range(h):
            outr += [er[j], dr[j]]
            outi += [ei[j], di[j]]
        return outr, outi

    return step(re, im)


def split(x):
    high = x.astype(BF16)
    return high, (x - high.astype(F32)).astype(BF16)


def dot(a, b):
    return jnp.dot(a, b, preferred_element_type=F32)


def dot_t(a, b):
    return lax.dot_general(a, b, (((1,), (1,)), ((), ())), preferred_element_type=F32)


def kernel(
    sig, filt, gate, skip, m256, m512, tb, ta, t2, out,
    fv, ev, gv, m256v, m512v, tbv, tav, t2v,
    s32, xs, xb, x32, fs, hb, hf, fz, tw, zh, zl, gg, ce, ch, cl,
    yo, yw, pb, v32, h32, ye, yb, se, sb, lsem, ssem, rsem, swap_s, swap_r,
):
    ctx, cp = lax.axis_index("ctx"), lax.axis_index("cp")
    core = lax.rem(ctx, 2)
    other = 1 - core
    chip = (ctx // 2) * 8 + cp
    here = ctx * 8 + cp
    even = (1 - core).astype(F32)

    def device(t, k):
        return ((t // 8) * 2 + k, lax.rem(t, 8))

    def remote(src, dst, sem, t, k):
        return pltpu.make_async_remote_copy(
            src_ref=src, dst_ref=dst, send_sem=ssem.at[sem], recv_sem=rsem.at[sem],
            device_id=device(t, k), device_id_type=pl.DeviceIdType.MESH,
        )

    def loop(n, body, start=0):
        def wrapped(i, carry):
            body(i)
            return carry

        lax.fori_loop(start, n, wrapped, 0)

    barrier = pltpu.get_barrier_semaphore()

    def greet(i):
        t = lax.rem(here + i, 256)
        pl.semaphore_signal(
            barrier, inc=1, device_id=(t // 8, lax.rem(t, 8)), device_id_type=pl.DeviceIdType.MESH
        )

    loop(256, greet, 1)

    group, place = here // 64, lax.rem(here, 64)
    upper = (place >= 32).astype(jnp.int32)
    loads = [
        pltpu.make_async_copy(filt.at[:, pl.ds(upper * 8, 8)], fv, lsem.at[0]),
        pltpu.make_async_copy(filt.at[:, pl.ds(8, 1), pl.ds(0, 128)], ev, lsem.at[1]),
        pltpu.make_async_copy(ta.at[core], tav, lsem.at[2]),
        pltpu.make_async_copy(tb.at[core], tbv, lsem.at[3]),
        pltpu.make_async_copy(m256.at[core], m256v, lsem.at[4]),
        pltpu.make_async_copy(m512, m512v, lsem.at[5]),
        pltpu.make_async_copy(t2, t2v, lsem.at[6]),
        pltpu.make_async_copy(gate, gv, lsem.at[7]),
    ]
    for load in loads:
        load.start()

    def turn_signal(a):
        block = sig[pl.ds(pl.multiple_of(a * 128, 128), 128), :].astype(F32)
        s32[pl.ds(a, 128, stride=16), :] = block.T

    loop(16, turn_signal)

    def pack(dst, base):
        def body(i):
            rows = s32[pl.ds(pl.multiple_of(i * 256, 256), 256), :]
            dst[pl.ds(base + i * 16, 16)] = rows.astype(BF16).reshape(16, 16, 128)

        loop(8, body)

    pack(xs, 0)

    loads[0].wait()
    loads[1].wait()

    def turn_filter(k):
        for blk in range(4):
            row = jnp.where(upper == 1, UPP[k][blk], LOW[k][blk])

            def body(j, row=row, blk=blk):
                ri, qh = j // 2, lax.rem(j, 2)
                block = fv[ri, row, pl.ds(pl.multiple_of(qh * 128, 128), 128), :].astype(F32)
                s32[pl.ds(ri * 8 + blk * 2 + qh, 128, stride=16), :] = block.T

            loop(4, body)

    def pack_mirrors():
        for ri in range(2):
            s32[pl.ds(ri * 8 + 7, 128, stride=16), :] = ev[ri, 0].astype(F32).T
        head = lax.broadcasted_iota(jnp.int32, (128, 128), 0) == 0
        middle = fv[0, 0, 128:136, :].astype(F32)[0:1]
        block = jnp.where(head, middle, fv[1, 0, 0:128, :].astype(F32))
        s32[pl.ds(8 + 6, 128, stride=16), :] = block.T

    turn_filter(0)
    pl.when(here == 0)(pack_mirrors)
    pack(fs, 0)
    turn_filter(1)
    pack(fs, 128)

    loads[2].wait()
    loads[3].wait()

    def make_twiddle(r):
        rows = pl.ds(pl.multiple_of(r * 16, 16), 16)
        cols = tav[rows, :]
        for al in range(8):
            c = jnp.broadcast_to(cols[:, al : al + 1], (16, 256))
            s = jnp.broadcast_to(cols[:, 8 + al : 9 + al], (16, 256))
            tw[al, 0, rows, :], tw[al, 1, rows, :] = cmul(c, s, tbv[0, rows, :], tbv[1, rows, :])

    loop(9, make_twiddle)

    pl.semaphore_wait(barrier, 255)
    slot = core * 128 + chip

    def send_signal(i):
        t = lax.rem(chip + i, 128)
        remote(xs.at[t], xb.at[slot], 0, t, core).start()

    pltpu.make_async_copy(xs.at[chip], xb.at[slot], rsem.at[0]).start()
    loop(128, send_signal, 1)

    fslot = jnp.where(upper == 1, (7 - group) * 32 + 63 - place, group * 32 + place)

    def send_filter(i):
        t = lax.rem(chip + i, 128)
        for k in range(2):
            remote(fs.at[k * 128 + t], hb.at[fslot], 1, t, k).start()

    pltpu.make_async_copy(fs.at[core * 128 + chip], hb.at[fslot], rsem.at[1]).start()
    remote(fs.at[other * 128 + chip], hb.at[fslot], 1, chip, other).start()
    loop(128, send_filter, 1)

    mine = xb.at[pl.ds(core * 128, 128)]
    theirs = xb.at[pl.ds(other * 128, 128)]
    pltpu.make_async_copy(mine, mine, rsem.at[0]).wait()
    forward = remote(mine, mine, 3, chip, other)
    forward.start()
    for load in loads[4:]:
        load.wait()
    pltpu.make_async_copy(theirs, theirs, rsem.at[3]).wait()

    def widen(src, dst):
        def body(i):
            dst[pl.ds(pl.multiple_of(i * 256, 256), 256), :] = (
                src[pl.ds(i * 16, 16)].astype(F32).reshape(256, 128)
            )

        loop(16, body)

    widen(xb, x32)

    top = (lax.broadcasted_iota(jnp.int32, (8, 256), 0) == 0).astype(F32)

    def first(al):
        x = jnp.concatenate(
            [x32[pl.ds(2 * al, 256, stride=16), :], x32[pl.ds(2 * al + 1, 256, stride=16), :]], 1
        ).astype(BF16)
        f = dot(m256v[0], x) + dot(m256v[1], x)
        fz[al, 0, 0:128, :] = f[0:128]
        fz[al, 1, 0:128, :] = f[128:256]
        lone = f[224:232] * (top * even)
        fz[al, 1, 96:104, :] = f[224:232] - lone
        fz[al, 0, 128:136, :] = lone
        fz[al, 0, 136:144, :] = jnp.zeros((8, 256), F32)
        fz[al, 1, 128:144, :] = jnp.zeros((16, 256), F32)

    loop(8, first)

    def second(r):
        rows = pl.ds(pl.multiple_of(r * 16, 16), 16)
        for half in range(2):
            ln = slice(half * 128, half * 128 + 128)
            lm = slice(256 + half * 128, 384 + half * 128)
            pairs = [
                cmul(fz[al, 0, rows, ln], fz[al, 1, rows, ln], tw[al, 0, rows, ln], tw[al, 1, rows, ln])
                for al in range(8)
            ]
            re, im = dft8([p[0] for p in pairs], [p[1] for p in pairs], -1)
            for e in range(8):
                a, b = re[e], im[e]
                if e:
                    a, b = cmul(a, b, t2v[0, e : e + 1, ln], t2v[1, e : e + 1, ln])
                zh[e, rows, ln], zl[e, rows, ln] = split(a)
                zh[e, rows, lm], zl[e, rows, lm] = split(b)

    loop(9, second)

    def third(mul):
        def body(j):
            a = zh[pl.ds(j * 2, 2)].reshape(2 * ROWS, 512)
            b = zl[pl.ds(j * 2, 2)].reshape(2 * ROWS, 512)
            g = mul(a, m512v[0]) + mul(a, m512v[1]) + mul(b, m512v[0])
            gg[pl.ds(j * 2, 2)] = g.reshape(2, ROWS, 512)

        loop(4, body)

    third(dot)

    pltpu.make_async_copy(hb, hb, rsem.at[1]).wait()
    widen(hb, h32)

    def place_filter(e, shift):
        for ri in range(2):
            hf[e, ri, 128:144, :] = jnp.zeros((16, 256), F32)
            if shift:
                hf[e, ri, 96:104, :] = jnp.zeros((8, 256), F32)
            for blk in range(4):
                lo = blk * 32 + (1 if shift and blk == 3 else 0)
                for qh in range(2):
                    start = e * 512 + (ri * 8 + blk * 2 + qh)
                    hf[e, ri, lo : lo + 32, qh * 128 : qh * 128 + 128] = h32[
                        pl.ds(start, 32, stride=16), :
                    ]

    loop(4, lambda e: place_filter(e, False))

    @pl.when(core == 1)
    def _():
        loop(8, lambda e: place_filter(e, False), 4)

    @pl.when(core == 0)
    def _():
        loop(8, lambda e: place_filter(e, True), 4)
        lane = (lax.broadcasted_iota(jnp.int32, (1, 128), 1) == 0).astype(F32)
        re, im = hf[0, 0, 96:97, 0:128], hf[0, 1, 96:97, 0:128]
        for ri in range(2):
            hf[4, ri, 96:97, 0:128] = hf[0, ri, 96:97, 128:256]
        hf[0, 0, 96:97, 0:128] = re * (1.0 - 0.5 * lane)
        hf[0, 1, 96:97, 0:128] = im * (1.0 - lane)
        hf[0, 0, 96:97, 128:256] = im * (0.5 * lane)
        hf[0, 1, 96:97, 128:256] = jnp.zeros((1, 128), F32)

    def apply_filter(e):
        def body(r):
            rows = pl.ds(pl.multiple_of(r * 16, 16), 16)
            a, b = cmul(
                gg[e, rows, 0:256], gg[e, rows, 256:512], hf[e, 0, rows, :], hf[e, 1, rows, :]
            )
            zh[e, rows, 0:256], zl[e, rows, 0:256] = split(a)
            zh[e, rows, 256:512], zl[e, rows, 256:512] = split(b)

        loop(9, body)

    loop(8, apply_filter)
    third(dot_t)

    def back(r, last):
        rows = pl.ds(r * 16, 16) if last else pl.ds(pl.multiple_of(r * 16, 16), 16)
        for half in range(2):
            ln = slice(half * 128, half * 128 + 128)
            lm = slice(256 + half * 128, 384 + half * 128)
            re, im = [], []
            for e in range(8):
                a, b = gg[e, rows, ln], gg[e, rows, lm]
                if e:
                    a, b = cmul(a, b, t2v[0, e : e + 1, ln], -t2v[1, e : e + 1, ln])
                re.append(a)
                im.append(b)
            re, im = dft8(re, im, 1)
            for al in range(8):
                a, b = cmul(re[al], im[al], tw[al, 0, rows, ln], -tw[al, 1, rows, ln])
                if last:
                    ce[al, :, ln] = a[0:8]
                else:
                    mark = top[:, 0:128] * (even * (r == 6).astype(F32))
                    head = b[0:8] * (1.0 - mark) + ce[al, 0:1, ln] * mark
                    b = jnp.concatenate([head, b[8:16]], 0)
                    down = pl.ds(pl.multiple_of(128 + r * 16, 16), 16)
                    ch[al, rows, ln], cl[al, rows, ln] = split(a)
                    ch[al, down, ln], cl[al, down, ln] = split(b)

    back(8, True)
    loop(8, lambda r: back(r, False))

    def swap(al):
        return pltpu.make_async_remote_copy(
            src_ref=yo.at[al], dst_ref=pb.at[al], send_sem=swap_s.at[al], recv_sem=swap_r.at[al],
            device_id=device(chip, other), device_id_type=pl.DeviceIdType.MESH,
        )

    def combine(al):
        vh, vl = m256v[2], m256v[3]
        y = dot(vh, ch[al]) + dot(vh, cl[al]) + dot(vl, ch[al])
        yo[al] = y[0:128]
        swap(al).start()
        yw[al] = y[128:256]

    loop(8, combine)

    weight = skip[chip]

    def add_up(al, peak):
        swap(al).wait()
        for half in range(2):
            ln = slice(half * 128, half * 128 + 128)
            x = x32[pl.ds(core * 2048 + 2 * al + half, 128, stride=16), :]
            value = yw[al, :, ln] + pb[al, :, ln] + weight * x
            v32[pl.ds(2 * al + half, 128, stride=16), :] = value
            peak = jnp.maximum(peak, jnp.max(jnp.abs(value).reshape(16, 8, 128), axis=0))
        return peak

    peak = lax.fori_loop(0, 8, add_up, jnp.zeros((8, 128), F32))
    peak = jnp.max(jnp.max(peak, axis=1, keepdims=True), axis=0, keepdims=True)
    peak = jnp.maximum(jnp.broadcast_to(peak, (1, 128)), 2.0**-118)
    se[0] = peak * (1.0 / SPAN)
    shrink = SPAN / peak

    def encode(i):
        rows = pl.ds(pl.multiple_of(i * 128, 128), 128)
        value = v32[rows, :] * shrink
        power = value * value
        power = power * power
        power = power * power
        power = power * power
        code = jnp.where(value < 0, -power, power)
        ye[pl.ds(i * 8, 8)] = code.astype(BF16).reshape(8, 16, 128)

    loop(16, encode)

    def send_out(i):
        t = lax.rem(chip + i, 128)
        remote(ye.at[t], yb.at[chip], 5, t, core).start()

    def send_scale(i):
        t = lax.rem(chip + i, 128)
        remote(se.at[0], sb.at[chip], 6, t, core).start()

    pltpu.make_async_copy(ye.at[chip], yb.at[chip], rsem.at[5]).start()
    pltpu.make_async_copy(se.at[0], sb.at[chip], rsem.at[6]).start()
    loop(128, send_out, 1)
    loop(128, send_scale, 1)
    pltpu.make_async_copy(sb, sb, rsem.at[6]).wait()
    pltpu.make_async_copy(yb, yb, rsem.at[5]).wait()

    def decode(i):
        for j in range(8):
            code = yb[i * 8 + j].astype(F32)
            size = jnp.maximum(jnp.abs(code), 2.0**-126)
            size = lax.rsqrt(lax.rsqrt(lax.rsqrt(lax.rsqrt(size)))) * sb[i * 8 + j]
            rows = pl.ds(pl.multiple_of(i * 128 + j * 16, 16), 16)
            s32[rows, :] = jnp.where(code < 0, -size, size)

    def finish(a):
        rows = pl.ds(pl.multiple_of(a * 128, 128), 128)
        value = s32[pl.ds(a, 128, stride=16), :].T
        out[rows, :] = (gv[rows, :].astype(F32) * value).astype(BF16)

    loop(16, decode)
    loop(16, finish)

    def sent(ref, sem):
        pltpu.make_async_copy(ref, ref, ssem.at[sem]).wait()

    sent(xs.at[pl.ds(0, 127)], 0)
    sent(fs.at[pl.ds(0, 255)], 1)

    forward.wait_send()
    sent(ye.at[pl.ds(0, 127)], 5)
    sent(sb.at[pl.ds(0, 127)], 6)


def body(signal, gate, filters, skip):
    m256, m512, tb, ta, t2 = (jnp.asarray(t) for t in tables())
    vmem = pl.BlockSpec(memory_space=pltpu.VMEM)
    hbm = pl.BlockSpec(memory_space=pl.ANY)
    smem = pl.BlockSpec(memory_space=pltpu.SMEM)
    return pl.pallas_call(
        kernel,
        out_shape=jax.ShapeDtypeStruct(signal.shape, BF16),
        in_specs=[vmem, hbm, hbm, smem, hbm, hbm, hbm, hbm, hbm],
        out_specs=vmem,
        scratch_shapes=[
            pltpu.VMEM((2, 8, 256, 128), BF16),
            pltpu.VMEM((2, 1, 128, 128), BF16),
            pltpu.VMEM((2048, 128), BF16),
            pltpu.VMEM((4, 256, 256), BF16),
            pltpu.VMEM((2, 512, 512), BF16),
            pltpu.VMEM((2, ROWS, 256), F32),
            pltpu.VMEM((ROWS, 128), F32),
            pltpu.VMEM((2, 8, 256), F32),
            pltpu.VMEM((2048, 128), F32),
            pltpu.VMEM((128, 16, 128), BF16),
            pltpu.VMEM((256, 16, 128), BF16),
            pltpu.VMEM((4096, 128), F32),
            pltpu.VMEM((256, 16, 128), BF16),
            pltpu.VMEM((256, 16, 128), BF16),
            pltpu.VMEM((8, 2, ROWS, 256), F32),
            pltpu.VMEM((8, 2, ROWS, 256), F32),
            pltpu.VMEM((8, 2, ROWS, 256), F32),
            pltpu.VMEM((8, ROWS, 512), BF16),
            pltpu.VMEM((8, ROWS, 512), BF16),
            pltpu.VMEM((8, ROWS, 512), F32),
            pltpu.VMEM((8, 8, 256), F32),
            pltpu.VMEM((8, 256, 256), BF16),
            pltpu.VMEM((8, 256, 256), BF16),
            pltpu.VMEM((8, 128, 256), F32),
            pltpu.VMEM((8, 128, 256), F32),
            pltpu.VMEM((8, 128, 256), F32),
            pltpu.VMEM((2048, 128), F32),
            pltpu.VMEM((4096, 128), F32),
            pltpu.VMEM((128, 16, 128), BF16),
            pltpu.VMEM((128, 16, 128), BF16),
            pltpu.VMEM((1, 1, 128), F32),
            pltpu.VMEM((128, 1, 128), F32),
            pltpu.SemaphoreType.DMA((8,)),
            pltpu.SemaphoreType.DMA((7,)),
            pltpu.SemaphoreType.DMA((7,)),
            pltpu.SemaphoreType.DMA((8,)),
            pltpu.SemaphoreType.DMA((8,)),
        ],
        compiler_params=pltpu.CompilerParams(
            collective_id=0, has_side_effects=True, vmem_limit_bytes=56 << 20
        ),
    )(signal, filters, gate, skip, m256, m512, tb, ta, t2)


def solution(mesh):
    placed = (
        P(("ctx", "cp"), None),
        P(("ctx", "cp"), None),
        P(None, ("ctx", "cp"), None, None),
        P(),
    )
    return jax.shard_map(
        body, mesh=mesh, in_specs=placed, out_specs=P(("ctx", "cp"), None), check_vma=False
    )
```

```python
import functools
import math

import jax
import jax.numpy as jnp
import ml_dtypes
import numpy as np
from jax import lax
from jax.experimental import pallas as pl
from jax.experimental.pallas import tpu as pltpu
from jax.sharding import PartitionSpec as P


FULL = 1 << 20
SPAN = 2.0**7.75
ROWS = 144
F32 = jnp.float32
BF16 = jnp.bfloat16

LOW = ((2, 4, 6, 0), (3, 5, 7, 1))
UPP = ((6, 4, 2, 0), (5, 3, 1, 7))


def phase(product, length):
    angle = 2 * math.pi * (np.asarray(product, dtype=np.int64) % length) / length
    return np.cos(angle), np.sin(angle)


def split_np(array):
    high = array.astype(ml_dtypes.bfloat16)
    low = (array - high.astype(np.float64)).astype(ml_dtypes.bfloat16)
    return high, low


def row_sigma(core):
    index = np.concatenate([4 * np.arange(32) + t for t in (1, 2, 3, 0)] + [np.array([128])])
    sigma = 2 * index + core
    if core == 1:
        sigma[128] = 0
    return sigma


@functools.lru_cache(maxsize=None)
def tables():
    pos = np.arange(256)
    core_of, chip_of = pos // 128, pos % 128
    block = ((chip_of // 8) * 2 + core_of) * 8 + chip_of % 8
    m256 = []
    tb = np.zeros((2, 2, ROWS, 256), np.float32)
    ta = np.zeros((2, ROWS, 128), np.float32)
    beta, al = np.arange(256), np.arange(8)
    for core in (0, 1):
        sigma = row_sigma(core)
        cos, sin = phase(sigma[:128, None] * block[None, :], 512)
        fwd = np.concatenate([cos, -sin], 0)
        inv = np.concatenate([cos.T, -sin.T], 1)
        if core == 0:
            nyquist = phase(256 * block, 512)[0]
            fwd[128 + 96] = nyquist
            inv[:, 128 + 96] = nyquist
        inv = np.roll(inv, 128 * core - 128, axis=0) * (2.0 / FULL)
        m256.append(np.stack([*split_np(fwd), *split_np(inv)]))
        cos, sin = phase(sigma[:, None] * beta[None, :], FULL)
        tb[core, 0, :129], tb[core, 1, :129] = cos, -sin
        cos, sin = phase(sigma[:, None] * al[None, :], 4096)
        ta[core, :129, 0:8], ta[core, :129, 8:16] = cos, -sin
    cos, sin = phase(beta[:, None] * beta[None, :], 256)
    m512 = np.stack(split_np(np.block([[cos, -sin], [sin, cos]])))
    cos, sin = phase(al[:, None] * beta[None, :], 2048)
    t2 = np.stack([cos, -sin]).astype(np.float32)
    return np.stack(m256), m512, tb, ta, t2


def cmul(a, b, c, d):
    return a * c - b * d, a * d + b * c


def dft8(re, im, sign):
    root = math.sqrt(0.5)

    def turn(x, y, power):
        if power == 0:
            return x, y
        if power == 2:
            return (-y, x) if sign > 0 else (y, -x)
        if power == 1:
            if sign > 0:
                return (x - y) * root, (x + y) * root
            return (x + y) * root, (y - x) * root
        if sign > 0:
            return (-x - y) * root, (x - y) * root
        return (y - x) * root, (-x - y) * root

    def step(res, ims):
        n = len(res)
        if n == 1:
            return res, ims
        h = n // 2
        er = [res[j] + res[j + h] for j in range(h)]
        ei = [ims[j] + ims[j + h] for j in range(h)]
        odd = [turn(res[j] - res[j + h], ims[j] - ims[j + h], j * (8 // n)) for j in range(h)]
        er, ei = step(er, ei)
        dr, di = step([o[0] for o in odd], [o[1] for o in odd])
        outr, outi = [], []
        for j in range(h):
            outr += [er[j], dr[j]]
            outi += [ei[j], di[j]]
        return outr, outi

    return step(re, im)


def split(x):
    high = x.astype(BF16)
    return high, (x - high.astype(F32)).astype(BF16)


def dot(a, b):
    return jnp.dot(a, b, preferred_element_type=F32)


def slot_of(e):
    return 2 * e if e < 4 else 2 * (7 - e) + 1


def dot_t(a, b):
    return lax.dot_general(a, b, (((1,), (1,)), ((), ())), preferred_element_type=F32)


def kernel(
    sig, filt, gate, skip, m256, m512, tb, ta, t2, out,
    fv, ev, gv, m256v, m512v, tbv, tav, t2v,
    s32, xs, xb, x32, fs, hb, hf, fz, tw, zh, zl, gg, keep, ce, ch, cl,
    yo, yw, pb, v32, h32, ye, yb, se, sb, lsem, ssem, rsem, swap_s, swap_r, wave_r,
):
    ctx, cp = lax.axis_index("ctx"), lax.axis_index("cp")
    core = lax.rem(ctx, 2)
    other = 1 - core
    chip = (ctx // 2) * 8 + cp
    here = ctx * 8 + cp
    even = (1 - core).astype(F32)

    def device(t, k):
        return ((t // 8) * 2 + k, lax.rem(t, 8))

    def remote(src, dst, sem, t, k):
        return pltpu.make_async_remote_copy(
            src_ref=src, dst_ref=dst, send_sem=ssem.at[sem], recv_sem=rsem.at[sem],
            device_id=device(t, k), device_id_type=pl.DeviceIdType.MESH,
        )

    def loop(n, body, start=0):
        def wrapped(i, carry):
            body(i)
            return carry

        lax.fori_loop(start, n, wrapped, 0)

    barrier = pltpu.get_barrier_semaphore()

    def greet(i):
        t = lax.rem(here + i, 256)
        pl.semaphore_signal(
            barrier, inc=1, device_id=(t // 8, lax.rem(t, 8)), device_id_type=pl.DeviceIdType.MESH
        )

    loop(256, greet, 1)

    group, place = here // 64, lax.rem(here, 64)
    upper = (place >= 32).astype(jnp.int32)
    loads = [
        pltpu.make_async_copy(filt.at[:, pl.ds(upper * 8, 8)], fv, lsem.at[0]),
        pltpu.make_async_copy(filt.at[:, pl.ds(8, 1), pl.ds(0, 128)], ev, lsem.at[1]),
        pltpu.make_async_copy(ta.at[core], tav, lsem.at[2]),
        pltpu.make_async_copy(tb.at[core], tbv, lsem.at[3]),
        pltpu.make_async_copy(m256.at[core], m256v, lsem.at[4]),
        pltpu.make_async_copy(m512, m512v, lsem.at[5]),
        pltpu.make_async_copy(t2, t2v, lsem.at[6]),
        pltpu.make_async_copy(gate, gv, lsem.at[7]),
    ]
    for load in loads:
        load.start()

    def turn_signal(a):
        block = sig[pl.ds(pl.multiple_of(a * 128, 128), 128), :].astype(F32)
        s32[pl.ds(a, 128, stride=16), :] = block.T

    loop(16, turn_signal)

    def pack(dst, base):
        def body(i):
            rows = s32[pl.ds(pl.multiple_of(i * 256, 256), 256), :]
            dst[pl.ds(base + i * 16, 16)] = rows.astype(BF16).reshape(16, 16, 128)

        loop(8, body)

    pack(xs, 0)

    loads[0].wait()
    loads[1].wait()

    def turn_filter(k):
        for blk in range(4):
            row = jnp.where(upper == 1, UPP[k][blk], LOW[k][blk])

            def body(j, row=row, blk=blk):
                ri, qh = j // 2, lax.rem(j, 2)
                block = fv[ri, row, pl.ds(pl.multiple_of(qh * 128, 128), 128), :].astype(F32)
                s32[pl.ds(ri * 8 + blk * 2 + qh, 128, stride=16), :] = block.T

            loop(4, body)

    def pack_mirrors():
        for ri in range(2):
            s32[pl.ds(ri * 8 + 7, 128, stride=16), :] = ev[ri, 0].astype(F32).T
        head = lax.broadcasted_iota(jnp.int32, (128, 128), 0) == 0
        middle = fv[0, 0, 128:136, :].astype(F32)[0:1]
        block = jnp.where(head, middle, fv[1, 0, 0:128, :].astype(F32))
        s32[pl.ds(8 + 6, 128, stride=16), :] = block.T

    turn_filter(0)
    pl.when(here == 0)(pack_mirrors)
    pack(fs, 0)
    turn_filter(1)
    pack(fs, 128)

    loads[2].wait()
    loads[3].wait()

    def make_twiddle(r):
        rows = pl.ds(pl.multiple_of(r * 16, 16), 16)
        cols = tav[rows, :]
        for al in range(8):
            c = jnp.broadcast_to(cols[:, al : al + 1], (16, 256))
            s = jnp.broadcast_to(cols[:, 8 + al : 9 + al], (16, 256))
            tw[al, 0, rows, :], tw[al, 1, rows, :] = cmul(c, s, tbv[0, rows, :], tbv[1, rows, :])

    loop(9, make_twiddle)

    pl.semaphore_wait(barrier, 255)
    slot = core * 128 + chip

    def send_signal(i):
        t = lax.rem(chip + i, 128)
        remote(xs.at[t], xb.at[slot], 0, t, core).start()

    pltpu.make_async_copy(xs.at[chip], xb.at[slot], rsem.at[0]).start()
    loop(128, send_signal, 1)

    zlo, low = chip // 32, lax.rem(chip, 32)
    fslot = (2 * group + upper) * 32 + jnp.where(upper == 1, 63 - place, place)

    def send_filter(j, r):
        t = lax.rem(zlo + j, 4) * 32 + lax.rem(low + r, 32)
        for k in range(2):
            pltpu.make_async_remote_copy(
                src_ref=fs.at[k * 128 + t], dst_ref=hb.at[fslot], send_sem=ssem.at[1],
                recv_sem=wave_r.at[j], device_id=device(t, k), device_id_type=pl.DeviceIdType.MESH,
            ).start()

    loop(64, lambda i: send_filter(1 + 2 * lax.rem(i, 2), i // 2))
    loop(32, lambda i: send_filter(2, i))
    pltpu.make_async_copy(fs.at[core * 128 + chip], hb.at[fslot], wave_r.at[0]).start()
    pltpu.make_async_remote_copy(
        src_ref=fs.at[other * 128 + chip], dst_ref=hb.at[fslot], send_sem=ssem.at[1],
        recv_sem=wave_r.at[0], device_id=device(chip, other), device_id_type=pl.DeviceIdType.MESH,
    ).start()
    loop(32, lambda i: send_filter(0, i), 1)

    mine = xb.at[pl.ds(core * 128, 128)]
    theirs = xb.at[pl.ds(other * 128, 128)]
    pltpu.make_async_copy(mine, mine, rsem.at[0]).wait()
    forward = remote(mine, mine, 3, chip, other)
    forward.start()
    for load in loads[4:]:
        load.wait()
    pltpu.make_async_copy(theirs, theirs, rsem.at[3]).wait()

    def widen(src, dst):
        def body(i):
            dst[pl.ds(pl.multiple_of(i * 256, 256), 256), :] = (
                src[pl.ds(i * 16, 16)].astype(F32).reshape(256, 128)
            )

        loop(16, body)

    widen(xb, x32)

    top = (lax.broadcasted_iota(jnp.int32, (8, 256), 0) == 0).astype(F32)

    def first(al):
        x = jnp.concatenate(
            [x32[pl.ds(2 * al, 256, stride=16), :], x32[pl.ds(2 * al + 1, 256, stride=16), :]], 1
        ).astype(BF16)
        f = dot(m256v[0], x) + dot(m256v[1], x)
        fz[al, 0, 0:128, :] = f[0:128]
        fz[al, 1, 0:128, :] = f[128:256]
        lone = f[224:232] * (top * even)
        fz[al, 1, 96:104, :] = f[224:232] - lone
        fz[al, 0, 128:136, :] = lone
        fz[al, 0, 136:144, :] = jnp.zeros((8, 256), F32)
        fz[al, 1, 128:144, :] = jnp.zeros((16, 256), F32)

    loop(8, first)

    def second(r):
        rows = pl.ds(pl.multiple_of(r * 16, 16), 16)
        for half in range(2):
            ln = slice(half * 128, half * 128 + 128)
            lm = slice(256 + half * 128, 384 + half * 128)
            pairs = [
                cmul(fz[al, 0, rows, ln], fz[al, 1, rows, ln], tw[al, 0, rows, ln], tw[al, 1, rows, ln])
                for al in range(8)
            ]
            re, im = dft8([p[0] for p in pairs], [p[1] for p in pairs], -1)
            for e in range(8):
                a, b, m = re[e], im[e], slot_of(e)
                if e:
                    a, b = cmul(a, b, t2v[0, e : e + 1, ln], t2v[1, e : e + 1, ln])
                zh[m, rows, ln], zl[m, rows, ln] = split(a)
                zh[m, rows, lm], zl[m, rows, lm] = split(b)

    loop(9, second)

    def third(mul, j):
        a = zh[pl.ds(j * 2, 2)].reshape(2 * ROWS, 512)
        b = zl[pl.ds(j * 2, 2)].reshape(2 * ROWS, 512)
        g = mul(a, m512v[0]) + mul(a, m512v[1]) + mul(b, m512v[0])
        gg[pl.ds(j * 2, 2)] = g.reshape(2, ROWS, 512)

    loop(4, lambda j: third(dot, j))
    keep[...] = gg[7, 96:104, :]

    def place_filter(m, shift):
        for ri in range(2):
            hf[m, ri, 128:144, :] = jnp.zeros((16, 256), F32)
            if shift:
                hf[m, ri, 96:104, :] = jnp.zeros((8, 256), F32)
            for blk in range(4):
                lo = blk * 32 + (1 if shift and blk == 3 else 0)
                for qh in range(2):
                    start = m * 512 + (ri * 8 + blk * 2 + qh)
                    hf[m, ri, lo : lo + 32, qh * 128 : qh * 128 + 128] = h32[
                        pl.ds(start, 32, stride=16), :
                    ]

    def apply_filter(m):
        def body(r):
            rows = pl.ds(pl.multiple_of(r * 16, 16), 16)
            a, b = cmul(
                gg[m, rows, 0:256], gg[m, rows, 256:512], hf[m, 0, rows, :], hf[m, 1, rows, :]
            )
            zh[m, rows, 0:256], zl[m, rows, 0:256] = split(a)
            zh[m, rows, 256:512], zl[m, rows, 256:512] = split(b)

        loop(9, body)

    def mirrors():
        lane = (lax.broadcasted_iota(jnp.int32, (1, 128), 1) == 0).astype(F32)
        re, im = hf[0, 0, 96:97, 0:128], hf[0, 1, 96:97, 0:128]
        hr = hf[0, 0, 96:104, 128:256] * top[:, 0:128]
        hi = hf[0, 1, 96:104, 128:256] * top[:, 0:128]
        hf[0, 0, 96:97, 0:128] = re * (1.0 - 0.5 * lane)
        hf[0, 1, 96:97, 0:128] = im * (1.0 - lane)
        hf[0, 0, 96:97, 128:256] = im * (0.5 * lane)
        hf[0, 1, 96:97, 128:256] = jnp.zeros((1, 128), F32)
        a, b = cmul(keep[:, 0:128], keep[:, 256:384], hr, hi)
        none = jnp.zeros((8, 128), F32)
        row = jnp.concatenate([a, none, b, none], 1)
        high, rest = split(jnp.concatenate([row, jnp.zeros((8, 512), F32)], 0))
        g = dot_t(high, m512v[0]) + dot_t(high, m512v[1]) + dot_t(rest, m512v[0])
        keep[...] = g[0:8]

    def wave(w):
        j = lax.rem(w * 2 + 1, 4) + jnp.where(w == 2, 1, 0) - jnp.where(w == 3, 3, 0)
        z = lax.rem(zlo + 4 - j, 4)
        part = hb.at[pl.ds(z * 64, 64)]
        pltpu.make_async_copy(part, part, wave_r.at[j]).wait()

        def widen_part(i):
            h32[pl.ds(pl.multiple_of(z * 1024 + i * 256, 256), 256), :] = (
                hb[pl.ds(z * 64 + i * 16, 16)].astype(F32).reshape(256, 128)
            )

        loop(4, widen_part)
        place_filter(2 * z, False)
        pl.when(core == 1)(lambda: place_filter(2 * z + 1, False))
        pl.when(core == 0)(lambda: place_filter(2 * z + 1, True))
        pl.when((core == 0) & (z == 0))(mirrors)
        apply_filter(2 * z)
        apply_filter(2 * z + 1)
        third(dot_t, z)

    loop(4, wave)

    @pl.when(core == 0)
    def _():
        gg[7, 96:104, :] = gg[7, 96:104, :] + keep[...]

    def back(r, last):
        rows = pl.ds(r * 16, 16) if last else pl.ds(pl.multiple_of(r * 16, 16), 16)
        for half in range(2):
            ln = slice(half * 128, half * 128 + 128)
            lm = slice(256 + half * 128, 384 + half * 128)
            re, im = [], []
            for e in range(8):
                a, b = gg[slot_of(e), rows, ln], gg[slot_of(e), rows, lm]
                if e:
                    a, b = cmul(a, b, t2v[0, e : e + 1, ln], -t2v[1, e : e + 1, ln])
                re.append(a)
                im.append(b)
            re, im = dft8(re, im, 1)
            for al in range(8):
                a, b = cmul(re[al], im[al], tw[al, 0, rows, ln], -tw[al, 1, rows, ln])
                if last:
                    ce[al, :, ln] = a[0:8]
                else:
                    mark = top[:, 0:128] * (even * (r == 6).astype(F32))
                    head = b[0:8] * (1.0 - mark) + ce[al, 0:1, ln] * mark
                    b = jnp.concatenate([head, b[8:16]], 0)
                    down = pl.ds(pl.multiple_of(128 + r * 16, 16), 16)
                    ch[al, rows, ln], cl[al, rows, ln] = split(a)
                    ch[al, down, ln], cl[al, down, ln] = split(b)

    back(8, True)
    loop(8, lambda r: back(r, False))

    def swap(al):
        return pltpu.make_async_remote_copy(
            src_ref=yo.at[al], dst_ref=pb.at[al], send_sem=swap_s.at[al], recv_sem=swap_r.at[al],
            device_id=device(chip, other), device_id_type=pl.DeviceIdType.MESH,
        )

    def combine(al):
        vh, vl = m256v[2], m256v[3]
        y = dot(vh, ch[al]) + dot(vh, cl[al]) + dot(vl, ch[al])
        yo[al] = y[0:128]
        swap(al).start()
        yw[al] = y[128:256]

    loop(8, combine)

    weight = skip[chip]

    def add_up(al, peak):
        swap(al).wait()
        for half in range(2):
            ln = slice(half * 128, half * 128 + 128)
            x = x32[pl.ds(core * 2048 + 2 * al + half, 128, stride=16), :]
            value = yw[al, :, ln] + pb[al, :, ln] + weight * x
            v32[pl.ds(2 * al + half, 128, stride=16), :] = value
            peak = jnp.maximum(peak, jnp.max(jnp.abs(value).reshape(16, 8, 128), axis=0))
        return peak

    peak = lax.fori_loop(0, 8, add_up, jnp.zeros((8, 128), F32))
    peak = jnp.max(jnp.max(peak, axis=1, keepdims=True), axis=0, keepdims=True)
    peak = jnp.maximum(jnp.broadcast_to(peak, (1, 128)), 2.0**-118)
    se[0] = peak * (1.0 / SPAN)
    shrink = SPAN / peak

    def encode(i):
        rows = pl.ds(pl.multiple_of(i * 128, 128), 128)
        value = v32[rows, :] * shrink
        power = value * value
        power = power * power
        power = power * power
        power = power * power
        code = jnp.where(value < 0, -power, power)
        ye[pl.ds(i * 8, 8)] = code.astype(BF16).reshape(8, 16, 128)

    loop(16, encode)

    def send_out(i):
        t = lax.rem(chip + i, 128)
        remote(ye.at[t], yb.at[chip], 5, t, core).start()

    def send_scale(i):
        t = lax.rem(chip + i, 128)
        remote(se.at[0], sb.at[chip], 6, t, core).start()

    pltpu.make_async_copy(ye.at[chip], yb.at[chip], rsem.at[5]).start()
    pltpu.make_async_copy(se.at[0], sb.at[chip], rsem.at[6]).start()
    loop(128, send_out, 1)
    loop(128, send_scale, 1)
    pltpu.make_async_copy(sb, sb, rsem.at[6]).wait()
    pltpu.make_async_copy(yb, yb, rsem.at[5]).wait()

    def decode(i):
        for j in range(8):
            code = yb[i * 8 + j].astype(F32)
            size = jnp.maximum(jnp.abs(code), 2.0**-126)
            size = lax.rsqrt(lax.rsqrt(lax.rsqrt(lax.rsqrt(size)))) * sb[i * 8 + j]
            rows = pl.ds(pl.multiple_of(i * 128 + j * 16, 16), 16)
            s32[rows, :] = jnp.where(code < 0, -size, size)

    def finish(a):
        rows = pl.ds(pl.multiple_of(a * 128, 128), 128)
        value = s32[pl.ds(a, 128, stride=16), :].T
        out[rows, :] = (gv[rows, :].astype(F32) * value).astype(BF16)

    loop(16, decode)
    loop(16, finish)

    def sent(ref, sem):
        pltpu.make_async_copy(ref, ref, ssem.at[sem]).wait()

    sent(xs.at[pl.ds(0, 127)], 0)
    sent(fs.at[pl.ds(0, 255)], 1)

    forward.wait_send()
    sent(ye.at[pl.ds(0, 127)], 5)
    sent(sb.at[pl.ds(0, 127)], 6)


def body(signal, gate, filters, skip):
    m256, m512, tb, ta, t2 = (jnp.asarray(t) for t in tables())
    vmem = pl.BlockSpec(memory_space=pltpu.VMEM)
    hbm = pl.BlockSpec(memory_space=pl.ANY)
    smem = pl.BlockSpec(memory_space=pltpu.SMEM)
    return pl.pallas_call(
        kernel,
        out_shape=jax.ShapeDtypeStruct(signal.shape, BF16),
        in_specs=[vmem, hbm, hbm, smem, hbm, hbm, hbm, hbm, hbm],
        out_specs=vmem,
        scratch_shapes=[
            pltpu.VMEM((2, 8, 256, 128), BF16),
            pltpu.VMEM((2, 1, 128, 128), BF16),
            pltpu.VMEM((2048, 128), BF16),
            pltpu.VMEM((4, 256, 256), BF16),
            pltpu.VMEM((2, 512, 512), BF16),
            pltpu.VMEM((2, ROWS, 256), F32),
            pltpu.VMEM((ROWS, 128), F32),
            pltpu.VMEM((2, 8, 256), F32),
            pltpu.VMEM((2048, 128), F32),
            pltpu.VMEM((128, 16, 128), BF16),
            pltpu.VMEM((256, 16, 128), BF16),
            pltpu.VMEM((4096, 128), F32),
            pltpu.VMEM((256, 16, 128), BF16),
            pltpu.VMEM((256, 16, 128), BF16),
            pltpu.VMEM((8, 2, ROWS, 256), F32),
            pltpu.VMEM((8, 2, ROWS, 256), F32),
            pltpu.VMEM((8, 2, ROWS, 256), F32),
            pltpu.VMEM((8, ROWS, 512), BF16),
            pltpu.VMEM((8, ROWS, 512), BF16),
            pltpu.VMEM((8, ROWS, 512), F32),
            pltpu.VMEM((8, 512), F32),
            pltpu.VMEM((8, 8, 256), F32),
            pltpu.VMEM((8, 256, 256), BF16),
            pltpu.VMEM((8, 256, 256), BF16),
            pltpu.VMEM((8, 128, 256), F32),
            pltpu.VMEM((8, 128, 256), F32),
            pltpu.VMEM((8, 128, 256), F32),
            pltpu.VMEM((2048, 128), F32),
            pltpu.VMEM((4096, 128), F32),
            pltpu.VMEM((128, 16, 128), BF16),
            pltpu.VMEM((128, 16, 128), BF16),
            pltpu.VMEM((1, 1, 128), F32),
            pltpu.VMEM((128, 1, 128), F32),
            pltpu.SemaphoreType.DMA((8,)),
            pltpu.SemaphoreType.DMA((7,)),
            pltpu.SemaphoreType.DMA((7,)),
            pltpu.SemaphoreType.DMA((8,)),
            pltpu.SemaphoreType.DMA((8,)),
            pltpu.SemaphoreType.DMA((4,)),
        ],
        compiler_params=pltpu.CompilerParams(
            collective_id=0, has_side_effects=True, vmem_limit_bytes=56 << 20
        ),
    )(signal, filters, gate, skip, m256, m512, tb, ta, t2)


def solution(mesh):
    placed = (
        P(("ctx", "cp"), None),
        P(("ctx", "cp"), None),
        P(None, ("ctx", "cp"), None, None),
        P(),
    )
    return jax.shard_map(
        body, mesh=mesh, in_specs=placed, out_specs=P(("ctx", "cp"), None), check_vma=False
    )
```

```python
import functools
import math

import jax
import jax.numpy as jnp
import ml_dtypes
import numpy as np
from jax import lax
from jax.experimental import pallas as pl
from jax.experimental.pallas import tpu as pltpu
from jax.sharding import PartitionSpec as P


FULL = 1 << 20
SPAN = 2.0**7.75
ROWS = 144
F32 = jnp.float32
BF16 = jnp.bfloat16

LOW = ((2, 4, 6, 0), (3, 5, 7, 1))
UPP = ((6, 4, 2, 0), (5, 3, 1, 7))


def phase(product, length):
    angle = 2 * math.pi * (np.asarray(product, dtype=np.int64) % length) / length
    return np.cos(angle), np.sin(angle)


def split_np(array):
    high = array.astype(ml_dtypes.bfloat16)
    low = (array - high.astype(np.float64)).astype(ml_dtypes.bfloat16)
    return high, low


def row_sigma(core):
    index = np.concatenate([4 * np.arange(32) + t for t in (1, 2, 3, 0)] + [np.array([128])])
    sigma = 2 * index + core
    if core == 1:
        sigma[128] = 0
    return sigma


@functools.lru_cache(maxsize=None)
def tables():
    pos = np.arange(256)
    core_of, chip_of = pos // 128, pos % 128
    block = ((chip_of // 8) * 2 + core_of) * 8 + chip_of % 8
    m256 = []
    tb = np.zeros((2, 2, ROWS, 256), np.float32)
    ta = np.zeros((2, ROWS, 128), np.float32)
    beta, al = np.arange(256), np.arange(8)
    for core in (0, 1):
        sigma = row_sigma(core)
        cos, sin = phase(sigma[:128, None] * block[None, :], 512)
        fwd = np.concatenate([cos, -sin], 0)
        inv = np.concatenate([cos.T, -sin.T], 1)
        if core == 0:
            nyquist = phase(256 * block, 512)[0]
            fwd[128 + 96] = nyquist
            inv[:, 128 + 96] = nyquist
        inv = np.roll(inv, 128 * core - 128, axis=0) * (2.0 / FULL)
        m256.append(np.stack([*split_np(fwd), *split_np(inv)]))
        cos, sin = phase(sigma[:, None] * beta[None, :], FULL)
        tb[core, 0, :129], tb[core, 1, :129] = cos, -sin
        cos, sin = phase(sigma[:, None] * al[None, :], 4096)
        ta[core, :129, 0:8], ta[core, :129, 8:16] = cos, -sin
    cos, sin = phase(beta[:, None] * beta[None, :], 256)
    m512 = np.stack(split_np(np.block([[cos, -sin], [sin, cos]])))
    cos, sin = phase(al[:, None] * beta[None, :], 2048)
    t2 = np.stack([cos, -sin]).astype(np.float32)
    return np.stack(m256), m512, tb, ta, t2


def cmul(a, b, c, d):
    return a * c - b * d, a * d + b * c


def dft8(re, im, sign):
    root = math.sqrt(0.5)

    def turn(x, y, power):
        if power == 0:
            return x, y
        if power == 2:
            return (-y, x) if sign > 0 else (y, -x)
        if power == 1:
            if sign > 0:
                return (x - y) * root, (x + y) * root
            return (x + y) * root, (y - x) * root
        if sign > 0:
            return (-x - y) * root, (x - y) * root
        return (y - x) * root, (-x - y) * root

    def step(res, ims):
        n = len(res)
        if n == 1:
            return res, ims
        h = n // 2
        er = [res[j] + res[j + h] for j in range(h)]
        ei = [ims[j] + ims[j + h] for j in range(h)]
        odd = [turn(res[j] - res[j + h], ims[j] - ims[j + h], j * (8 // n)) for j in range(h)]
        er, ei = step(er, ei)
        dr, di = step([o[0] for o in odd], [o[1] for o in odd])
        outr, outi = [], []
        for j in range(h):
            outr += [er[j], dr[j]]
            outi += [ei[j], di[j]]
        return outr, outi

    return step(re, im)


def split(x):
    high = x.astype(BF16)
    return high, (x - high.astype(F32)).astype(BF16)


def dot(a, b):
    return jnp.dot(a, b, preferred_element_type=F32)


def slot_of(e):
    return 2 * e if e < 4 else 2 * (7 - e) + 1


def dot_t(a, b):
    return lax.dot_general(a, b, (((1,), (1,)), ((), ())), preferred_element_type=F32)


def kernel(
    sig, filt, gate, skip, m256, m512, tb, ta, t2, out,
    sv, fv, ev, gv, ob, m256v, m512v, tbv, tav, t2v,
    s32, xs, xb, x32, fs, hb, hf, fz, tw, zh, zl, gg, keep, ce, ch, cl,
    yo, yw, pb, v32, h32, ye, yb, se, sb, lsem, ssem, rsem, swap_s, swap_r, wave_r, out_r,
):
    ctx, cp = lax.axis_index("ctx"), lax.axis_index("cp")
    core = lax.rem(ctx, 2)
    other = 1 - core
    chip = (ctx // 2) * 8 + cp
    here = ctx * 8 + cp
    even = (1 - core).astype(F32)

    def device(t, k):
        return ((t // 8) * 2 + k, lax.rem(t, 8))

    def remote(src, dst, sem, t, k):
        return pltpu.make_async_remote_copy(
            src_ref=src, dst_ref=dst, send_sem=ssem.at[sem], recv_sem=rsem.at[sem],
            device_id=device(t, k), device_id_type=pl.DeviceIdType.MESH,
        )

    def loop(n, body, start=0):
        def wrapped(i, carry):
            body(i)
            return carry

        lax.fori_loop(start, n, wrapped, 0)

    barrier = pltpu.get_barrier_semaphore()

    def greet(i):
        t = lax.rem(here + i, 256)
        pl.semaphore_signal(
            barrier, inc=1, device_id=(t // 8, lax.rem(t, 8)), device_id_type=pl.DeviceIdType.MESH
        )

    load_signal = pltpu.make_async_copy(sig, sv, lsem.at[8])
    load_signal.start()
    loop(256, greet, 1)

    group, place = here // 64, lax.rem(here, 64)
    upper = (place >= 32).astype(jnp.int32)
    loads = [
        pltpu.make_async_copy(filt.at[:, pl.ds(upper * 8, 8)], fv, lsem.at[0]),
        pltpu.make_async_copy(filt.at[:, pl.ds(8, 1), pl.ds(0, 128)], ev, lsem.at[1]),
        pltpu.make_async_copy(ta.at[core], tav, lsem.at[2]),
        pltpu.make_async_copy(tb.at[core], tbv, lsem.at[3]),
        pltpu.make_async_copy(m256.at[core], m256v, lsem.at[4]),
        pltpu.make_async_copy(m512, m512v, lsem.at[5]),
        pltpu.make_async_copy(t2, t2v, lsem.at[6]),
        pltpu.make_async_copy(gate, gv, lsem.at[7]),
    ]
    for load in loads:
        load.start()

    def turn_signal(a):
        block = sv[pl.ds(pl.multiple_of(a * 128, 128), 128), :].astype(F32)
        s32[pl.ds(a, 128, stride=16), :] = block.T

    load_signal.wait()
    loop(16, turn_signal)

    def pack(dst, base):
        def body(i):
            rows = s32[pl.ds(pl.multiple_of(i * 256, 256), 256), :]
            dst[pl.ds(base + i * 16, 16)] = rows.astype(BF16).reshape(16, 16, 128)

        loop(8, body)

    pack(xs, 0)

    loads[0].wait()
    loads[1].wait()

    def turn_filter(k):
        for blk in range(4):
            row = jnp.where(upper == 1, UPP[k][blk], LOW[k][blk])

            def body(j, row=row, blk=blk):
                ri, qh = j // 2, lax.rem(j, 2)
                block = fv[ri, row, pl.ds(pl.multiple_of(qh * 128, 128), 128), :].astype(F32)
                s32[pl.ds(ri * 8 + blk * 2 + qh, 128, stride=16), :] = block.T

            loop(4, body)

    def pack_mirrors():
        for ri in range(2):
            s32[pl.ds(ri * 8 + 7, 128, stride=16), :] = ev[ri, 0].astype(F32).T
        head = lax.broadcasted_iota(jnp.int32, (128, 128), 0) == 0
        middle = fv[0, 0, 128:136, :].astype(F32)[0:1]
        block = jnp.where(head, middle, fv[1, 0, 0:128, :].astype(F32))
        s32[pl.ds(8 + 6, 128, stride=16), :] = block.T

    turn_filter(0)
    pl.when(here == 0)(pack_mirrors)
    pack(fs, 0)
    turn_filter(1)
    pack(fs, 128)

    loads[2].wait()
    loads[3].wait()

    def make_twiddle(r):
        rows = pl.ds(pl.multiple_of(r * 16, 16), 16)
        cols = tav[rows, :]
        for al in range(8):
            c = jnp.broadcast_to(cols[:, al : al + 1], (16, 256))
            s = jnp.broadcast_to(cols[:, 8 + al : 9 + al], (16, 256))
            tw[al, 0, rows, :], tw[al, 1, rows, :] = cmul(c, s, tbv[0, rows, :], tbv[1, rows, :])

    loop(9, make_twiddle)

    pl.semaphore_wait(barrier, 255)
    slot = core * 128 + chip

    def send_signal(i):
        t = lax.rem(chip + i, 128)
        remote(xs.at[t], xb.at[slot], 0, t, core).start()

    pltpu.make_async_copy(xs.at[chip], xb.at[slot], rsem.at[0]).start()
    loop(128, send_signal, 1)

    zlo, low = chip // 32, lax.rem(chip, 32)
    fslot = (2 * group + upper) * 32 + jnp.where(upper == 1, 63 - place, place)

    def send_filter(j, r):
        t = lax.rem(zlo + j, 4) * 32 + lax.rem(low + r, 32)
        for k in range(2):
            pltpu.make_async_remote_copy(
                src_ref=fs.at[k * 128 + t], dst_ref=hb.at[fslot], send_sem=ssem.at[1],
                recv_sem=wave_r.at[j], device_id=device(t, k), device_id_type=pl.DeviceIdType.MESH,
            ).start()

    loop(64, lambda i: send_filter(1 + 2 * lax.rem(i, 2), i // 2))
    loop(32, lambda i: send_filter(2, i))
    pltpu.make_async_copy(fs.at[core * 128 + chip], hb.at[fslot], wave_r.at[0]).start()
    pltpu.make_async_remote_copy(
        src_ref=fs.at[other * 128 + chip], dst_ref=hb.at[fslot], send_sem=ssem.at[1],
        recv_sem=wave_r.at[0], device_id=device(chip, other), device_id_type=pl.DeviceIdType.MESH,
    ).start()
    loop(32, lambda i: send_filter(0, i), 1)

    mine = xb.at[pl.ds(core * 128, 128)]
    theirs = xb.at[pl.ds(other * 128, 128)]
    pltpu.make_async_copy(mine, mine, rsem.at[0]).wait()
    forward = remote(mine, mine, 3, chip, other)
    forward.start()
    for load in loads[4:]:
        load.wait()
    pltpu.make_async_copy(theirs, theirs, rsem.at[3]).wait()

    def widen(src, dst):
        def body(i):
            dst[pl.ds(pl.multiple_of(i * 256, 256), 256), :] = (
                src[pl.ds(i * 16, 16)].astype(F32).reshape(256, 128)
            )

        loop(16, body)

    widen(xb, x32)

    top = (lax.broadcasted_iota(jnp.int32, (8, 256), 0) == 0).astype(F32)

    def first(al):
        x = jnp.concatenate(
            [x32[pl.ds(2 * al, 256, stride=16), :], x32[pl.ds(2 * al + 1, 256, stride=16), :]], 1
        ).astype(BF16)
        f = dot(m256v[0], x) + dot(m256v[1], x)
        fz[al, 0, 0:128, :] = f[0:128]
        fz[al, 1, 0:128, :] = f[128:256]
        lone = f[224:232] * (top * even)
        fz[al, 1, 96:104, :] = f[224:232] - lone
        fz[al, 0, 128:136, :] = lone
        fz[al, 0, 136:144, :] = jnp.zeros((8, 256), F32)
        fz[al, 1, 128:144, :] = jnp.zeros((16, 256), F32)

    loop(8, first)

    def second(r):
        rows = pl.ds(pl.multiple_of(r * 16, 16), 16)
        for half in range(2):
            ln = slice(half * 128, half * 128 + 128)
            lm = slice(256 + half * 128, 384 + half * 128)
            pairs = [
                cmul(fz[al, 0, rows, ln], fz[al, 1, rows, ln], tw[al, 0, rows, ln], tw[al, 1, rows, ln])
                for al in range(8)
            ]
            re, im = dft8([p[0] for p in pairs], [p[1] for p in pairs], -1)
            for e in range(8):
                a, b, m = re[e], im[e], slot_of(e)
                if e:
                    a, b = cmul(a, b, t2v[0, e : e + 1, ln], t2v[1, e : e + 1, ln])
                zh[m, rows, ln], zl[m, rows, ln] = split(a)
                zh[m, rows, lm], zl[m, rows, lm] = split(b)

    loop(9, second)

    def third(mul, j):
        a = zh[pl.ds(j * 2, 2)].reshape(2 * ROWS, 512)
        b = zl[pl.ds(j * 2, 2)].reshape(2 * ROWS, 512)
        g = mul(a, m512v[0]) + mul(a, m512v[1]) + mul(b, m512v[0])
        gg[pl.ds(j * 2, 2)] = g.reshape(2, ROWS, 512)

    loop(4, lambda j: third(dot, j))
    keep[...] = gg[7, 96:104, :]

    def place_filter(m, shift):
        for ri in range(2):
            hf[m, ri, 128:144, :] = jnp.zeros((16, 256), F32)
            if shift:
                hf[m, ri, 96:104, :] = jnp.zeros((8, 256), F32)
            for blk in range(4):
                lo = blk * 32 + (1 if shift and blk == 3 else 0)
                for qh in range(2):
                    start = m * 512 + (ri * 8 + blk * 2 + qh)
                    hf[m, ri, lo : lo + 32, qh * 128 : qh * 128 + 128] = h32[
                        pl.ds(start, 32, stride=16), :
                    ]

    def apply_filter(m):
        def body(r):
            rows = pl.ds(pl.multiple_of(r * 16, 16), 16)
            a, b = cmul(
                gg[m, rows, 0:256], gg[m, rows, 256:512], hf[m, 0, rows, :], hf[m, 1, rows, :]
            )
            zh[m, rows, 0:256], zl[m, rows, 0:256] = split(a)
            zh[m, rows, 256:512], zl[m, rows, 256:512] = split(b)

        loop(9, body)

    def wave_of(w):
        return lax.rem(w * 2 + 1, 4) + jnp.where(w == 2, 1, 0) - jnp.where(w == 3, 3, 0)

    def mirrors():
        lane = (lax.broadcasted_iota(jnp.int32, (1, 128), 1) == 0).astype(F32)
        re, im = hf[0, 0, 96:97, 0:128], hf[0, 1, 96:97, 0:128]
        hr = hf[0, 0, 96:104, 128:256] * top[:, 0:128]
        hi = hf[0, 1, 96:104, 128:256] * top[:, 0:128]
        hf[0, 0, 96:97, 0:128] = re * (1.0 - 0.5 * lane)
        hf[0, 1, 96:97, 0:128] = im * (1.0 - lane)
        hf[0, 0, 96:97, 128:256] = im * (0.5 * lane)
        hf[0, 1, 96:97, 128:256] = jnp.zeros((1, 128), F32)
        a, b = cmul(keep[:, 0:128], keep[:, 256:384], hr, hi)
        none = jnp.zeros((8, 128), F32)
        row = jnp.concatenate([a, none, b, none], 1)
        high, rest = split(jnp.concatenate([row, jnp.zeros((8, 512), F32)], 0))
        g = dot_t(high, m512v[0]) + dot_t(high, m512v[1]) + dot_t(rest, m512v[0])
        keep[...] = g[0:8]

    def wave(w):
        j = wave_of(w)
        z = lax.rem(zlo + 4 - j, 4)
        part = hb.at[pl.ds(z * 64, 64)]
        pltpu.make_async_copy(part, part, wave_r.at[j]).wait()

        def widen_part(i):
            h32[pl.ds(pl.multiple_of(z * 1024 + i * 256, 256), 256), :] = (
                hb[pl.ds(z * 64 + i * 16, 16)].astype(F32).reshape(256, 128)
            )

        loop(4, widen_part)
        place_filter(2 * z, False)
        pl.when(core == 1)(lambda: place_filter(2 * z + 1, False))
        pl.when(core == 0)(lambda: place_filter(2 * z + 1, True))
        pl.when((core == 0) & (z == 0))(mirrors)
        apply_filter(2 * z)
        apply_filter(2 * z + 1)
        third(dot_t, z)

    loop(4, wave)

    @pl.when(core == 0)
    def _():
        gg[7, 96:104, :] = gg[7, 96:104, :] + keep[...]

    def back(r, last):
        rows = pl.ds(r * 16, 16) if last else pl.ds(pl.multiple_of(r * 16, 16), 16)
        for half in range(2):
            ln = slice(half * 128, half * 128 + 128)
            lm = slice(256 + half * 128, 384 + half * 128)
            re, im = [], []
            for e in range(8):
                a, b = gg[slot_of(e), rows, ln], gg[slot_of(e), rows, lm]
                if e:
                    a, b = cmul(a, b, t2v[0, e : e + 1, ln], -t2v[1, e : e + 1, ln])
                re.append(a)
                im.append(b)
            re, im = dft8(re, im, 1)
            for al in range(8):
                a, b = cmul(re[al], im[al], tw[al, 0, rows, ln], -tw[al, 1, rows, ln])
                if last:
                    ce[al, :, ln] = a[0:8]
                else:
                    mark = top[:, 0:128] * (even * (r == 6).astype(F32))
                    head = b[0:8] * (1.0 - mark) + ce[al, 0:1, ln] * mark
                    b = jnp.concatenate([head, b[8:16]], 0)
                    down = pl.ds(pl.multiple_of(128 + r * 16, 16), 16)
                    ch[al, rows, ln], cl[al, rows, ln] = split(a)
                    ch[al, down, ln], cl[al, down, ln] = split(b)

    back(8, True)
    loop(8, lambda r: back(r, False))

    def swap(al):
        return pltpu.make_async_remote_copy(
            src_ref=yo.at[al], dst_ref=pb.at[al], send_sem=swap_s.at[al], recv_sem=swap_r.at[al],
            device_id=device(chip, other), device_id_type=pl.DeviceIdType.MESH,
        )

    def combine(al):
        vh, vl = m256v[2], m256v[3]
        y = dot(vh, ch[al]) + dot(vh, cl[al]) + dot(vl, ch[al])
        yo[al] = y[0:128]
        swap(al).start()
        yw[al] = y[128:256]

    loop(8, combine)

    weight = skip[chip]

    def add_up(al, peak):
        swap(al).wait()
        for half in range(2):
            ln = slice(half * 128, half * 128 + 128)
            x = x32[pl.ds(core * 2048 + 2 * al + half, 128, stride=16), :]
            value = yw[al, :, ln] + pb[al, :, ln] + weight * x
            v32[pl.ds(2 * al + half, 128, stride=16), :] = value
            peak = jnp.maximum(peak, jnp.max(jnp.abs(value).reshape(16, 8, 128), axis=0))
        return peak

    peak = lax.fori_loop(0, 8, add_up, jnp.zeros((8, 128), F32))
    peak = jnp.max(jnp.max(peak, axis=1, keepdims=True), axis=0, keepdims=True)
    peak = jnp.maximum(jnp.broadcast_to(peak, (1, 128)), 2.0**-118)
    se[0] = peak * (1.0 / SPAN)
    shrink = SPAN / peak

    def encode(i):
        rows = pl.ds(pl.multiple_of(i * 128, 128), 128)
        value = v32[rows, :] * shrink
        power = value * value
        power = power * power
        power = power * power
        power = power * power
        code = jnp.where(value < 0, -power, power)
        ye[pl.ds(i * 8, 8)] = code.astype(BF16).reshape(8, 16, 128)

    loop(16, encode)

    row = (chip // 8) * 8

    def send_scale(i):
        t = row + lax.rem(cp + i, 8)
        remote(se.at[0], sb.at[chip], 6, t, core).start()

    pltpu.make_async_copy(se.at[0], sb.at[chip], rsem.at[6]).start()
    loop(8, send_scale, 1)

    def send_out(j, r):
        t = lax.rem(zlo + j, 4) * 32 + lax.rem(low + r, 32)
        pltpu.make_async_remote_copy(
            src_ref=ye.at[t], dst_ref=yb.at[chip], send_sem=ssem.at[5],
            recv_sem=out_r.at[j], device_id=device(t, core), device_id_type=pl.DeviceIdType.MESH,
        ).start()

    loop(64, lambda i: send_out(1 + 2 * lax.rem(i, 2), i // 2))

    mates = sb.at[pl.ds(row, 8)]
    pltpu.make_async_copy(mates, mates, rsem.at[6]).wait()

    def pass_scale(i):
        t = lax.rem(chip + i * 8, 128)
        remote(mates, mates, 7, t, core).start()

    loop(16, pass_scale, 1)

    loop(32, lambda i: send_out(2, i))
    pltpu.make_async_copy(ye.at[chip], yb.at[chip], out_r.at[0]).start()
    loop(32, lambda i: send_out(0, i), 1)

    most = sb.at[pl.ds(0, 120)]
    pltpu.make_async_copy(most, most, rsem.at[7]).wait()

    def decode(w):
        j = wave_of(w)
        base = lax.rem(zlo + 4 - j, 4) * 32
        part = yb.at[pl.ds(base, 32)]
        pltpu.make_async_copy(part, part, out_r.at[j]).wait()

        def eight(i):
            for n in range(8):
                c = base + i * 8 + n
                code = yb[c].astype(F32)
                size = jnp.maximum(jnp.abs(code), 2.0**-126)
                size = lax.rsqrt(lax.rsqrt(lax.rsqrt(lax.rsqrt(size)))) * sb[c]
                s32[pl.ds(pl.multiple_of(c * 16, 16), 16), :] = jnp.where(code < 0, -size, size)

        loop(4, eight)

    def finish(a):
        rows = pl.ds(pl.multiple_of(a * 128, 128), 128)
        value = s32[pl.ds(a, 128, stride=16), :].T
        ob[rows, :] = (gv[rows, :].astype(F32) * value).astype(BF16)
        pltpu.make_async_copy(ob.at[rows], out.at[rows], lsem.at[9]).start()

    loop(4, decode)
    loop(16, finish)
    pltpu.make_async_copy(ob, out, lsem.at[9]).wait()

    def sent(ref, sem):
        pltpu.make_async_copy(ref, ref, ssem.at[sem]).wait()

    sent(xs.at[pl.ds(0, 127)], 0)
    sent(fs.at[pl.ds(0, 255)], 1)

    forward.wait_send()
    sent(ye.at[pl.ds(0, 127)], 5)
    sent(sb.at[pl.ds(0, 7)], 6)
    sent(most, 7)


def body(signal, gate, filters, skip):
    m256, m512, tb, ta, t2 = (jnp.asarray(t) for t in tables())
    hbm = pl.BlockSpec(memory_space=pl.ANY)
    smem = pl.BlockSpec(memory_space=pltpu.SMEM)
    return pl.pallas_call(
        kernel,
        out_shape=jax.ShapeDtypeStruct(signal.shape, BF16),
        in_specs=[hbm, hbm, hbm, smem, hbm, hbm, hbm, hbm, hbm],
        out_specs=hbm,
        scratch_shapes=[
            pltpu.VMEM((2048, 128), BF16),
            pltpu.VMEM((2, 8, 256, 128), BF16),
            pltpu.VMEM((2, 1, 128, 128), BF16),
            pltpu.VMEM((2048, 128), BF16),
            pltpu.VMEM((2048, 128), BF16),
            pltpu.VMEM((4, 256, 256), BF16),
            pltpu.VMEM((2, 512, 512), BF16),
            pltpu.VMEM((2, ROWS, 256), F32),
            pltpu.VMEM((ROWS, 128), F32),
            pltpu.VMEM((2, 8, 256), F32),
            pltpu.VMEM((2048, 128), F32),
            pltpu.VMEM((128, 16, 128), BF16),
            pltpu.VMEM((256, 16, 128), BF16),
            pltpu.VMEM((4096, 128), F32),
            pltpu.VMEM((256, 16, 128), BF16),
            pltpu.VMEM((256, 16, 128), BF16),
            pltpu.VMEM((8, 2, ROWS, 256), F32),
            pltpu.VMEM((8, 2, ROWS, 256), F32),
            pltpu.VMEM((8, 2, ROWS, 256), F32),
            pltpu.VMEM((8, ROWS, 512), BF16),
            pltpu.VMEM((8, ROWS, 512), BF16),
            pltpu.VMEM((8, ROWS, 512), F32),
            pltpu.VMEM((8, 512), F32),
            pltpu.VMEM((8, 8, 256), F32),
            pltpu.VMEM((8, 256, 256), BF16),
            pltpu.VMEM((8, 256, 256), BF16),
            pltpu.VMEM((8, 128, 256), F32),
            pltpu.VMEM((8, 128, 256), F32),
            pltpu.VMEM((8, 128, 256), F32),
            pltpu.VMEM((2048, 128), F32),
            pltpu.VMEM((4096, 128), F32),
            pltpu.VMEM((128, 16, 128), BF16),
            pltpu.VMEM((128, 16, 128), BF16),
            pltpu.VMEM((1, 1, 128), F32),
            pltpu.VMEM((128, 1, 128), F32),
            pltpu.SemaphoreType.DMA((10,)),
            pltpu.SemaphoreType.DMA((8,)),
            pltpu.SemaphoreType.DMA((8,)),
            pltpu.SemaphoreType.DMA((8,)),
            pltpu.SemaphoreType.DMA((8,)),
            pltpu.SemaphoreType.DMA((4,)),
            pltpu.SemaphoreType.DMA((4,)),
        ],
        compiler_params=pltpu.CompilerParams(
            collective_id=0, has_side_effects=True, vmem_limit_bytes=56 << 20
        ),
    )(signal, filters, gate, skip, m256, m512, tb, ta, t2)


def solution(mesh):
    placed = (
        P(("ctx", "cp"), None),
        P(("ctx", "cp"), None),
        P(None, ("ctx", "cp"), None, None),
        P(),
    )
    return jax.shard_map(
        body, mesh=mesh, in_specs=placed, out_specs=P(("ctx", "cp"), None), check_vma=False
    )
```

```python
import functools
import math

import jax
import jax.numpy as jnp
import ml_dtypes
import numpy as np
from jax import lax
from jax.experimental import pallas as pl
from jax.experimental.pallas import tpu as pltpu
from jax.sharding import PartitionSpec as P


FULL = 1 << 20
SPAN = 2.0**7.75
ROWS = 144
F32 = jnp.float32
BF16 = jnp.bfloat16

LOW = ((2, 4, 6, 0), (3, 5, 7, 1))
UPP = ((6, 4, 2, 0), (5, 3, 1, 7))


def phase(product, length):
    angle = 2 * math.pi * (np.asarray(product, dtype=np.int64) % length) / length
    return np.cos(angle), np.sin(angle)


def split_np(array):
    high = array.astype(ml_dtypes.bfloat16)
    low = (array - high.astype(np.float64)).astype(ml_dtypes.bfloat16)
    return high, low


def row_sigma(core):
    index = np.concatenate([4 * np.arange(32) + t for t in (1, 2, 3, 0)] + [np.array([128])])
    sigma = 2 * index + core
    if core == 1:
        sigma[128] = 0
    return sigma


@functools.lru_cache(maxsize=None)
def tables():
    pos = np.arange(256)
    core_of, chip_of = pos // 128, pos % 128
    block = ((chip_of // 8) * 2 + core_of) * 8 + chip_of % 8
    m256 = []
    tb = np.zeros((2, 2, ROWS, 256), np.float32)
    ta = np.zeros((2, ROWS, 128), np.float32)
    beta, al = np.arange(256), np.arange(8)
    for core in (0, 1):
        sigma = row_sigma(core)
        cos, sin = phase(sigma[:128, None] * block[None, :], 512)
        fwd = np.concatenate([cos, -sin], 0)
        inv = np.concatenate([cos.T, -sin.T], 1)
        if core == 0:
            nyquist = phase(256 * block, 512)[0]
            fwd[128 + 96] = nyquist
            inv[:, 128 + 96] = nyquist
        inv = np.roll(inv, 128 * core - 128, axis=0) * (2.0 / FULL)
        m256.append(np.stack([*split_np(fwd), *split_np(inv)]))
        cos, sin = phase(sigma[:, None] * beta[None, :], FULL)
        tb[core, 0, :129], tb[core, 1, :129] = cos, -sin
        cos, sin = phase(sigma[:, None] * al[None, :], 4096)
        ta[core, :129, 0:8], ta[core, :129, 8:16] = cos, -sin
    cos, sin = phase(beta[:, None] * beta[None, :], 256)
    m512 = np.stack(split_np(np.block([[cos, -sin], [sin, cos]])))
    cos, sin = phase(al[:, None] * beta[None, :], 2048)
    t2 = np.stack([cos, -sin]).astype(np.float32)
    return np.stack(m256), m512, tb, ta, t2


def cmul(a, b, c, d):
    return a * c - b * d, a * d + b * c


def dft8(re, im, sign):
    root = math.sqrt(0.5)

    def turn(x, y, power):
        if power == 0:
            return x, y
        if power == 2:
            return (-y, x) if sign > 0 else (y, -x)
        if power == 1:
            if sign > 0:
                return (x - y) * root, (x + y) * root
            return (x + y) * root, (y - x) * root
        if sign > 0:
            return (-x - y) * root, (x - y) * root
        return (y - x) * root, (-x - y) * root

    def step(res, ims):
        n = len(res)
        if n == 1:
            return res, ims
        h = n // 2
        er = [res[j] + res[j + h] for j in range(h)]
        ei = [ims[j] + ims[j + h] for j in range(h)]
        odd = [turn(res[j] - res[j + h], ims[j] - ims[j + h], j * (8 // n)) for j in range(h)]
        er, ei = step(er, ei)
        dr, di = step([o[0] for o in odd], [o[1] for o in odd])
        outr, outi = [], []
        for j in range(h):
            outr += [er[j], dr[j]]
            outi += [ei[j], di[j]]
        return outr, outi

    return step(re, im)


def split(x):
    high = x.astype(BF16)
    return high, (x - high.astype(F32)).astype(BF16)


def dot(a, b):
    return jnp.dot(a, b, preferred_element_type=F32)


def slot_of(e):
    return 2 * e if e < 4 else 2 * (7 - e) + 1


def dot_t(a, b):
    return lax.dot_general(a, b, (((1,), (1,)), ((), ())), preferred_element_type=F32)


def kernel(
    sig, filt, gate, skip, m256, m512, tb, ta, t2, out,
    sv, fv, ev, gv, ob, m256v, m512v, tbv, tav, t2v,
    s32, xs, xb, x32, fs, hb, hf, fz, tw, zh, zl, gg, keep, ce, ch, cl,
    yo, yw, pb, v32, h32, ye, yb, se, sb, lsem, ssem, rsem, swap_s, swap_r, wave_r, out_r,
):
    ctx, cp = lax.axis_index("ctx"), lax.axis_index("cp")
    core = lax.rem(ctx, 2)
    other = 1 - core
    chip = (ctx // 2) * 8 + cp
    here = ctx * 8 + cp
    even = (1 - core).astype(F32)

    def device(t, k):
        return ((t // 8) * 2 + k, lax.rem(t, 8))

    def push(src, dst, send, recv, line, column):
        return pltpu.make_async_remote_copy(
            src_ref=src, dst_ref=dst, send_sem=send, recv_sem=recv,
            device_id=(line, column), device_id_type=pl.DeviceIdType.MESH,
        )

    def remote(src, dst, sem, t, k):
        return push(src, dst, ssem.at[sem], rsem.at[sem], *device(t, k))

    def loop(n, body, start=0):
        def wrapped(i, carry):
            body(i)
            return carry

        lax.fori_loop(start, n, wrapped, 0)

    barrier = pltpu.get_barrier_semaphore()

    columns = [lax.rem(cp + r, 8) for r in range(8)]

    def greet(i, first=0):
        line = lax.rem(ctx + i, 32)
        for column in columns[first:]:
            pl.semaphore_signal(
                barrier, inc=1, device_id=(line, column), device_id_type=pl.DeviceIdType.MESH
            )

    load_signal = pltpu.make_async_copy(sig, sv, lsem.at[8])
    load_signal.start()
    loop(32, greet, 1)
    greet(0, 1)

    group, place = here // 64, lax.rem(here, 64)
    upper = (place >= 32).astype(jnp.int32)
    loads = [
        pltpu.make_async_copy(filt.at[:, pl.ds(upper * 8, 8)], fv, lsem.at[0]),
        pltpu.make_async_copy(filt.at[:, pl.ds(8, 1), pl.ds(0, 128)], ev, lsem.at[1]),
        pltpu.make_async_copy(ta.at[core], tav, lsem.at[2]),
        pltpu.make_async_copy(tb.at[core], tbv, lsem.at[3]),
        pltpu.make_async_copy(m256.at[core], m256v, lsem.at[4]),
        pltpu.make_async_copy(m512, m512v, lsem.at[5]),
        pltpu.make_async_copy(t2, t2v, lsem.at[6]),
        pltpu.make_async_copy(gate, gv, lsem.at[7]),
    ]
    for load in loads:
        load.start()

    def turn_signal(a):
        block = sv[pl.ds(pl.multiple_of(a * 128, 128), 128), :].astype(F32)
        s32[pl.ds(a, 128, stride=16), :] = block.T

    load_signal.wait()
    loop(16, turn_signal)

    def pack(dst, base):
        def body(i):
            rows = s32[pl.ds(pl.multiple_of(i * 256, 256), 256), :]
            dst[pl.ds(base + i * 16, 16)] = rows.astype(BF16).reshape(16, 16, 128)

        loop(8, body)

    pack(xs, 0)

    loads[0].wait()
    loads[1].wait()

    def turn_filter(k):
        for blk in range(4):
            row = jnp.where(upper == 1, UPP[k][blk], LOW[k][blk])

            def body(j, row=row, blk=blk):
                ri, qh = j // 2, lax.rem(j, 2)
                block = fv[ri, row, pl.ds(pl.multiple_of(qh * 128, 128), 128), :].astype(F32)
                s32[pl.ds(ri * 8 + blk * 2 + qh, 128, stride=16), :] = block.T

            loop(4, body)

    def pack_mirrors():
        for ri in range(2):
            s32[pl.ds(ri * 8 + 7, 128, stride=16), :] = ev[ri, 0].astype(F32).T
        head = lax.broadcasted_iota(jnp.int32, (128, 128), 0) == 0
        middle = fv[0, 0, 128:136, :].astype(F32)[0:1]
        block = jnp.where(head, middle, fv[1, 0, 0:128, :].astype(F32))
        s32[pl.ds(8 + 6, 128, stride=16), :] = block.T

    turn_filter(0)
    pl.when(here == 0)(pack_mirrors)
    pack(fs, 0)
    turn_filter(1)
    pack(fs, 128)

    loads[2].wait()
    loads[3].wait()

    def make_twiddle(r):
        rows = pl.ds(pl.multiple_of(r * 16, 16), 16)
        cols = tav[rows, :]
        for al in range(8):
            c = jnp.broadcast_to(cols[:, al : al + 1], (16, 256))
            s = jnp.broadcast_to(cols[:, 8 + al : 9 + al], (16, 256))
            tw[al, 0, rows, :], tw[al, 1, rows, :] = cmul(c, s, tbv[0, rows, :], tbv[1, rows, :])

    loop(9, make_twiddle)

    pl.semaphore_wait(barrier, 255)
    slot = core * 128 + chip

    home = ctx // 2
    zlo, wide = home // 4, lax.rem(home, 4)

    def send_signal(i, first=0):
        row = lax.rem(home + i, 16)
        for column in columns[first:]:
            push(
                xs.at[row * 8 + column], xb.at[slot], ssem.at[0], rsem.at[0], row * 2 + core, column
            ).start()

    pltpu.make_async_copy(xs.at[chip], xb.at[slot], rsem.at[0]).start()
    send_signal(0, 1)
    loop(16, send_signal, 1)

    def in_waves(send, own):
        loop(8, lambda i: send(1 + 2 * lax.rem(i, 2), i // 2))
        loop(4, lambda i: send(2, i))
        own()
        send(0, 0, 1)
        loop(4, lambda i: send(0, i), 1)

    def row_of(j, i):
        return lax.rem(zlo + j, 4) * 4 + lax.rem(wide + i, 4)

    fslot = (2 * group + upper) * 32 + jnp.where(upper == 1, 63 - place, place)

    def send_filter(j, i, first=0):
        row = row_of(j, i)
        for column in columns[first:]:
            for k in range(2):
                push(
                    fs.at[k * 128 + row * 8 + column], hb.at[fslot],
                    ssem.at[1], wave_r.at[j], row * 2 + k, column,
                ).start()

    def own_filter():
        pltpu.make_async_copy(fs.at[core * 128 + chip], hb.at[fslot], wave_r.at[0]).start()
        push(
            fs.at[other * 128 + chip], hb.at[fslot], ssem.at[1], wave_r.at[0], home * 2 + other, cp
        ).start()

    in_waves(send_filter, own_filter)

    mine = xb.at[pl.ds(core * 128, 128)]
    theirs = xb.at[pl.ds(other * 128, 128)]
    pltpu.make_async_copy(mine, mine, rsem.at[0]).wait()
    forward = remote(mine, mine, 3, chip, other)
    forward.start()
    for load in loads[4:]:
        load.wait()
    pltpu.make_async_copy(theirs, theirs, rsem.at[3]).wait()

    def widen(src, dst):
        def body(i):
            dst[pl.ds(pl.multiple_of(i * 256, 256), 256), :] = (
                src[pl.ds(i * 16, 16)].astype(F32).reshape(256, 128)
            )

        loop(16, body)

    widen(xb, x32)

    top = (lax.broadcasted_iota(jnp.int32, (8, 256), 0) == 0).astype(F32)

    def first(al):
        x = jnp.concatenate(
            [x32[pl.ds(2 * al, 256, stride=16), :], x32[pl.ds(2 * al + 1, 256, stride=16), :]], 1
        ).astype(BF16)
        f = dot(m256v[0], x) + dot(m256v[1], x)
        fz[al, 0, 0:128, :] = f[0:128]
        fz[al, 1, 0:128, :] = f[128:256]
        lone = f[224:232] * (top * even)
        fz[al, 1, 96:104, :] = f[224:232] - lone
        fz[al, 0, 128:136, :] = lone
        fz[al, 0, 136:144, :] = jnp.zeros((8, 256), F32)
        fz[al, 1, 128:144, :] = jnp.zeros((16, 256), F32)

    loop(8, first)

    def second(r):
        rows = pl.ds(pl.multiple_of(r * 16, 16), 16)
        for half in range(2):
            ln = slice(half * 128, half * 128 + 128)
            lm = slice(256 + half * 128, 384 + half * 128)
            pairs = [
                cmul(fz[al, 0, rows, ln], fz[al, 1, rows, ln], tw[al, 0, rows, ln], tw[al, 1, rows, ln])
                for al in range(8)
            ]
            re, im = dft8([p[0] for p in pairs], [p[1] for p in pairs], -1)
            for e in range(8):
                a, b, m = re[e], im[e], slot_of(e)
                if e:
                    a, b = cmul(a, b, t2v[0, e : e + 1, ln], t2v[1, e : e + 1, ln])
                zh[m, rows, ln], zl[m, rows, ln] = split(a)
                zh[m, rows, lm], zl[m, rows, lm] = split(b)

    loop(9, second)

    def third(mul, j):
        a = zh[pl.ds(j * 2, 2)].reshape(2 * ROWS, 512)
        b = zl[pl.ds(j * 2, 2)].reshape(2 * ROWS, 512)
        g = mul(a, m512v[0]) + mul(a, m512v[1]) + mul(b, m512v[0])
        gg[pl.ds(j * 2, 2)] = g.reshape(2, ROWS, 512)

    loop(4, lambda j: third(dot, j))
    keep[...] = gg[7, 96:104, :]

    def place_filter(m, shift):
        for ri in range(2):
            hf[m, ri, 128:144, :] = jnp.zeros((16, 256), F32)
            if shift:
                hf[m, ri, 96:104, :] = jnp.zeros((8, 256), F32)
            for blk in range(4):
                lo = blk * 32 + (1 if shift and blk == 3 else 0)
                for qh in range(2):
                    start = m * 512 + (ri * 8 + blk * 2 + qh)
                    hf[m, ri, lo : lo + 32, qh * 128 : qh * 128 + 128] = h32[
                        pl.ds(start, 32, stride=16), :
                    ]

    def apply_filter(m):
        def body(r):
            rows = pl.ds(pl.multiple_of(r * 16, 16), 16)
            a, b = cmul(
                gg[m, rows, 0:256], gg[m, rows, 256:512], hf[m, 0, rows, :], hf[m, 1, rows, :]
            )
            zh[m, rows, 0:256], zl[m, rows, 0:256] = split(a)
            zh[m, rows, 256:512], zl[m, rows, 256:512] = split(b)

        loop(9, body)

    def wave_of(w):
        return lax.rem(w * 2 + 1, 4) + jnp.where(w == 2, 1, 0) - jnp.where(w == 3, 3, 0)

    def mirrors():
        lane = (lax.broadcasted_iota(jnp.int32, (1, 128), 1) == 0).astype(F32)
        re, im = hf[0, 0, 96:97, 0:128], hf[0, 1, 96:97, 0:128]
        hr = hf[0, 0, 96:104, 128:256] * top[:, 0:128]
        hi = hf[0, 1, 96:104, 128:256] * top[:, 0:128]
        hf[0, 0, 96:97, 0:128] = re * (1.0 - 0.5 * lane)
        hf[0, 1, 96:97, 0:128] = im * (1.0 - lane)
        hf[0, 0, 96:97, 128:256] = im * (0.5 * lane)
        hf[0, 1, 96:97, 128:256] = jnp.zeros((1, 128), F32)
        a, b = cmul(keep[:, 0:128], keep[:, 256:384], hr, hi)
        none = jnp.zeros((8, 128), F32)
        row = jnp.concatenate([a, none, b, none], 1)
        high, rest = split(jnp.concatenate([row, jnp.zeros((8, 512), F32)], 0))
        g = dot_t(high, m512v[0]) + dot_t(high, m512v[1]) + dot_t(rest, m512v[0])
        keep[...] = g[0:8]

    def wave(w):
        j = wave_of(w)
        z = lax.rem(zlo + 4 - j, 4)
        part = hb.at[pl.ds(z * 64, 64)]
        pltpu.make_async_copy(part, part, wave_r.at[j]).wait()

        def widen_part(i):
            h32[pl.ds(pl.multiple_of(z * 1024 + i * 256, 256), 256), :] = (
                hb[pl.ds(z * 64 + i * 16, 16)].astype(F32).reshape(256, 128)
            )

        loop(4, widen_part)
        place_filter(2 * z, False)
        pl.when(core == 1)(lambda: place_filter(2 * z + 1, False))
        pl.when(core == 0)(lambda: place_filter(2 * z + 1, True))
        pl.when((core == 0) & (z == 0))(mirrors)
        apply_filter(2 * z)
        apply_filter(2 * z + 1)
        third(dot_t, z)

    loop(4, wave)

    @pl.when(core == 0)
    def _():
        gg[7, 96:104, :] = gg[7, 96:104, :] + keep[...]

    def back(r, last):
        rows = pl.ds(r * 16, 16) if last else pl.ds(pl.multiple_of(r * 16, 16), 16)
        for half in range(2):
            ln = slice(half * 128, half * 128 + 128)
            lm = slice(256 + half * 128, 384 + half * 128)
            re, im = [], []
            for e in range(8):
                a, b = gg[slot_of(e), rows, ln], gg[slot_of(e), rows, lm]
                if e:
                    a, b = cmul(a, b, t2v[0, e : e + 1, ln], -t2v[1, e : e + 1, ln])
                re.append(a)
                im.append(b)
            re, im = dft8(re, im, 1)
            for al in range(8):
                a, b = cmul(re[al], im[al], tw[al, 0, rows, ln], -tw[al, 1, rows, ln])
                if last:
                    ce[al, :, ln] = a[0:8]
                else:
                    mark = top[:, 0:128] * (even * (r == 6).astype(F32))
                    head = b[0:8] * (1.0 - mark) + ce[al, 0:1, ln] * mark
                    b = jnp.concatenate([head, b[8:16]], 0)
                    down = pl.ds(pl.multiple_of(128 + r * 16, 16), 16)
                    ch[al, rows, ln], cl[al, rows, ln] = split(a)
                    ch[al, down, ln], cl[al, down, ln] = split(b)

    back(8, True)
    loop(8, lambda r: back(r, False))

    def swap(al):
        return pltpu.make_async_remote_copy(
            src_ref=yo.at[al], dst_ref=pb.at[al], send_sem=swap_s.at[al], recv_sem=swap_r.at[al],
            device_id=device(chip, other), device_id_type=pl.DeviceIdType.MESH,
        )

    def combine(al):
        vh, vl = m256v[2], m256v[3]
        y = dot(vh, ch[al]) + dot(vh, cl[al]) + dot(vl, ch[al])
        yo[al] = y[0:128]
        swap(al).start()
        yw[al] = y[128:256]

    loop(8, combine)

    weight = skip[chip]

    def add_up(al, peak):
        swap(al).wait()
        for half in range(2):
            ln = slice(half * 128, half * 128 + 128)
            x = x32[pl.ds(core * 2048 + 2 * al + half, 128, stride=16), :]
            value = yw[al, :, ln] + pb[al, :, ln] + weight * x
            v32[pl.ds(2 * al + half, 128, stride=16), :] = value
            peak = jnp.maximum(peak, jnp.max(jnp.abs(value).reshape(16, 8, 128), axis=0))
        return peak

    peak = lax.fori_loop(0, 8, add_up, jnp.zeros((8, 128), F32))
    peak = jnp.max(jnp.max(peak, axis=1, keepdims=True), axis=0, keepdims=True)
    peak = jnp.maximum(jnp.broadcast_to(peak, (1, 128)), 2.0**-118)
    se[0] = peak * (1.0 / SPAN)
    shrink = SPAN / peak

    def encode(i):
        rows = pl.ds(pl.multiple_of(i * 128, 128), 128)
        value = v32[rows, :] * shrink
        power = value * value
        power = power * power
        power = power * power
        power = power * power
        code = jnp.where(value < 0, -power, power)
        ye[pl.ds(i * 8, 8)] = code.astype(BF16).reshape(8, 16, 128)

    loop(16, encode)

    pltpu.make_async_copy(se.at[0], sb.at[chip], rsem.at[6]).start()
    for column in columns[1:]:
        push(se.at[0], sb.at[chip], ssem.at[6], rsem.at[6], ctx, column).start()

    def send_out(j, i, first=0):
        row = row_of(j, i)
        for column in columns[first:]:
            push(
                ye.at[row * 8 + column], yb.at[chip], ssem.at[5], out_r.at[j], row * 2 + core, column
            ).start()

    def own_out():
        pltpu.make_async_copy(ye.at[chip], yb.at[chip], out_r.at[0]).start()

    in_waves(send_out, own_out)

    mates = sb.at[pl.ds(home * 8, 8)]
    pltpu.make_async_copy(mates, mates, rsem.at[6]).wait()

    def pass_scale(i):
        row = lax.rem(home + i, 16)
        push(mates, mates, ssem.at[7], rsem.at[7], row * 2 + core, cp).start()

    loop(16, pass_scale, 1)

    most = sb.at[pl.ds(0, 120)]
    pltpu.make_async_copy(most, most, rsem.at[7]).wait()

    def decode(w):
        j = wave_of(w)
        base = lax.rem(zlo + 4 - j, 4) * 32
        part = yb.at[pl.ds(base, 32)]
        pltpu.make_async_copy(part, part, out_r.at[j]).wait()

        def eight(i):
            for n in range(8):
                c = base + i * 8 + n
                code = yb[c].astype(F32)
                size = jnp.maximum(jnp.abs(code), 2.0**-126)
                size = lax.rsqrt(lax.rsqrt(lax.rsqrt(lax.rsqrt(size)))) * sb[c]
                s32[pl.ds(pl.multiple_of(c * 16, 16), 16), :] = jnp.where(code < 0, -size, size)

        loop(4, eight)

    def finish(a):
        rows = pl.ds(pl.multiple_of(a * 128, 128), 128)
        value = s32[pl.ds(a, 128, stride=16), :].T
        ob[rows, :] = (gv[rows, :].astype(F32) * value).astype(BF16)
        pltpu.make_async_copy(ob.at[rows], out.at[rows], lsem.at[9]).start()

    loop(4, decode)
    loop(16, finish)
    pltpu.make_async_copy(ob, out, lsem.at[9]).wait()

    def sent(ref, sem):
        pltpu.make_async_copy(ref, ref, ssem.at[sem]).wait()

    sent(xs.at[pl.ds(0, 127)], 0)
    sent(fs.at[pl.ds(0, 255)], 1)

    forward.wait_send()
    sent(ye.at[pl.ds(0, 127)], 5)
    sent(sb.at[pl.ds(0, 7)], 6)
    sent(most, 7)


def body(signal, gate, filters, skip):
    m256, m512, tb, ta, t2 = (jnp.asarray(t) for t in tables())
    hbm = pl.BlockSpec(memory_space=pl.ANY)
    smem = pl.BlockSpec(memory_space=pltpu.SMEM)
    return pl.pallas_call(
        kernel,
        out_shape=jax.ShapeDtypeStruct(signal.shape, BF16),
        in_specs=[hbm, hbm, hbm, smem, hbm, hbm, hbm, hbm, hbm],
        out_specs=hbm,
        scratch_shapes=[
            pltpu.VMEM((2048, 128), BF16),
            pltpu.VMEM((2, 8, 256, 128), BF16),
            pltpu.VMEM((2, 1, 128, 128), BF16),
            pltpu.VMEM((2048, 128), BF16),
            pltpu.VMEM((2048, 128), BF16),
            pltpu.VMEM((4, 256, 256), BF16),
            pltpu.VMEM((2, 512, 512), BF16),
            pltpu.VMEM((2, ROWS, 256), F32),
            pltpu.VMEM((ROWS, 128), F32),
            pltpu.VMEM((2, 8, 256), F32),
            pltpu.VMEM((2048, 128), F32),
            pltpu.VMEM((128, 16, 128), BF16),
            pltpu.VMEM((256, 16, 128), BF16),
            pltpu.VMEM((4096, 128), F32),
            pltpu.VMEM((256, 16, 128), BF16),
            pltpu.VMEM((256, 16, 128), BF16),
            pltpu.VMEM((8, 2, ROWS, 256), F32),
            pltpu.VMEM((8, 2, ROWS, 256), F32),
            pltpu.VMEM((8, 2, ROWS, 256), F32),
            pltpu.VMEM((8, ROWS, 512), BF16),
            pltpu.VMEM((8, ROWS, 512), BF16),
            pltpu.VMEM((8, ROWS, 512), F32),
            pltpu.VMEM((8, 512), F32),
            pltpu.VMEM((8, 8, 256), F32),
            pltpu.VMEM((8, 256, 256), BF16),
            pltpu.VMEM((8, 256, 256), BF16),
            pltpu.VMEM((8, 128, 256), F32),
            pltpu.VMEM((8, 128, 256), F32),
            pltpu.VMEM((8, 128, 256), F32),
            pltpu.VMEM((2048, 128), F32),
            pltpu.VMEM((4096, 128), F32),
            pltpu.VMEM((128, 16, 128), BF16),
            pltpu.VMEM((128, 16, 128), BF16),
            pltpu.VMEM((1, 1, 128), F32),
            pltpu.VMEM((128, 1, 128), F32),
            pltpu.SemaphoreType.DMA((10,)),
            pltpu.SemaphoreType.DMA((8,)),
            pltpu.SemaphoreType.DMA((8,)),
            pltpu.SemaphoreType.DMA((8,)),
            pltpu.SemaphoreType.DMA((8,)),
            pltpu.SemaphoreType.DMA((4,)),
            pltpu.SemaphoreType.DMA((4,)),
        ],
        compiler_params=pltpu.CompilerParams(
            collective_id=0, has_side_effects=True, vmem_limit_bytes=56 << 20
        ),
    )(signal, filters, gate, skip, m256, m512, tb, ta, t2)


def solution(mesh):
    placed = (
        P(("ctx", "cp"), None),
        P(("ctx", "cp"), None),
        P(None, ("ctx", "cp"), None, None),
        P(),
    )
    return jax.shard_map(
        body, mesh=mesh, in_specs=placed, out_specs=P(("ctx", "cp"), None), check_vma=False
    )
```

```python
import functools
import math

import jax
import jax.numpy as jnp
import ml_dtypes
import numpy as np
from jax import lax
from jax.experimental import pallas as pl
from jax.experimental.pallas import tpu as pltpu
from jax.sharding import PartitionSpec as P


FULL = 1 << 20
SPAN = 2.0**7.75
ROWS = 144
F32 = jnp.float32
BF16 = jnp.bfloat16

LOW = ((2, 4, 6, 0), (3, 5, 7, 1))
UPP = ((6, 4, 2, 0), (5, 3, 1, 7))


def phase(product, length):
    angle = 2 * math.pi * (np.asarray(product, dtype=np.int64) % length) / length
    return np.cos(angle), np.sin(angle)


def split_np(array):
    high = array.astype(ml_dtypes.bfloat16)
    low = (array - high.astype(np.float64)).astype(ml_dtypes.bfloat16)
    return high, low


def row_sigma(core):
    index = np.concatenate([4 * np.arange(32) + t for t in (1, 2, 3, 0)] + [np.array([128])])
    sigma = 2 * index + core
    if core == 1:
        sigma[128] = 0
    return sigma


@functools.lru_cache(maxsize=None)
def tables():
    pos = np.arange(256)
    core_of, chip_of = pos // 128, pos % 128
    block = ((chip_of // 8) * 2 + core_of) * 8 + chip_of % 8
    m256 = []
    tb = np.zeros((2, 2, ROWS, 256), np.float32)
    ta = np.zeros((2, ROWS, 128), np.float32)
    beta, al = np.arange(256), np.arange(8)
    for core in (0, 1):
        sigma = row_sigma(core)
        cos, sin = phase(sigma[:128, None] * block[None, :], 512)
        fwd = np.concatenate([cos, -sin], 0)
        inv = np.concatenate([cos.T, -sin.T], 1)
        if core == 0:
            nyquist = phase(256 * block, 512)[0]
            fwd[128 + 96] = nyquist
            inv[:, 128 + 96] = nyquist
        inv = np.roll(inv, 128 * core - 128, axis=0) * (2.0 / FULL)
        m256.append(np.stack([*split_np(fwd), *split_np(inv)]))
        cos, sin = phase(sigma[:, None] * beta[None, :], FULL)
        tb[core, 0, :129], tb[core, 1, :129] = cos, -sin
        cos, sin = phase(sigma[:, None] * al[None, :], 4096)
        ta[core, :129, 0:8], ta[core, :129, 8:16] = cos, -sin
    cos, sin = phase(beta[:, None] * beta[None, :], 256)
    m512 = np.stack(split_np(np.block([[cos, -sin], [sin, cos]])))
    cos, sin = phase(al[:, None] * beta[None, :], 2048)
    t2 = np.stack([cos, -sin]).astype(np.float32)
    return np.stack(m256), m512, tb, ta, t2


def cmul(a, b, c, d):
    return a * c - b * d, a * d + b * c


def dft8(re, im, sign):
    root = math.sqrt(0.5)

    def turn(x, y, power):
        if power == 0:
            return x, y
        if power == 2:
            return (-y, x) if sign > 0 else (y, -x)
        if power == 1:
            if sign > 0:
                return (x - y) * root, (x + y) * root
            return (x + y) * root, (y - x) * root
        if sign > 0:
            return (-x - y) * root, (x - y) * root
        return (y - x) * root, (-x - y) * root

    def step(res, ims):
        n = len(res)
        if n == 1:
            return res, ims
        h = n // 2
        er = [res[j] + res[j + h] for j in range(h)]
        ei = [ims[j] + ims[j + h] for j in range(h)]
        odd = [turn(res[j] - res[j + h], ims[j] - ims[j + h], j * (8 // n)) for j in range(h)]
        er, ei = step(er, ei)
        dr, di = step([o[0] for o in odd], [o[1] for o in odd])
        outr, outi = [], []
        for j in range(h):
            outr += [er[j], dr[j]]
            outi += [ei[j], di[j]]
        return outr, outi

    return step(re, im)


def split(x):
    high = x.astype(BF16)
    return high, (x - high.astype(F32)).astype(BF16)


def dot(a, b):
    return jnp.dot(a, b, preferred_element_type=F32)


def slot_of(e):
    return 2 * e if e < 4 else 2 * (7 - e) + 1


def dot_t(a, b):
    return lax.dot_general(a, b, (((1,), (1,)), ((), ())), preferred_element_type=F32)


def kernel(
    sig, filt, gate, skip, m256, m512, tb, ta, t2, out,
    sv, fv, ev, gv, ob, m256v, m512v, tbv, tav, t2v,
    s32, xs, xb, x32, fs, hb, hf, fz, tw, zh, zl, gg, keep, ce, ch, cl,
    yo, yw, pb, v32, h32, ye, yb, se, sb, lsem, ssem, rsem, swap_s, swap_r, wave_r, out_r,
):
    ctx, cp = lax.axis_index("ctx"), lax.axis_index("cp")
    core = lax.rem(ctx, 2)
    other = 1 - core
    chip = (ctx // 2) * 8 + cp
    here = ctx * 8 + cp
    even = (1 - core).astype(F32)

    def device(t, k):
        return ((t // 8) * 2 + k, lax.rem(t, 8))

    def push(src, dst, send, recv, line, column):
        return pltpu.make_async_remote_copy(
            src_ref=src, dst_ref=dst, send_sem=send, recv_sem=recv,
            device_id=(line, column), device_id_type=pl.DeviceIdType.MESH,
        )

    def remote(src, dst, sem, t, k):
        return push(src, dst, ssem.at[sem], rsem.at[sem], *device(t, k))

    def loop(n, body, start=0):
        def wrapped(i, carry):
            body(i)
            return carry

        lax.fori_loop(start, n, wrapped, 0)

    barrier = pltpu.get_barrier_semaphore()

    columns = [lax.rem(cp + r, 8) for r in range(8)]

    def greet(i, first=0):
        line = lax.rem(ctx + i, 32)
        for column in columns[first:]:
            pl.semaphore_signal(
                barrier, inc=1, device_id=(line, column), device_id_type=pl.DeviceIdType.MESH
            )

    load_signal = pltpu.make_async_copy(sig, sv, lsem.at[8])
    load_signal.start()
    loop(32, greet, 1)
    greet(0, 1)

    group, place = here // 64, lax.rem(here, 64)
    upper = (place >= 32).astype(jnp.int32)
    loads = [
        pltpu.make_async_copy(filt.at[:, pl.ds(upper * 8, 8)], fv, lsem.at[0]),
        pltpu.make_async_copy(filt.at[:, pl.ds(8, 1), pl.ds(0, 128)], ev, lsem.at[1]),
        pltpu.make_async_copy(ta.at[core], tav, lsem.at[2]),
        pltpu.make_async_copy(tb.at[core], tbv, lsem.at[3]),
        pltpu.make_async_copy(m256.at[core], m256v, lsem.at[4]),
        pltpu.make_async_copy(m512, m512v, lsem.at[5]),
        pltpu.make_async_copy(t2, t2v, lsem.at[6]),
        pltpu.make_async_copy(gate, gv, lsem.at[7]),
    ]
    for load in loads:
        load.start()

    def turn_signal(a):
        block = sv[pl.ds(pl.multiple_of(a * 128, 128), 128), :].astype(F32)
        s32[pl.ds(a, 128, stride=16), :] = block.T

    load_signal.wait()
    loop(16, turn_signal)

    def pack(dst, base):
        def body(i):
            rows = s32[pl.ds(pl.multiple_of(i * 256, 256), 256), :]
            dst[pl.ds(base + i * 16, 16)] = rows.astype(BF16).reshape(16, 16, 128)

        loop(8, body)

    pack(xs, 0)

    pl.semaphore_wait(barrier, 255)
    slot = core * 128 + chip

    home = ctx // 2
    zlo, wide = home // 4, lax.rem(home, 4)

    def send_signal(i, first=0):
        row = lax.rem(home + i, 16)
        for column in columns[first:]:
            push(
                xs.at[row * 8 + column], xb.at[slot], ssem.at[0], rsem.at[0], row * 2 + core, column
            ).start()

    pltpu.make_async_copy(xs.at[chip], xb.at[slot], rsem.at[0]).start()
    send_signal(0, 1)
    loop(16, send_signal, 1)

    def in_waves(send, own):
        loop(8, lambda i: send(1 + 2 * lax.rem(i, 2), i // 2))
        own()
        send(0, 0, 1)
        loop(4, lambda i: send(0, i), 1)
        loop(4, lambda i: send(2, i))

    def row_of(j, i):
        return lax.rem(zlo + j, 4) * 4 + lax.rem(wide + i, 4)

    loads[0].wait()
    loads[1].wait()

    def turn_filter(k):
        for blk in range(4):
            row = jnp.where(upper == 1, UPP[k][blk], LOW[k][blk])

            def body(j, row=row, blk=blk):
                ri, qh = j // 2, lax.rem(j, 2)
                block = fv[ri, row, pl.ds(pl.multiple_of(qh * 128, 128), 128), :].astype(F32)
                s32[pl.ds(ri * 8 + blk * 2 + qh, 128, stride=16), :] = block.T

            loop(4, body)

    def pack_mirrors():
        for ri in range(2):
            s32[pl.ds(ri * 8 + 7, 128, stride=16), :] = ev[ri, 0].astype(F32).T
        head = lax.broadcasted_iota(jnp.int32, (128, 128), 0) == 0
        middle = fv[0, 0, 128:136, :].astype(F32)[0:1]
        block = jnp.where(head, middle, fv[1, 0, 0:128, :].astype(F32))
        s32[pl.ds(8 + 6, 128, stride=16), :] = block.T

    turn_filter(0)
    pl.when(here == 0)(pack_mirrors)
    pack(fs, 0)
    turn_filter(1)
    pack(fs, 128)

    fslot = (2 * group + upper) * 32 + jnp.where(upper == 1, 63 - place, place)

    def send_filter(j, i, first=0):
        row = row_of(j, i)
        for column in columns[first:]:
            for k in range(2):
                push(
                    fs.at[k * 128 + row * 8 + column], hb.at[fslot],
                    ssem.at[1], wave_r.at[j], row * 2 + k, column,
                ).start()

    def own_filter():
        pltpu.make_async_copy(fs.at[core * 128 + chip], hb.at[fslot], wave_r.at[0]).start()
        push(
            fs.at[other * 128 + chip], hb.at[fslot], ssem.at[1], wave_r.at[0], home * 2 + other, cp
        ).start()

    in_waves(send_filter, own_filter)

    loads[2].wait()
    loads[3].wait()

    def make_twiddle(r):
        rows = pl.ds(pl.multiple_of(r * 16, 16), 16)
        cols = tav[rows, :]
        for al in range(8):
            c = jnp.broadcast_to(cols[:, al : al + 1], (16, 256))
            s = jnp.broadcast_to(cols[:, 8 + al : 9 + al], (16, 256))
            tw[al, 0, rows, :], tw[al, 1, rows, :] = cmul(c, s, tbv[0, rows, :], tbv[1, rows, :])

    loop(9, make_twiddle)

    mine = xb.at[pl.ds(core * 128, 128)]
    theirs = xb.at[pl.ds(other * 128, 128)]
    pltpu.make_async_copy(mine, mine, rsem.at[0]).wait()
    forward = remote(mine, mine, 3, chip, other)
    forward.start()
    for load in loads[4:]:
        load.wait()
    pltpu.make_async_copy(theirs, theirs, rsem.at[3]).wait()

    def widen(src, dst):
        def body(i):
            dst[pl.ds(pl.multiple_of(i * 256, 256), 256), :] = (
                src[pl.ds(i * 16, 16)].astype(F32).reshape(256, 128)
            )

        loop(16, body)

    widen(xb, x32)

    top = (lax.broadcasted_iota(jnp.int32, (8, 256), 0) == 0).astype(F32)

    def first(al):
        x = jnp.concatenate(
            [x32[pl.ds(2 * al, 256, stride=16), :], x32[pl.ds(2 * al + 1, 256, stride=16), :]], 1
        ).astype(BF16)
        f = dot(m256v[0], x) + dot(m256v[1], x)
        fz[al, 0, 0:128, :] = f[0:128]
        fz[al, 1, 0:128, :] = f[128:256]
        lone = f[224:232] * (top * even)
        fz[al, 1, 96:104, :] = f[224:232] - lone
        fz[al, 0, 128:136, :] = lone
        fz[al, 0, 136:144, :] = jnp.zeros((8, 256), F32)
        fz[al, 1, 128:144, :] = jnp.zeros((16, 256), F32)

    loop(8, first)

    def second(r):
        rows = pl.ds(pl.multiple_of(r * 16, 16), 16)
        for half in range(2):
            ln = slice(half * 128, half * 128 + 128)
            lm = slice(256 + half * 128, 384 + half * 128)
            pairs = [
                cmul(fz[al, 0, rows, ln], fz[al, 1, rows, ln], tw[al, 0, rows, ln], tw[al, 1, rows, ln])
                for al in range(8)
            ]
            re, im = dft8([p[0] for p in pairs], [p[1] for p in pairs], -1)
            for e in range(8):
                a, b, m = re[e], im[e], slot_of(e)
                if e:
                    a, b = cmul(a, b, t2v[0, e : e + 1, ln], t2v[1, e : e + 1, ln])
                zh[m, rows, ln], zl[m, rows, ln] = split(a)
                zh[m, rows, lm], zl[m, rows, lm] = split(b)

    loop(9, second)

    def third(mul, j):
        a = zh[pl.ds(j * 2, 2)].reshape(2 * ROWS, 512)
        b = zl[pl.ds(j * 2, 2)].reshape(2 * ROWS, 512)
        g = mul(a, m512v[0]) + mul(a, m512v[1]) + mul(b, m512v[0])
        gg[pl.ds(j * 2, 2)] = g.reshape(2, ROWS, 512)

    loop(4, lambda j: third(dot, j))
    keep[...] = gg[7, 96:104, :]

    def place_filter(m, shift):
        for ri in range(2):
            hf[m, ri, 128:144, :] = jnp.zeros((16, 256), F32)
            if shift:
                hf[m, ri, 96:104, :] = jnp.zeros((8, 256), F32)
            for blk in range(4):
                lo = blk * 32 + (1 if shift and blk == 3 else 0)
                for qh in range(2):
                    start = m * 512 + (ri * 8 + blk * 2 + qh)
                    hf[m, ri, lo : lo + 32, qh * 128 : qh * 128 + 128] = h32[
                        pl.ds(start, 32, stride=16), :
                    ]

    def apply_filter(m):
        def body(r):
            rows = pl.ds(pl.multiple_of(r * 16, 16), 16)
            a, b = cmul(
                gg[m, rows, 0:256], gg[m, rows, 256:512], hf[m, 0, rows, :], hf[m, 1, rows, :]
            )
            zh[m, rows, 0:256], zl[m, rows, 0:256] = split(a)
            zh[m, rows, 256:512], zl[m, rows, 256:512] = split(b)

        loop(9, body)

    def wave_of(w):
        return lax.rem(w * 2 + 1, 4) - jnp.where(w >= 2, 1, 0)

    def mirrors():
        lane = (lax.broadcasted_iota(jnp.int32, (1, 128), 1) == 0).astype(F32)
        re, im = hf[0, 0, 96:97, 0:128], hf[0, 1, 96:97, 0:128]
        hr = hf[0, 0, 96:104, 128:256] * top[:, 0:128]
        hi = hf[0, 1, 96:104, 128:256] * top[:, 0:128]
        hf[0, 0, 96:97, 0:128] = re * (1.0 - 0.5 * lane)
        hf[0, 1, 96:97, 0:128] = im * (1.0 - lane)
        hf[0, 0, 96:97, 128:256] = im * (0.5 * lane)
        hf[0, 1, 96:97, 128:256] = jnp.zeros((1, 128), F32)
        a, b = cmul(keep[:, 0:128], keep[:, 256:384], hr, hi)
        none = jnp.zeros((8, 128), F32)
        row = jnp.concatenate([a, none, b, none], 1)
        high, rest = split(jnp.concatenate([row, jnp.zeros((8, 512), F32)], 0))
        g = dot_t(high, m512v[0]) + dot_t(high, m512v[1]) + dot_t(rest, m512v[0])
        keep[...] = g[0:8]

    def wave(w):
        j = wave_of(w)
        z = lax.rem(zlo + 4 - j, 4)
        part = hb.at[pl.ds(z * 64, 64)]
        pltpu.make_async_copy(part, part, wave_r.at[j]).wait()

        def widen_part(i):
            h32[pl.ds(pl.multiple_of(z * 1024 + i * 256, 256), 256), :] = (
                hb[pl.ds(z * 64 + i * 16, 16)].astype(F32).reshape(256, 128)
            )

        loop(4, widen_part)
        place_filter(2 * z, False)
        pl.when(core == 1)(lambda: place_filter(2 * z + 1, False))
        pl.when(core == 0)(lambda: place_filter(2 * z + 1, True))
        pl.when((core == 0) & (z == 0))(mirrors)
        apply_filter(2 * z)
        apply_filter(2 * z + 1)
        third(dot_t, z)

    loop(4, wave)

    @pl.when(core == 0)
    def _():
        gg[7, 96:104, :] = gg[7, 96:104, :] + keep[...]

    def back(r, last):
        rows = pl.ds(r * 16, 16) if last else pl.ds(pl.multiple_of(r * 16, 16), 16)
        for half in range(2):
            ln = slice(half * 128, half * 128 + 128)
            lm = slice(256 + half * 128, 384 + half * 128)
            re, im = [], []
            for e in range(8):
                a, b = gg[slot_of(e), rows, ln], gg[slot_of(e), rows, lm]
                if e:
                    a, b = cmul(a, b, t2v[0, e : e + 1, ln], -t2v[1, e : e + 1, ln])
                re.append(a)
                im.append(b)
            re, im = dft8(re, im, 1)
            for al in range(8):
                a, b = cmul(re[al], im[al], tw[al, 0, rows, ln], -tw[al, 1, rows, ln])
                if last:
                    ce[al, :, ln] = a[0:8]
                else:
                    mark = top[:, 0:128] * (even * (r == 6).astype(F32))
                    head = b[0:8] * (1.0 - mark) + ce[al, 0:1, ln] * mark
                    b = jnp.concatenate([head, b[8:16]], 0)
                    down = pl.ds(pl.multiple_of(128 + r * 16, 16), 16)
                    ch[al, rows, ln], cl[al, rows, ln] = split(a)
                    ch[al, down, ln], cl[al, down, ln] = split(b)

    back(8, True)
    loop(8, lambda r: back(r, False))

    def swap(al):
        return pltpu.make_async_remote_copy(
            src_ref=yo.at[al], dst_ref=pb.at[al], send_sem=swap_s.at[al], recv_sem=swap_r.at[al],
            device_id=device(chip, other), device_id_type=pl.DeviceIdType.MESH,
        )

    def combine(al):
        vh, vl = m256v[2], m256v[3]
        y = dot(vh, ch[al]) + dot(vh, cl[al]) + dot(vl, ch[al])
        yo[al] = y[0:128]
        swap(al).start()
        yw[al] = y[128:256]

    loop(8, combine)

    weight = skip[chip]

    def add_up(al, peak):
        swap(al).wait()
        for half in range(2):
            ln = slice(half * 128, half * 128 + 128)
            x = x32[pl.ds(core * 2048 + 2 * al + half, 128, stride=16), :]
            value = yw[al, :, ln] + pb[al, :, ln] + weight * x
            v32[pl.ds(2 * al + half, 128, stride=16), :] = value
            peak = jnp.maximum(peak, jnp.max(jnp.abs(value).reshape(16, 8, 128), axis=0))
        return peak

    peak = lax.fori_loop(0, 8, add_up, jnp.zeros((8, 128), F32))
    peak = jnp.max(jnp.max(peak, axis=1, keepdims=True), axis=0, keepdims=True)
    peak = jnp.maximum(jnp.broadcast_to(peak, (1, 128)), 2.0**-118)
    se[0] = peak * (1.0 / SPAN)
    shrink = SPAN / peak

    def encode(i):
        rows = pl.ds(pl.multiple_of(i * 128, 128), 128)
        value = v32[rows, :] * shrink
        power = value * value
        power = power * power
        power = power * power
        power = power * power
        code = jnp.where(value < 0, -power, power)
        ye[pl.ds(i * 8, 8)] = code.astype(BF16).reshape(8, 16, 128)


    pltpu.make_async_copy(se.at[0], sb.at[chip], rsem.at[6]).start()
    for column in columns[1:]:
        push(se.at[0], sb.at[chip], ssem.at[6], rsem.at[6], ctx, column).start()

    def send_out(j, i, first=0):
        row = row_of(j, i)
        if not first:
            encode(row)
        for column in columns[first:]:
            push(
                ye.at[row * 8 + column], yb.at[chip], ssem.at[5], out_r.at[j], row * 2 + core, column
            ).start()

    def own_out():
        encode(home)
        pltpu.make_async_copy(ye.at[chip], yb.at[chip], out_r.at[0]).start()

    in_waves(send_out, own_out)

    mates = sb.at[pl.ds(home * 8, 8)]
    pltpu.make_async_copy(mates, mates, rsem.at[6]).wait()

    def pass_scale(i):
        row = lax.rem(home + i, 16)
        push(mates, mates, ssem.at[7], rsem.at[7], row * 2 + core, cp).start()

    loop(16, pass_scale, 1)

    most = sb.at[pl.ds(0, 120)]
    pltpu.make_async_copy(most, most, rsem.at[7]).wait()

    def decode(w):
        j = wave_of(w)
        base = lax.rem(zlo + 4 - j, 4) * 32
        part = yb.at[pl.ds(base, 32)]
        pltpu.make_async_copy(part, part, out_r.at[j]).wait()

        def eight(i):
            for n in range(8):
                c = base + i * 8 + n
                code = yb[c].astype(F32)
                size = jnp.maximum(jnp.abs(code), 2.0**-126)
                size = lax.rsqrt(lax.rsqrt(lax.rsqrt(lax.rsqrt(size)))) * sb[c]
                s32[pl.ds(pl.multiple_of(c * 16, 16), 16), :] = jnp.where(code < 0, -size, size)

        loop(4, eight)

    def finish(a):
        rows = pl.ds(pl.multiple_of(a * 128, 128), 128)
        value = s32[pl.ds(a, 128, stride=16), :].T
        ob[rows, :] = (gv[rows, :].astype(F32) * value).astype(BF16)
        pltpu.make_async_copy(ob.at[rows], out.at[rows], lsem.at[9]).start()

    loop(4, decode)
    loop(16, finish)
    pltpu.make_async_copy(ob, out, lsem.at[9]).wait()

    def sent(ref, sem):
        pltpu.make_async_copy(ref, ref, ssem.at[sem]).wait()

    sent(xs.at[pl.ds(0, 127)], 0)
    sent(fs.at[pl.ds(0, 255)], 1)

    forward.wait_send()
    sent(ye.at[pl.ds(0, 127)], 5)
    sent(sb.at[pl.ds(0, 7)], 6)
    sent(most, 7)


def body(signal, gate, filters, skip):
    m256, m512, tb, ta, t2 = (jnp.asarray(t) for t in tables())
    hbm = pl.BlockSpec(memory_space=pl.ANY)
    smem = pl.BlockSpec(memory_space=pltpu.SMEM)
    return pl.pallas_call(
        kernel,
        out_shape=jax.ShapeDtypeStruct(signal.shape, BF16),
        in_specs=[hbm, hbm, hbm, smem, hbm, hbm, hbm, hbm, hbm],
        out_specs=hbm,
        scratch_shapes=[
            pltpu.VMEM((2048, 128), BF16),
            pltpu.VMEM((2, 8, 256, 128), BF16),
            pltpu.VMEM((2, 1, 128, 128), BF16),
            pltpu.VMEM((2048, 128), BF16),
            pltpu.VMEM((2048, 128), BF16),
            pltpu.VMEM((4, 256, 256), BF16),
            pltpu.VMEM((2, 512, 512), BF16),
            pltpu.VMEM((2, ROWS, 256), F32),
            pltpu.VMEM((ROWS, 128), F32),
            pltpu.VMEM((2, 8, 256), F32),
            pltpu.VMEM((2048, 128), F32),
            pltpu.VMEM((128, 16, 128), BF16),
            pltpu.VMEM((256, 16, 128), BF16),
            pltpu.VMEM((4096, 128), F32),
            pltpu.VMEM((256, 16, 128), BF16),
            pltpu.VMEM((256, 16, 128), BF16),
            pltpu.VMEM((8, 2, ROWS, 256), F32),
            pltpu.VMEM((8, 2, ROWS, 256), F32),
            pltpu.VMEM((8, 2, ROWS, 256), F32),
            pltpu.VMEM((8, ROWS, 512), BF16),
            pltpu.VMEM((8, ROWS, 512), BF16),
            pltpu.VMEM((8, ROWS, 512), F32),
            pltpu.VMEM((8, 512), F32),
            pltpu.VMEM((8, 8, 256), F32),
            pltpu.VMEM((8, 256, 256), BF16),
            pltpu.VMEM((8, 256, 256), BF16),
            pltpu.VMEM((8, 128, 256), F32),
            pltpu.VMEM((8, 128, 256), F32),
            pltpu.VMEM((8, 128, 256), F32),
            pltpu.VMEM((2048, 128), F32),
            pltpu.VMEM((4096, 128), F32),
            pltpu.VMEM((128, 16, 128), BF16),
            pltpu.VMEM((128, 16, 128), BF16),
            pltpu.VMEM((1, 1, 128), F32),
            pltpu.VMEM((128, 1, 128), F32),
            pltpu.SemaphoreType.DMA((10,)),
            pltpu.SemaphoreType.DMA((8,)),
            pltpu.SemaphoreType.DMA((8,)),
            pltpu.SemaphoreType.DMA((8,)),
            pltpu.SemaphoreType.DMA((8,)),
            pltpu.SemaphoreType.DMA((4,)),
            pltpu.SemaphoreType.DMA((4,)),
        ],
        compiler_params=pltpu.CompilerParams(
            collective_id=0, has_side_effects=True, vmem_limit_bytes=56 << 20
        ),
    )(signal, filters, gate, skip, m256, m512, tb, ta, t2)


def solution(mesh):
    placed = (
        P(("ctx", "cp"), None),
        P(("ctx", "cp"), None),
        P(None, ("ctx", "cp"), None, None),
        P(),
    )
    return jax.shard_map(
        body, mesh=mesh, in_specs=placed, out_specs=P(("ctx", "cp"), None), check_vma=False
    )
```

```python
import functools
import math

import jax
import jax.numpy as jnp
import ml_dtypes
import numpy as np
from jax import lax
from jax.experimental import pallas as pl
from jax.experimental.pallas import tpu as pltpu
from jax.sharding import PartitionSpec as P


FULL = 1 << 20
SPAN = 2.0**7.75
ROWS = 144
F32 = jnp.float32
BF16 = jnp.bfloat16

LOW = ((2, 4, 6, 0), (3, 5, 7, 1))
UPP = ((6, 4, 2, 0), (5, 3, 1, 7))


def phase(product, length):
    angle = 2 * math.pi * (np.asarray(product, dtype=np.int64) % length) / length
    return np.cos(angle), np.sin(angle)


def split_np(array):
    high = array.astype(ml_dtypes.bfloat16)
    low = (array - high.astype(np.float64)).astype(ml_dtypes.bfloat16)
    return high, low


def row_sigma(core):
    index = np.concatenate([4 * np.arange(32) + t for t in (1, 2, 3, 0)] + [np.array([128])])
    sigma = 2 * index + core
    if core == 1:
        sigma[128] = 0
    return sigma


@functools.lru_cache(maxsize=None)
def tables():
    pos = np.arange(256)
    core_of, chip_of = pos // 128, pos % 128
    block = ((chip_of // 8) * 2 + core_of) * 8 + chip_of % 8
    m256 = []
    tb = np.zeros((2, 2, ROWS, 256), np.float32)
    ta = np.zeros((2, ROWS, 128), np.float32)
    beta, al = np.arange(256), np.arange(8)
    for core in (0, 1):
        sigma = row_sigma(core)
        cos, sin = phase(sigma[:128, None] * block[None, :], 512)
        fwd = np.concatenate([cos, -sin], 0)
        inv = np.concatenate([cos.T, -sin.T], 1)
        if core == 0:
            nyquist = phase(256 * block, 512)[0]
            fwd[128 + 96] = nyquist
            inv[:, 128 + 96] = nyquist
        inv = np.roll(inv, 128 * core - 128, axis=0) * (2.0 / FULL)
        m256.append(np.stack([*split_np(fwd), *split_np(inv)]))
        cos, sin = phase(sigma[:, None] * beta[None, :], FULL)
        tb[core, 0, :129], tb[core, 1, :129] = cos, -sin
        cos, sin = phase(sigma[:, None] * al[None, :], 4096)
        ta[core, :129, 0:8], ta[core, :129, 8:16] = cos, -sin
    cos, sin = phase(beta[:, None] * beta[None, :], 256)
    m512 = np.stack(split_np(np.block([[cos, -sin], [sin, cos]])))
    cos, sin = phase(al[:, None] * beta[None, :], 2048)
    t2 = np.stack([cos, -sin]).astype(np.float32)
    return np.stack(m256), m512, tb, ta, t2


def cmul(a, b, c, d):
    return a * c - b * d, a * d + b * c


def dft8(re, im, sign):
    root = math.sqrt(0.5)

    def turn(x, y, power):
        if power == 0:
            return x, y
        if power == 2:
            return (-y, x) if sign > 0 else (y, -x)
        if power == 1:
            if sign > 0:
                return (x - y) * root, (x + y) * root
            return (x + y) * root, (y - x) * root
        if sign > 0:
            return (-x - y) * root, (x - y) * root
        return (y - x) * root, (-x - y) * root

    def step(res, ims):
        n = len(res)
        if n == 1:
            return res, ims
        h = n // 2
        er = [res[j] + res[j + h] for j in range(h)]
        ei = [ims[j] + ims[j + h] for j in range(h)]
        odd = [turn(res[j] - res[j + h], ims[j] - ims[j + h], j * (8 // n)) for j in range(h)]
        er, ei = step(er, ei)
        dr, di = step([o[0] for o in odd], [o[1] for o in odd])
        outr, outi = [], []
        for j in range(h):
            outr += [er[j], dr[j]]
            outi += [ei[j], di[j]]
        return outr, outi

    return step(re, im)


def split(x):
    high = x.astype(BF16)
    return high, (x - high.astype(F32)).astype(BF16)


def dot(a, b):
    return jnp.dot(a, b, preferred_element_type=F32)


def slot_of(e):
    return 2 * e if e < 4 else 2 * (7 - e) + 1


def dot_t(a, b):
    return lax.dot_general(a, b, (((1,), (1,)), ((), ())), preferred_element_type=F32)


def kernel(
    sig, filt, gate, skip, m256, m512, tb, ta, t2, out,
    sv, fv, ev, gv, ob, m256v, m512v, tbv, tav, t2v,
    s32, xs, xb, x32, fs, hb, hf, fz, tw, zh, zl, gg, keep, ce, ch, cl,
    yo, yw, pb, v32, h32, ye, yb, se, sb, lsem, ssem, rsem, swap_s, swap_r, wave_r, out_r,
):
    ctx, cp = lax.axis_index("ctx"), lax.axis_index("cp")
    core = lax.rem(ctx, 2)
    other = 1 - core
    chip = (ctx // 2) * 8 + cp
    here = ctx * 8 + cp
    even = (1 - core).astype(F32)

    def device(t, k):
        return ((t // 8) * 2 + k, lax.rem(t, 8))

    def push(src, dst, send, recv, line, column):
        return pltpu.make_async_remote_copy(
            src_ref=src, dst_ref=dst, send_sem=send, recv_sem=recv,
            device_id=(line, column), device_id_type=pl.DeviceIdType.MESH,
        )

    def remote(src, dst, sem, t, k):
        return push(src, dst, ssem.at[sem], rsem.at[sem], *device(t, k))

    def loop(n, body, start=0):
        def wrapped(i, carry):
            body(i)
            return carry

        lax.fori_loop(start, n, wrapped, 0)

    barrier = pltpu.get_barrier_semaphore()

    columns = [lax.rem(cp + r, 8) for r in range(8)]

    near = (cp // 4) * 4
    sides = [[base + lax.rem(cp + r, 4) for r in range(4)] for base in (4 - near, near)]

    def greet(i, side, first=0):
        line = lax.rem(ctx + i, 32)
        for column in sides[side][first:]:
            pl.semaphore_signal(
                barrier, inc=1, device_id=(line, column), device_id_type=pl.DeviceIdType.MESH
            )

    def greet_two(i, side):
        greet(2 * i, side)
        greet(2 * i + 1, side)

    load_signal = pltpu.make_async_copy(sig, sv, lsem.at[8])
    load_signal.start()
    loop(16, lambda i: greet_two(i, 0))
    loop(16, lambda i: greet_two(i, 1), 1)
    greet(1, 1)
    greet(0, 1, 1)

    group, place = here // 64, lax.rem(here, 64)
    upper = (place >= 32).astype(jnp.int32)
    loads = [
        pltpu.make_async_copy(filt.at[:, pl.ds(upper * 8, 8)], fv, lsem.at[0]),
        pltpu.make_async_copy(filt.at[:, pl.ds(8, 1), pl.ds(0, 128)], ev, lsem.at[1]),
        pltpu.make_async_copy(ta.at[core], tav, lsem.at[2]),
        pltpu.make_async_copy(tb.at[core], tbv, lsem.at[3]),
        pltpu.make_async_copy(m256.at[core], m256v, lsem.at[4]),
        pltpu.make_async_copy(m512, m512v, lsem.at[5]),
        pltpu.make_async_copy(t2, t2v, lsem.at[6]),
        pltpu.make_async_copy(gate, gv, lsem.at[7]),
    ]
    for load in loads:
        load.start()

    def turn_signal(a):
        block = sv[pl.ds(pl.multiple_of(a * 128, 128), 128), :].astype(F32)
        s32[pl.ds(a, 128, stride=16), :] = block.T

    load_signal.wait()
    loop(16, turn_signal)

    def pack(dst, base):
        def body(i):
            rows = s32[pl.ds(pl.multiple_of(i * 256, 256), 256), :]
            dst[pl.ds(base + i * 16, 16)] = rows.astype(BF16).reshape(16, 16, 128)

        loop(8, body)

    pack(xs, 0)

    pl.semaphore_wait(barrier, 255)
    slot = core * 128 + chip

    home = ctx // 2
    zlo, wide = home // 4, lax.rem(home, 4)

    def send_signal(i, first=0):
        row = lax.rem(home + i, 16)
        for column in columns[first:]:
            push(
                xs.at[row * 8 + column], xb.at[slot], ssem.at[0], rsem.at[0], row * 2 + core, column
            ).start()

    pltpu.make_async_copy(xs.at[chip], xb.at[slot], rsem.at[0]).start()
    send_signal(0, 1)
    loop(16, send_signal, 1)

    def in_waves(send, own):
        loop(8, lambda i: send(1 + 2 * lax.rem(i, 2), i // 2))
        own()
        send(0, 0, 1)
        loop(4, lambda i: send(0, i), 1)
        loop(4, lambda i: send(2, i))

    def row_of(j, i):
        return lax.rem(zlo + j, 4) * 4 + lax.rem(wide + i, 4)

    loads[0].wait()
    loads[1].wait()

    def turn_filter(k):
        for blk in range(4):
            row = jnp.where(upper == 1, UPP[k][blk], LOW[k][blk])

            def body(j, row=row, blk=blk):
                ri, qh = j // 2, lax.rem(j, 2)
                block = fv[ri, row, pl.ds(pl.multiple_of(qh * 128, 128), 128), :].astype(F32)
                s32[pl.ds(ri * 8 + blk * 2 + qh, 128, stride=16), :] = block.T

            loop(4, body)

    def pack_mirrors():
        for ri in range(2):
            s32[pl.ds(ri * 8 + 7, 128, stride=16), :] = ev[ri, 0].astype(F32).T
        head = lax.broadcasted_iota(jnp.int32, (128, 128), 0) == 0
        middle = fv[0, 0, 128:136, :].astype(F32)[0:1]
        block = jnp.where(head, middle, fv[1, 0, 0:128, :].astype(F32))
        s32[pl.ds(8 + 6, 128, stride=16), :] = block.T

    turn_filter(0)
    pl.when(here == 0)(pack_mirrors)
    pack(fs, 0)
    turn_filter(1)
    pack(fs, 128)

    fslot = (2 * group + upper) * 32 + jnp.where(upper == 1, 63 - place, place)

    def send_filter(j, i, first=0):
        row = row_of(j, i)
        for column in columns[first:]:
            for k in range(2):
                push(
                    fs.at[k * 128 + row * 8 + column], hb.at[fslot],
                    ssem.at[1], wave_r.at[j], row * 2 + k, column,
                ).start()

    def own_filter():
        pltpu.make_async_copy(fs.at[core * 128 + chip], hb.at[fslot], wave_r.at[0]).start()
        push(
            fs.at[other * 128 + chip], hb.at[fslot], ssem.at[1], wave_r.at[0], home * 2 + other, cp
        ).start()

    in_waves(send_filter, own_filter)

    loads[2].wait()
    loads[3].wait()

    def make_twiddle(r):
        rows = pl.ds(pl.multiple_of(r * 16, 16), 16)
        cols = tav[rows, :]
        for al in range(8):
            c = jnp.broadcast_to(cols[:, al : al + 1], (16, 256))
            s = jnp.broadcast_to(cols[:, 8 + al : 9 + al], (16, 256))
            tw[al, 0, rows, :], tw[al, 1, rows, :] = cmul(c, s, tbv[0, rows, :], tbv[1, rows, :])

    loop(9, make_twiddle)

    mine = xb.at[pl.ds(core * 128, 128)]
    theirs = xb.at[pl.ds(other * 128, 128)]
    pltpu.make_async_copy(mine, mine, rsem.at[0]).wait()
    forward = remote(mine, mine, 3, chip, other)
    forward.start()
    for load in loads[4:]:
        load.wait()
    pltpu.make_async_copy(theirs, theirs, rsem.at[3]).wait()

    def widen(src, dst):
        def body(i):
            dst[pl.ds(pl.multiple_of(i * 256, 256), 256), :] = (
                src[pl.ds(i * 16, 16)].astype(F32).reshape(256, 128)
            )

        loop(16, body)

    widen(xb, x32)

    top = (lax.broadcasted_iota(jnp.int32, (8, 256), 0) == 0).astype(F32)

    def first(al):
        x = jnp.concatenate(
            [x32[pl.ds(2 * al, 256, stride=16), :], x32[pl.ds(2 * al + 1, 256, stride=16), :]], 1
        ).astype(BF16)
        f = dot(m256v[0], x) + dot(m256v[1], x)
        fz[al, 0, 0:128, :] = f[0:128]
        fz[al, 1, 0:128, :] = f[128:256]
        lone = f[224:232] * (top * even)
        fz[al, 1, 96:104, :] = f[224:232] - lone
        fz[al, 0, 128:136, :] = lone
        fz[al, 0, 136:144, :] = jnp.zeros((8, 256), F32)
        fz[al, 1, 128:144, :] = jnp.zeros((16, 256), F32)

    loop(8, first)

    def second(r):
        rows = pl.ds(pl.multiple_of(r * 16, 16), 16)
        for half in range(2):
            ln = slice(half * 128, half * 128 + 128)
            lm = slice(256 + half * 128, 384 + half * 128)
            pairs = [
                cmul(fz[al, 0, rows, ln], fz[al, 1, rows, ln], tw[al, 0, rows, ln], tw[al, 1, rows, ln])
                for al in range(8)
            ]
            re, im = dft8([p[0] for p in pairs], [p[1] for p in pairs], -1)
            for e in range(8):
                a, b, m = re[e], im[e], slot_of(e)
                if e:
                    a, b = cmul(a, b, t2v[0, e : e + 1, ln], t2v[1, e : e + 1, ln])
                zh[m, rows, ln], zl[m, rows, ln] = split(a)
                zh[m, rows, lm], zl[m, rows, lm] = split(b)

    loop(9, second)

    def third(mul, j):
        a = zh[pl.ds(j * 2, 2)].reshape(2 * ROWS, 512)
        b = zl[pl.ds(j * 2, 2)].reshape(2 * ROWS, 512)
        g = mul(a, m512v[0]) + mul(a, m512v[1]) + mul(b, m512v[0])
        gg[pl.ds(j * 2, 2)] = g.reshape(2, ROWS, 512)

    loop(4, lambda j: third(dot, j))
    keep[...] = gg[7, 96:104, :]

    def place_filter(m, shift):
        for ri in range(2):
            hf[m, ri, 128:144, :] = jnp.zeros((16, 256), F32)
            if shift:
                hf[m, ri, 96:104, :] = jnp.zeros((8, 256), F32)
            for blk in range(4):
                lo = blk * 32 + (1 if shift and blk == 3 else 0)
                for qh in range(2):
                    start = m * 512 + (ri * 8 + blk * 2 + qh)
                    hf[m, ri, lo : lo + 32, qh * 128 : qh * 128 + 128] = h32[
                        pl.ds(start, 32, stride=16), :
                    ]

    def apply_filter(m):
        def body(r):
            rows = pl.ds(pl.multiple_of(r * 16, 16), 16)
            a, b = cmul(
                gg[m, rows, 0:256], gg[m, rows, 256:512], hf[m, 0, rows, :], hf[m, 1, rows, :]
            )
            zh[m, rows, 0:256], zl[m, rows, 0:256] = split(a)
            zh[m, rows, 256:512], zl[m, rows, 256:512] = split(b)

        loop(9, body)

    def wave_of(w):
        return lax.rem(w * 2 + 1, 4) - jnp.where(w >= 2, 1, 0)

    def mirrors():
        lane = (lax.broadcasted_iota(jnp.int32, (1, 128), 1) == 0).astype(F32)
        re, im = hf[0, 0, 96:97, 0:128], hf[0, 1, 96:97, 0:128]
        hr = hf[0, 0, 96:104, 128:256] * top[:, 0:128]
        hi = hf[0, 1, 96:104, 128:256] * top[:, 0:128]
        hf[0, 0, 96:97, 0:128] = re * (1.0 - 0.5 * lane)
        hf[0, 1, 96:97, 0:128] = im * (1.0 - lane)
        hf[0, 0, 96:97, 128:256] = im * (0.5 * lane)
        hf[0, 1, 96:97, 128:256] = jnp.zeros((1, 128), F32)
        a, b = cmul(keep[:, 0:128], keep[:, 256:384], hr, hi)
        none = jnp.zeros((8, 128), F32)
        row = jnp.concatenate([a, none, b, none], 1)
        high, rest = split(jnp.concatenate([row, jnp.zeros((8, 512), F32)], 0))
        g = dot_t(high, m512v[0]) + dot_t(high, m512v[1]) + dot_t(rest, m512v[0])
        keep[...] = g[0:8]

    def wave(w):
        j = wave_of(w)
        z = lax.rem(zlo + 4 - j, 4)
        part = hb.at[pl.ds(z * 64, 64)]
        pltpu.make_async_copy(part, part, wave_r.at[j]).wait()

        def widen_part(i):
            h32[pl.ds(pl.multiple_of(z * 1024 + i * 256, 256), 256), :] = (
                hb[pl.ds(z * 64 + i * 16, 16)].astype(F32).reshape(256, 128)
            )

        loop(4, widen_part)
        place_filter(2 * z, False)
        pl.when(core == 1)(lambda: place_filter(2 * z + 1, False))
        pl.when(core == 0)(lambda: place_filter(2 * z + 1, True))
        pl.when((core == 0) & (z == 0))(mirrors)
        apply_filter(2 * z)
        apply_filter(2 * z + 1)
        third(dot_t, z)

    loop(4, wave)

    @pl.when(core == 0)
    def _():
        gg[7, 96:104, :] = gg[7, 96:104, :] + keep[...]

    def back(r, last):
        rows = pl.ds(r * 16, 16) if last else pl.ds(pl.multiple_of(r * 16, 16), 16)
        for half in range(2):
            ln = slice(half * 128, half * 128 + 128)
            lm = slice(256 + half * 128, 384 + half * 128)
            re, im = [], []
            for e in range(8):
                a, b = gg[slot_of(e), rows, ln], gg[slot_of(e), rows, lm]
                if e:
                    a, b = cmul(a, b, t2v[0, e : e + 1, ln], -t2v[1, e : e + 1, ln])
                re.append(a)
                im.append(b)
            re, im = dft8(re, im, 1)
            for al in range(8):
                a, b = cmul(re[al], im[al], tw[al, 0, rows, ln], -tw[al, 1, rows, ln])
                if last:
                    ce[al, :, ln] = a[0:8]
                else:
                    mark = top[:, 0:128] * (even * (r == 6).astype(F32))
                    head = b[0:8] * (1.0 - mark) + ce[al, 0:1, ln] * mark
                    b = jnp.concatenate([head, b[8:16]], 0)
                    down = pl.ds(pl.multiple_of(128 + r * 16, 16), 16)
                    ch[al, rows, ln], cl[al, rows, ln] = split(a)
                    ch[al, down, ln], cl[al, down, ln] = split(b)

    back(8, True)
    loop(8, lambda r: back(r, False))

    def swap(al):
        return pltpu.make_async_remote_copy(
            src_ref=yo.at[al], dst_ref=pb.at[al], send_sem=swap_s.at[al], recv_sem=swap_r.at[al],
            device_id=device(chip, other), device_id_type=pl.DeviceIdType.MESH,
        )

    def combine(al):
        vh, vl = m256v[2], m256v[3]
        y = dot(vh, ch[al]) + dot(vh, cl[al]) + dot(vl, ch[al])
        yo[al] = y[0:128]
        swap(al).start()
        yw[al] = y[128:256]

    loop(8, combine)

    weight = skip[chip]

    def add_up(al, peak):
        swap(al).wait()
        for half in range(2):
            ln = slice(half * 128, half * 128 + 128)
            x = x32[pl.ds(core * 2048 + 2 * al + half, 128, stride=16), :]
            value = yw[al, :, ln] + pb[al, :, ln] + weight * x
            v32[pl.ds(2 * al + half, 128, stride=16), :] = value
            peak = jnp.maximum(peak, jnp.max(jnp.abs(value).reshape(16, 8, 128), axis=0))
        return peak

    peak = lax.fori_loop(0, 8, add_up, jnp.zeros((8, 128), F32))
    peak = jnp.max(jnp.max(peak, axis=1, keepdims=True), axis=0, keepdims=True)
    peak = jnp.maximum(jnp.broadcast_to(peak, (1, 128)), 2.0**-118)
    se[0] = peak * (1.0 / SPAN)
    shrink = SPAN / peak

    def encode(i):
        rows = pl.ds(pl.multiple_of(i * 128, 128), 128)
        value = v32[rows, :] * shrink
        power = value * value
        power = power * power
        power = power * power
        power = power * power
        code = jnp.where(value < 0, -power, power)
        ye[pl.ds(i * 8, 8)] = code.astype(BF16).reshape(8, 16, 128)


    pltpu.make_async_copy(se.at[0], sb.at[chip], rsem.at[6]).start()
    for column in columns[1:]:
        push(se.at[0], sb.at[chip], ssem.at[6], rsem.at[6], ctx, column).start()

    def send_out(j, i, first=0):
        row = row_of(j, i)
        if not first:
            encode(row)
        for column in columns[first:]:
            push(
                ye.at[row * 8 + column], yb.at[chip], ssem.at[5], out_r.at[j], row * 2 + core, column
            ).start()

    def own_out():
        encode(home)
        pltpu.make_async_copy(ye.at[chip], yb.at[chip], out_r.at[0]).start()

    in_waves(send_out, own_out)

    mates = sb.at[pl.ds(home * 8, 8)]
    pltpu.make_async_copy(mates, mates, rsem.at[6]).wait()

    def pass_scale(i):
        row = lax.rem(home + i, 16)
        push(mates, mates, ssem.at[7], rsem.at[7], row * 2 + core, cp).start()

    loop(16, pass_scale, 1)

    most = sb.at[pl.ds(0, 120)]
    pltpu.make_async_copy(most, most, rsem.at[7]).wait()

    def decode(w):
        j = wave_of(w)
        base = lax.rem(zlo + 4 - j, 4) * 32
        part = yb.at[pl.ds(base, 32)]
        pltpu.make_async_copy(part, part, out_r.at[j]).wait()

        def eight(i):
            for n in range(8):
                c = base + i * 8 + n
                code = yb[c].astype(F32)
                size = jnp.maximum(jnp.abs(code), 2.0**-126)
                size = lax.rsqrt(lax.rsqrt(lax.rsqrt(lax.rsqrt(size)))) * sb[c]
                s32[pl.ds(pl.multiple_of(c * 16, 16), 16), :] = jnp.where(code < 0, -size, size)

        loop(4, eight)

    def finish(a):
        rows = pl.ds(pl.multiple_of(a * 128, 128), 128)
        value = s32[pl.ds(a, 128, stride=16), :].T
        ob[rows, :] = (gv[rows, :].astype(F32) * value).astype(BF16)
        pltpu.make_async_copy(ob.at[rows], out.at[rows], lsem.at[9]).start()

    loop(4, decode)
    loop(16, finish)
    pltpu.make_async_copy(ob, out, lsem.at[9]).wait()

    def sent(ref, sem):
        pltpu.make_async_copy(ref, ref, ssem.at[sem]).wait()

    sent(xs.at[pl.ds(0, 127)], 0)
    sent(fs.at[pl.ds(0, 255)], 1)

    forward.wait_send()
    sent(ye.at[pl.ds(0, 127)], 5)
    sent(sb.at[pl.ds(0, 7)], 6)
    sent(most, 7)


def body(signal, gate, filters, skip):
    m256, m512, tb, ta, t2 = (jnp.asarray(t) for t in tables())
    hbm = pl.BlockSpec(memory_space=pl.ANY)
    smem = pl.BlockSpec(memory_space=pltpu.SMEM)
    return pl.pallas_call(
        kernel,
        out_shape=jax.ShapeDtypeStruct(signal.shape, BF16),
        in_specs=[hbm, hbm, hbm, smem, hbm, hbm, hbm, hbm, hbm],
        out_specs=hbm,
        scratch_shapes=[
            pltpu.VMEM((2048, 128), BF16),
            pltpu.VMEM((2, 8, 256, 128), BF16),
            pltpu.VMEM((2, 1, 128, 128), BF16),
            pltpu.VMEM((2048, 128), BF16),
            pltpu.VMEM((2048, 128), BF16),
            pltpu.VMEM((4, 256, 256), BF16),
            pltpu.VMEM((2, 512, 512), BF16),
            pltpu.VMEM((2, ROWS, 256), F32),
            pltpu.VMEM((ROWS, 128), F32),
            pltpu.VMEM((2, 8, 256), F32),
            pltpu.VMEM((2048, 128), F32),
            pltpu.VMEM((128, 16, 128), BF16),
            pltpu.VMEM((256, 16, 128), BF16),
            pltpu.VMEM((4096, 128), F32),
            pltpu.VMEM((256, 16, 128), BF16),
            pltpu.VMEM((256, 16, 128), BF16),
            pltpu.VMEM((8, 2, ROWS, 256), F32),
            pltpu.VMEM((8, 2, ROWS, 256), F32),
            pltpu.VMEM((8, 2, ROWS, 256), F32),
            pltpu.VMEM((8, ROWS, 512), BF16),
            pltpu.VMEM((8, ROWS, 512), BF16),
            pltpu.VMEM((8, ROWS, 512), F32),
            pltpu.VMEM((8, 512), F32),
            pltpu.VMEM((8, 8, 256), F32),
            pltpu.VMEM((8, 256, 256), BF16),
            pltpu.VMEM((8, 256, 256), BF16),
            pltpu.VMEM((8, 128, 256), F32),
            pltpu.VMEM((8, 128, 256), F32),
            pltpu.VMEM((8, 128, 256), F32),
            pltpu.VMEM((2048, 128), F32),
            pltpu.VMEM((4096, 128), F32),
            pltpu.VMEM((128, 16, 128), BF16),
            pltpu.VMEM((128, 16, 128), BF16),
            pltpu.VMEM((1, 1, 128), F32),
            pltpu.VMEM((128, 1, 128), F32),
            pltpu.SemaphoreType.DMA((10,)),
            pltpu.SemaphoreType.DMA((8,)),
            pltpu.SemaphoreType.DMA((8,)),
            pltpu.SemaphoreType.DMA((8,)),
            pltpu.SemaphoreType.DMA((8,)),
            pltpu.SemaphoreType.DMA((4,)),
            pltpu.SemaphoreType.DMA((4,)),
        ],
        compiler_params=pltpu.CompilerParams(
            collective_id=0, has_side_effects=True, vmem_limit_bytes=56 << 20
        ),
    )(signal, filters, gate, skip, m256, m512, tb, ta, t2)


def solution(mesh):
    placed = (
        P(("ctx", "cp"), None),
        P(("ctx", "cp"), None),
        P(None, ("ctx", "cp"), None, None),
        P(),
    )
    return jax.shard_map(
        body, mesh=mesh, in_specs=placed, out_specs=P(("ctx", "cp"), None), check_vma=False
    )
```
